256 devices in a mesh: lon: 16 (over x, y_lo, core), lat: 16 (over y_hi, z).
Axes of the slice: x: 4, y: 4 (y_hi: 2, y_lo: 2; y = y_hi * 2 + y_lo), z: 8, core: 2. Of those that a mesh axis runs over, the one named last changes fastest.
Arguments:
- fields_in: bfloat16 [64, 512, 2048], P(None, 'lat', 'lon'), may hold values from -6 to 6
- weight_one: bfloat16 [3, 3, 64, 64], replicated, may hold values from -0.25 to 0.25
- weight_two: bfloat16 [3, 3, 64, 64], replicated, may hold values from -0.25 to 0.25
- cotangent: bfloat16 [64, 512, 2048], P(None, 'lat', 'lon'), may hold values from -6 to 6
- north_map: int32 [16], replicated, may hold values from 0 to 15, each once
- north_code: int32 [16], replicated, may hold values from 0 to 1
- south_map: int32 [16], replicated, may hold values from 0 to 15, each once
- south_code: int32 [16], replicated, may hold values from 0 to 1
Outputs:
- output: bfloat16 [64, 512, 2048], P(None, 'lat', 'lon')
- d_fields: bfloat16 [64, 512, 2048], P(None, 'lat', 'lon')
- grad_one: float32 [3, 3, 64, 64], replicated
- grad_two: float32 [3, 3, 64, 64], replicated
The draws below stay inside these ranges and needn't reach their ends.
Inputs may be any that keep to these rules, and one draw needn't show every extreme that they name: north_map holds each longitude tile index once. south_map holds each longitude tile index once.
All inputs are finite; a program needn't handle non-finite values.
Results may differ from the reference program's by a relative error of at most 0.005.
Values may be sent and summed in bfloat16 or wider, within the bound.
A program may use at most 64 MiB of HBM per device.

```python
import jax
import jax.numpy as jnp

CHANNELS = 64
TILE_COLS = 128
GRID_ROWS = 512
GRID_COLS = 2048
PIXELS = 1048576
N_LON = 16


def touch_ends(drawn, own_key, low, largest):
    spot = [jax.random.randint(jax.random.fold_in(own_key, axis), (), 0, length) for axis, length in enumerate(drawn.shape)]
    widest = drawn.shape.index(max(drawn.shape))
    beside = spot[:widest] + [(spot[widest] + 1) % drawn.shape[widest]] + spot[widest + 1:]
    return drawn.at[tuple(spot)].set(low).at[tuple(beside)].set(largest)


def block_scale(rng, dims, shards, low, largest):
    def one(axis_at, shards_of):
        steps = jax.random.uniform(jax.random.fold_in(jax.random.fold_in(rng, 6), axis_at), (shards_of,), jnp.float32, low / len(shards), largest / len(shards))
        return jnp.repeat(jnp.exp(steps), dims[axis_at] // shards_of).reshape((-1,) + (1,) * (len(dims) - axis_at - 1))

    factor_of = one(*shards[0])
    for cut in shards[1:]:
        factor_of = factor_of * one(*cut)
    return factor_of


def bell_draw(rng, dims, deviation, limit, split=(), kind=jnp.bfloat16):
    drawn = deviation * jax.random.normal(rng, dims, jnp.float32)
    if split:
        drawn = drawn * block_scale(rng, dims, split, -0.22, 0.18)
    return jnp.clip(drawn, -limit, limit).astype(kind)


def setup_inputs(seed: int = 0) -> dict:
    key_list = jax.random.split(jax.random.key(seed), 9)
    return {
        "fields_in": bell_draw(key_list[0], (CHANNELS, GRID_ROWS, GRID_COLS), 1.0, 6.0, ((1, 16), (2, 16))),
        "weight_one": bell_draw(key_list[1], (3, 3, CHANNELS, CHANNELS), (9 * CHANNELS) ** -0.5, 0.25),
        "weight_two": bell_draw(key_list[2], (3, 3, CHANNELS, CHANNELS), (9 * CHANNELS) ** -0.5, 0.25),
        "cotangent": bell_draw(key_list[3], (CHANNELS, GRID_ROWS, GRID_COLS), 1.0, 6.0, ((1, 16), (2, 16))),
        "north_map": jax.random.permutation(key_list[4], N_LON).astype(jnp.int32),
        "north_code": touch_ends(jax.random.randint(key_list[5], (N_LON,), 0, 2), jax.random.fold_in(key_list[5], 1), 0, 1).astype(jnp.int32),
        "south_map": jax.random.permutation(key_list[6], N_LON).astype(jnp.int32),
        "south_code": touch_ends(jax.random.randint(key_list[7], (N_LON,), 0, 2), jax.random.fold_in(key_list[7], 1), 0, 1).astype(jnp.int32),
    }


def pole_row(edge_row, partner, code_row):
    tile_rows = edge_row.reshape(edge_row.shape[0], N_LON, TILE_COLS)
    chosen = tile_rows[:, partner, :]
    chosen = jnp.where((code_row == 1)[None, :, None], chosen[:, :, ::-1], chosen)
    return chosen.reshape(edge_row.shape[0], GRID_COLS)

def extend_global(values, north_map, north_code, south_map, south_code):
    north_row = pole_row(values[:, 0, :], north_map, north_code)
    south_row = pole_row(values[:, -1, :], south_map, south_code)
    tall_field = jnp.concatenate([north_row[:, None, :], values, south_row[:, None, :]], axis=1)
    return jnp.concatenate([tall_field[:, :, -1:], tall_field, tall_field[:, :, :1]], axis=2)

def convolve(padded, weight):
    summed = jnp.zeros((weight.shape[2], GRID_ROWS * GRID_COLS), jnp.float32)
    for shift_row in range(3):
        for shift_col in range(3):
            window = padded[:, shift_row:shift_row + GRID_ROWS, shift_col:shift_col + GRID_COLS].reshape(padded.shape[0], -1)
            summed = summed + jnp.dot(weight[shift_row, shift_col], window, preferred_element_type=jnp.float32)
    return summed.reshape(weight.shape[2], GRID_ROWS, GRID_COLS)

def back_conv(upstream, weight, padded):
    flat_up = upstream.reshape(upstream.shape[0], -1)
    d_pad = jnp.zeros(padded.shape, jnp.float32)
    grads = []
    for shift_row in range(3):
        for shift_col in range(3):
            window = padded[:, shift_row:shift_row + GRID_ROWS, shift_col:shift_col + GRID_COLS].reshape(padded.shape[0], -1)
            grads.append(jnp.dot(flat_up, window.T, preferred_element_type=jnp.float32))
            spread = jnp.dot(weight[shift_row, shift_col].T, flat_up, preferred_element_type=jnp.float32)
            spread = spread.reshape(weight.shape[3], GRID_ROWS, GRID_COLS)
            d_pad = d_pad.at[:, shift_row:shift_row + GRID_ROWS, shift_col:shift_col + GRID_COLS].add(spread)
    return (d_pad, jnp.stack(grads).reshape(3, 3, weight.shape[2], weight.shape[3]))

def reference(fields_in, weight_one, weight_two, cotangent, north_map, north_code, south_map, south_code):

    def extend(values):
        return extend_global(values, north_map, north_code, south_map, south_code)
    grad_scale = 1.0 / jnp.sqrt(jnp.float32(PIXELS))
    padded_in = extend(fields_in)
    pre_act = convolve(padded_in, weight_one)
    hidden = jax.nn.gelu(pre_act).astype(jnp.bfloat16)
    padded_hidden = extend(hidden)
    output = convolve(padded_hidden, weight_two).astype(jnp.bfloat16)
    spread_two, grad_two = back_conv(cotangent, weight_two, padded_hidden)
    _, pull_ext = jax.vjp(extend, hidden.astype(jnp.float32))
    back_hidden = pull_ext(spread_two)[0]
    _, pull_gelu = jax.vjp(jax.nn.gelu, pre_act)
    d_pre = pull_gelu(back_hidden)[0].astype(jnp.bfloat16)
    spread_one, grad_one = back_conv(d_pre, weight_one, padded_in)
    _, pull_in = jax.vjp(extend, fields_in.astype(jnp.float32))
    d_fields = pull_in(spread_one)[0].astype(jnp.bfloat16)
    return (output, d_fields, grad_one * grad_scale, grad_two * grad_scale)
```

```python
import functools
import math

import jax
import jax.numpy as jnp
from jax import lax
from jax.experimental import pallas as pl
from jax.experimental.pallas import tpu as pltpu
from jax.sharding import PartitionSpec as P

MESH = pl.DeviceIdType.MESH
LANES = 128
F32 = jnp.float32
BF16 = jnp.bfloat16


def lane_index(shape):
    return lax.broadcasted_iota(jnp.int32, shape, len(shape) - 1)


def aligned(start, step):
    return pl.multiple_of(start * step, step)


def kernel(
    nlon, nlat, rows, chans, owners, scale,
    fields_ref, cot_ref, w_ref, north_map, north_code, south_map, south_code,
    out_ref, df_ref, g1_ref, g2_ref,
    stage, fwide, gwide, hwide, dwide, slope, wedge,
    send_a, recv_a, pole_a, send_b, recv_b, pole_b, send_c, recv_c, pole_c,
    acc_one, acc_two, rs_send, rs_recv, ar_send, ar_recv, ag_buf,
    near_send, near_recv, pole_send, pole_recv,
    rs_ssem, rs_rsem, ar_ssem, ar_rsem, ag_ssem, ag_rsem,
):
    lon = lax.axis_index("lon")
    lat = lax.axis_index("lat")
    west = lax.rem(lon + nlon - 1, nlon)
    east = lax.rem(lon + 1, nlon)
    has_north = lat > 0
    has_south = lat < nlat - 1
    at_top = lat == 0
    at_pole = jnp.logical_or(lat == 0, lat == nlat - 1)
    at_bottom = lat == nlat - 1
    lane = lane_index((chans, LANES))
    own_rows = pl.ds(0, LANES)
    ghost_cols = pl.ds(LANES, LANES)
    piece = ag_buf.shape[0] // owners

    def other(k, me, count):
        return lax.rem(me + k, count)

    barrier = pltpu.get_barrier_semaphore()

    def greet(lat_at, lon_at):
        pl.semaphore_signal(
            barrier, inc=1, device_id={"lon": lon_at, "lat": lat_at}, device_id_type=MESH
        )

    def greet_lon(k, c):
        greet(lat, other(k, lon, nlon))
        return c

    def greet_lat(k, c):
        greet(other(k, lat, nlat), lon)
        return c

    lax.fori_loop(1, nlon, greet_lon, 0)
    lax.fori_loop(1, nlat, greet_lat, 0)

    @pl.when(has_north)
    def _():
        greet(lat - 1, west)
        greet(lat - 1, east)

    @pl.when(has_south)
    def _():
        greet(lat + 1, west)
        greet(lat + 1, east)

    diagonals = 2 * has_north.astype(jnp.int32) + 2 * has_south.astype(jnp.int32)

    def put(src, dst, ssem, rsem, lat_at, lon_at):
        return pltpu.make_async_remote_copy(
            src_ref=src, dst_ref=dst, send_sem=ssem, recv_sem=rsem,
            device_id={"lon": lon_at, "lat": lat_at}, device_id_type=MESH,
        )

    def near_copies(x, send, recv):
        def one(part, slot, at, lat_at, lon_at):
            return put(
                send.at[part], recv.at[slot], near_send.at[x, at], near_recv.at[x, slot],
                lat_at, lon_at,
            )

        sides = [one(2, 1, 0, lat, west), one(2, 0, 1, lat, east)]
        up = [
            one(0, 7, 2, lat - 1, west), one(0, 6, 3, lat - 1, lon), one(0, 5, 4, lat - 1, east)
        ]
        down = [
            one(1, 4, 5, lat + 1, west), one(1, 3, 6, lat + 1, lon), one(1, 2, 7, lat + 1, east)
        ]
        return sides, up, down

    def pole_copy(x, part, send, pole, k):
        target = other(k, lon, nlon)
        return put(
            send.at[part], pole.at[lon], pole_send.at[x, k], pole_recv.at[x, lon], lat, target
        )

    def start_exchange(x, send, recv, pole):
        sides, up, down = near_copies(x, send, recv)

        def pole_start(part):
            pole[lon] = send[part]

            def step(k, c):
                pole_copy(x, part, send, pole, k).start()
                return c

            lax.fori_loop(1, nlon, step, 0)

        @pl.when(at_top)
        def _():
            pole_start(0)

        @pl.when(at_bottom)
        def _():
            pole_start(1)

        for copy in sides:
            copy.start()

        @pl.when(has_north)
        def _():
            for copy in up:
                copy.start()

        @pl.when(has_south)
        def _():
            for copy in down:
                copy.start()

    def finish_exchange(x, send, recv, pole):
        sides, up, down = near_copies(x, send, recv)

        def arrived(slot):
            put(
                send.at[0], recv.at[slot], near_send.at[x, 0], near_recv.at[x, slot], lat, lon
            ).wait_recv()

        for copy in sides:
            copy.wait_send()
        arrived(0)
        arrived(1)

        @pl.when(has_north)
        def _():
            for copy in up:
                copy.wait_send()
            for slot in (2, 3, 4):
                arrived(slot)

        @pl.when(has_south)
        def _():
            for copy in down:
                copy.wait_send()
            for slot in (5, 6, 7):
                arrived(slot)

        @pl.when(at_pole)
        def _():
            def step(k, c):
                pole_copy(x, 0, send, pole, k).wait_send()
                source = other(k, lon, nlon)
                put(
                    send.at[0], pole.at[source], pole_send.at[x, k], pole_recv.at[x, source],
                    lat, lon,
                ).wait_recv()
                return c

            lax.fori_loop(1, nlon, step, 0)

    def map_at(k):
        return jnp.where(at_top, north_map[k], south_map[k])

    def code_at(k):
        return jnp.where(at_top, north_code[k], south_code[k])

    def owner_of_copy():
        def step(k, c):
            hit = map_at(k) == lon
            return jnp.where(hit, k, c[0]), jnp.where(hit, code_at(k), c[1])

        return lax.fori_loop(0, nlon, step, (jnp.int32(0), jnp.int32(0)))

    def turned(row, code):
        i = lax.broadcasted_iota(jnp.int32, (LANES, LANES), 0)
        j = lax.broadcasted_iota(jnp.int32, (LANES, LANES), 1)
        match = (i + (2 * code - 1) * j) == (LANES - 1) * code
        turn = jnp.where(match, 1.0, 0.0).astype(BF16)
        return jnp.dot(row, turn, preferred_element_type=F32)

    def set_ghost_row(wide, row, left, mid, right):
        place = pl.ds(row * chans, chans)
        wide[place, own_rows] = mid.astype(BF16)
        wide[place, ghost_cols] = jnp.where(lane == 0, right.astype(F32), left.astype(F32)).astype(
            BF16
        )

    def set_ghost_cols(wide, from_west, from_east):
        merged = jnp.where(lane % 2 == 0, from_east.astype(F32), from_west.astype(F32))

        def step(h, c):
            place = pl.ds(aligned(h + 1, chans), chans)
            wide[place, ghost_cols] = pltpu.roll(merged, lax.rem(LANES - 2 * h, LANES), 1).astype(
                BF16
            )
            return c

        lax.fori_loop(0, rows, step, 0, unroll=4)

    def edges_into(send, part, wide, packed):
        top, bottom, side = (
            (send.at[i] if part is None else send.at[i, part]) for i in range(3)
        )
        top[...] = wide[pl.ds(chans, chans), own_rows]
        bottom[...] = wide[pl.ds(rows * chans, chans), own_rows]
        side[...] = packed.astype(BF16)

    def pack_edge(h, value, packed):
        keep = jnp.logical_or(lane == 2 * h, lane == lax.rem(2 * h + LANES - 1, LANES))
        return jnp.where(keep, pltpu.roll(value, 2 * h, 1), packed)

    def take_in(source, wide, send, part):
        stage[...] = source[...].astype(F32)

        def step(h, packed):
            value = stage[pl.ds(h, chans, stride=rows), :]
            wide[pl.ds(aligned(h + 1, chans), chans), own_rows] = value.astype(BF16)
            return pack_edge(h, value, packed)

        packed = lax.fori_loop(0, rows, step, jnp.zeros((chans, LANES), F32), unroll=4)
        edges_into(send, part, wide, packed)

    def ghosts_forward(wide, recv, pole, part):
        def got(slot):
            return recv[slot] if part is None else recv[slot, part]

        def strip(k):
            index = map_at(k)
            row = pole[index] if part is None else pole[index, part]
            return turned(row, code_at(k))

        set_ghost_cols(wide, got(0), got(1))

        @pl.when(has_north)
        def _():
            set_ghost_row(wide, 0, got(2), got(3), got(4))

        @pl.when(has_south)
        def _():
            set_ghost_row(wide, rows + 1, got(5), got(6), got(7))

        @pl.when(at_top)
        def _():
            set_ghost_row(wide, 0, strip(west), strip(lon), strip(east))

        @pl.when(at_bottom)
        def _():
            set_ghost_row(wide, rows + 1, strip(west), strip(lon), strip(east))

    def ghosts_backward(wide, recv, pole, part):
        def got(slot):
            return recv[slot] if part is None else recv[slot, part]

        def rim(row):
            source, code = owner_of_copy()

            def strip(shift):
                index = lax.rem(source + shift + nlon, nlon)
                return turned(pole[index] if part is None else pole[index, part], code)

            before, mid, after = strip(-1), strip(0), strip(1)
            flip = code == 1
            set_ghost_row(
                wide, row, jnp.where(flip, after, before), mid, jnp.where(flip, before, after)
            )

        set_ghost_cols(wide, got(0), got(1))

        @pl.when(has_north)
        def _():
            set_ghost_row(wide, 0, got(2), got(3), got(4))

        @pl.when(has_south)
        def _():
            set_ghost_row(wide, rows + 1, got(5), got(6), got(7))

        @pl.when(at_top)
        def _():
            rim(0)

        @pl.when(at_bottom)
        def _():
            rim(rows + 1)

    def rim_weights():
        for kernel_at in range(2):
            base = w_ref[2 + kernel_at]
            for place in range(3):
                wedge[kernel_at * 3 + place] = base

            def replace(place, into, out_of):
                _, code = owner_of_copy()
                full = base.astype(F32)
                shown = lax.broadcasted_iota(jnp.int32, full.shape, 1) // chans == into
                width = full.shape[1]
                i = lax.broadcasted_iota(jnp.int32, (width, width), 0)
                j = lax.broadcasted_iota(jnp.int32, (width, width), 1)
                move = jnp.where(i - out_of * chans == j - into * chans, 1.0, 0.0).astype(BF16)
                moved = jnp.dot(base, move, preferred_element_type=F32)
                swapped = jnp.concatenate(
                    [moved[2 * chans :], moved[chans : 2 * chans], moved[:chans]], axis=0
                )
                chosen = jnp.where(code == 1, swapped, moved)
                wedge[kernel_at * 3 + place] = jnp.where(shown, chosen, full).astype(BF16)

            @pl.when(at_top)
            def _():
                replace(0, 0, 2)

            @pl.when(at_bottom)
            def _():
                replace(2, 2, 0)

    def conv_row(weights, wide, h):
        window = wide[pl.ds(aligned(h, chans), 3 * chans), :]
        y = jnp.dot(weights, window, preferred_element_type=F32)
        left = jnp.where(lane == LANES - 1, y[:chans, LANES:], y[:chans, :LANES])
        right = jnp.where(lane == 0, y[2 * chans :, LANES:], y[2 * chans :, :LANES])
        return (
            pltpu.roll(left, 1, 1) + y[chans : 2 * chans, :LANES] + pltpu.roll(right, LANES - 1, 1)
        )

    def gradient(up_wide, wide, acc):
        group = 4

        def shifted(h):
            g = up_wide[pl.ds(aligned(h + 1, chans), chans), own_rows].astype(F32)
            ahead = pltpu.roll(g, LANES - 1, 1)
            behind = pltpu.roll(g, 1, 1)
            zero = jnp.zeros_like(g)
            first = jnp.concatenate(
                [jnp.where(lane != LANES - 1, ahead, zero), g, jnp.where(lane != 0, behind, zero)],
                axis=0,
            )
            second = jnp.concatenate(
                [jnp.where(lane == LANES - 1, ahead, zero), zero, jnp.where(lane == 0, behind, zero)],
                axis=0,
            )
            return [first.astype(BF16), second.astype(BF16)]

        def step(i, c):
            lefts, rights = [], []
            for u in range(group):
                h = i * group + u
                lefts += shifted(h)
                rights.append(wide[pl.ds(aligned(h, chans), 3 * chans), :])
            acc[:, : 3 * chans] += lax.dot_general(
                jnp.concatenate(lefts, axis=1),
                jnp.concatenate(rights, axis=1),
                (((1,), (1,)), ((), ())),
                preferred_element_type=F32,
            )
            return c

        acc[...] = jnp.zeros_like(acc)
        lax.fori_loop(0, rows // group, step, 0)

    take_in(fields_ref, fwide, send_a, 0)
    take_in(cot_ref, gwide, send_a, 1)
    pl.semaphore_wait(barrier, nlon - 1 + nlat - 1 + diagonals)
    start_exchange(0, send_a, recv_a, pole_a)
    rim_weights()
    finish_exchange(0, send_a, recv_a, pole_a)
    ghosts_forward(fwide, recv_a, pole_a, 0)
    ghosts_backward(gwide, recv_a, pole_a, 1)

    root = math.sqrt(2.0 / math.pi)

    def hidden_row(h, packed):
        u = conv_row(w_ref[0], fwide, h)
        square = u * u
        t = jnp.tanh(root * (u + 0.044715 * (square * u)))
        half = 0.5 * (1.0 + t)
        slope[pl.ds(aligned(h, chans), chans), :] = half + (0.5 * root) * u * (1.0 - t * t) * (
            1.0 + (3 * 0.044715) * square
        )
        value = u * half
        hwide[pl.ds(aligned(h + 1, chans), chans), own_rows] = value.astype(BF16)
        return pack_edge(h, value, packed)

    none = jnp.zeros((chans, LANES), F32)
    packed = lax.fori_loop(0, rows, hidden_row, none, unroll=2)
    edges_into(send_b, None, hwide, packed)
    start_exchange(1, send_b, recv_b, pole_b)

    def weights_at(kernel_at, h):
        place = jnp.where(h == 0, 0, jnp.where(h == rows - 1, 2, 1))
        return wedge[kernel_at * 3 + place]

    def back_row(h, packed):
        back = conv_row(weights_at(1, h), gwide, h)
        value = back * slope[pl.ds(aligned(h, chans), chans), :]
        dwide[pl.ds(aligned(h + 1, chans), chans), own_rows] = value.astype(BF16)
        return pack_edge(h, value, packed)

    packed = lax.fori_loop(0, rows, back_row, none, unroll=2)
    edges_into(send_c, None, dwide, packed)
    start_exchange(2, send_c, recv_c, pole_c)

    gradient(dwide, fwide, acc_one)
    finish_exchange(1, send_b, recv_b, pole_b)
    ghosts_forward(hwide, recv_b, pole_b, None)
    gradient(gwide, hwide, acc_two)

    tall = 3 * chans
    tall_lane = lane_index((tall, LANES))
    rs_send[pl.ds(0, tall), :] = acc_one[:, :LANES].astype(BF16)
    rs_send[pl.ds(tall, tall), :] = acc_two[:, :LANES].astype(BF16)
    rs_send[pl.ds(2 * tall, tall), :] = jnp.where(
        tall_lane < chans, acc_one[:, LANES:], pltpu.roll(acc_two[:, LANES:], chans, 1)
    ).astype(BF16)

    def rows_of(k):
        return pl.ds(aligned(k, piece), piece)

    def rs_copy(k):
        return put(
            rs_send.at[rows_of(k)], rs_recv.at[lon], rs_ssem.at[k], rs_rsem.at[lon], lat, k
        )

    def rs_start(k, c):
        @pl.when(k != lon)
        def _():
            rs_copy(k).start()

        return c

    lax.fori_loop(0, owners, rs_start, 0)

    @pl.when(lon < owners)
    def _():
        rs_recv[lon] = rs_send[rows_of(lon), :]

    def out_row(h, c):
        stage[pl.ds(h, chans, stride=rows), :] = conv_row(w_ref[1], hwide, h)
        return c

    lax.fori_loop(0, rows, out_row, 0, unroll=2)
    out_ref[...] = stage[...].astype(BF16)

    def ar_copy(k):
        return put(
            ar_send, ar_recv.at[lat], ar_ssem.at[k], ar_rsem.at[lat], other(k, lat, nlat), lon
        )

    @pl.when(lon < owners)
    def _():
        def wait(k, c):
            source = other(k, lon, nlon)
            put(
                rs_recv.at[lon], rs_recv.at[source], rs_ssem.at[0], rs_rsem.at[source], lat, lon
            ).wait_recv()
            return c

        lax.fori_loop(1, nlon, wait, 0)
        total = rs_recv[0].astype(F32)
        for k in range(1, nlon):
            total = total + rs_recv[k].astype(F32)
        ar_send[...] = total.astype(BF16)
        ar_recv[lat] = total.astype(BF16)

        def start(k, c):
            ar_copy(k).start()
            return c

        lax.fori_loop(1, nlat, start, 0)

    def rs_wait(k, c):
        @pl.when(k != lon)
        def _():
            rs_copy(k).wait_send()

        return c

    lax.fori_loop(0, owners, rs_wait, 0)

    finish_exchange(2, send_c, recv_c, pole_c)
    ghosts_backward(dwide, recv_c, pole_c, None)

    def df_row(h, c):
        stage[pl.ds(h, chans, stride=rows), :] = conv_row(weights_at(0, h), dwide, h)
        return c

    lax.fori_loop(0, rows, df_row, 0, unroll=2)
    df_ref[...] = stage[...].astype(BF16)

    def ag_copy(k):
        return put(
            ag_buf.at[rows_of(lon)], ag_buf.at[rows_of(lon)], ag_ssem.at[k], ag_rsem.at[lon],
            lat, other(k, lon, nlon),
        )

    @pl.when(lon < owners)
    def _():
        def wait(k, c):
            source = other(k, lat, nlat)
            ar_copy(k).wait_send()
            put(
                ar_send, ar_recv.at[source], ar_ssem.at[k], ar_rsem.at[source], lat, lon
            ).wait_recv()
            return c

        lax.fori_loop(1, nlat, wait, 0)
        total = ar_recv[0].astype(F32)
        for k in range(1, nlat):
            total = total + ar_recv[k].astype(F32)
        ag_buf[rows_of(lon), :] = total.astype(BF16)

        def start(k, c):
            ag_copy(k).start()
            return c

        lax.fori_loop(1, nlon, start, 0)

    def ag_wait(k, c):
        @pl.when(k != lon)
        def _():
            put(
                ag_buf.at[rows_of(k)], ag_buf.at[rows_of(k)], ag_ssem.at[0], ag_rsem.at[k],
                lat, lon,
            ).wait_recv()

        return c

    lax.fori_loop(0, owners, ag_wait, 0)

    @pl.when(lon < owners)
    def _():
        def wait(k, c):
            ag_copy(k).wait_send()
            return c

        lax.fori_loop(1, nlon, wait, 0)

    last = ag_buf[pl.ds(2 * tall, tall), :].astype(F32) * scale
    last_turned = pltpu.roll(last, chans, 1)
    for which, ref in ((0, g1_ref), (1, g2_ref)):
        block = ag_buf[pl.ds(which * tall, tall), :].astype(F32) * scale
        turned_block = pltpu.roll(block, chans, 1)
        for s in range(3):
            cut = slice(s * chans, (s + 1) * chans)
            ref[0, s] = block[cut, :chans]
            ref[1, s] = turned_block[cut, :chans]
            ref[2, s] = (last if which == 0 else last_turned)[cut, :chans]


def on_device(
    nlon, nlat, fields_in, weight_one, weight_two, cotangent,
    north_map, north_code, south_map, south_code,
):
    chans, rows, cols = fields_in.shape
    scale = 1.0 / math.sqrt(float(rows * cols * nlon * nlat))
    tall = 3 * chans

    def forward_form(w):
        return jnp.transpose(w, (1, 2, 0, 3)).reshape(tall, tall)

    def backward_form(w):
        return jnp.transpose(w[::-1, ::-1], (1, 3, 0, 2)).reshape(tall, tall)

    weights = jnp.stack(
        [
            forward_form(weight_one), forward_form(weight_two),
            backward_form(weight_one), backward_form(weight_two),
        ]
    )
    total_rows = 3 * tall
    owners = max(k for k in range(1, nlon + 1) if total_rows % (16 * k) == 0)
    piece = total_rows // owners
    vmem = pl.BlockSpec(memory_space=pltpu.VMEM)
    smem = pl.BlockSpec(memory_space=pltpu.SMEM)
    wide = pltpu.VMEM(((rows + 2) * chans, 2 * LANES), BF16)
    edge = (chans, LANES)
    dma = pltpu.SemaphoreType.DMA
    scratch = [
        pltpu.VMEM((chans * rows, LANES), F32), wide, wide, wide, wide,
        pltpu.VMEM((chans * rows, LANES), F32),
        pltpu.VMEM((6, tall, tall), BF16),
        pltpu.VMEM((3, 2) + edge, BF16), pltpu.VMEM((8, 2) + edge, BF16),
        pltpu.VMEM((nlon, 2) + edge, BF16),
        pltpu.VMEM((3,) + edge, BF16), pltpu.VMEM((8,) + edge, BF16),
        pltpu.VMEM((nlon,) + edge, BF16),
        pltpu.VMEM((3,) + edge, BF16), pltpu.VMEM((8,) + edge, BF16),
        pltpu.VMEM((nlon,) + edge, BF16),
        pltpu.VMEM((tall, 2 * LANES), F32), pltpu.VMEM((tall, 2 * LANES), F32),
        pltpu.VMEM((total_rows, LANES), BF16), pltpu.VMEM((nlon, piece, LANES), BF16),
        pltpu.VMEM((piece, LANES), BF16), pltpu.VMEM((nlat, piece, LANES), BF16),
        pltpu.VMEM((total_rows, LANES), BF16),
        dma((3, 8)), dma((3, 8)), dma((3, nlon)), dma((3, nlon)),
        dma((nlon,)), dma((nlon,)), dma((nlat,)), dma((nlat,)), dma((nlon,)), dma((nlon,)),
    ]
    output, d_fields, grad_one, grad_two = pl.pallas_call(
        functools.partial(kernel, nlon, nlat, rows, chans, owners, scale),
        out_shape=(
            jax.ShapeDtypeStruct((chans * rows, cols), BF16),
            jax.ShapeDtypeStruct((chans * rows, cols), BF16),
            jax.ShapeDtypeStruct((3, 3, chans, chans), F32),
            jax.ShapeDtypeStruct((3, 3, chans, chans), F32),
        ),
        in_specs=[vmem, vmem, vmem, smem, smem, smem, smem],
        out_specs=(vmem, vmem, vmem, vmem),
        scratch_shapes=scratch,
        compiler_params=pltpu.CompilerParams(
            collective_id=0, has_side_effects=True, vmem_limit_bytes=48 * 1024 * 1024
        ),
    )(
        fields_in.reshape(chans * rows, cols), cotangent.reshape(chans * rows, cols), weights,
        north_map, north_code, south_map, south_code,
    )
    shape = (chans, rows, cols)
    return (output.reshape(shape), d_fields.reshape(shape), grad_one, grad_two)


def solution(mesh):
    placed = (P(None, "lat", "lon"), P(), P(), P(None, "lat", "lon"), P(), P(), P(), P())
    return jax.shard_map(
        functools.partial(on_device, mesh.shape["lon"], mesh.shape["lat"]),
        mesh=mesh,
        in_specs=placed,
        out_specs=(P(None, "lat", "lon"), P(None, "lat", "lon"), P(), P()),
        check_vma=False,
    )
```

```python
import functools
import math

import jax
import jax.numpy as jnp
from jax import lax
from jax.experimental import pallas as pl
from jax.experimental.pallas import tpu as pltpu
from jax.sharding import PartitionSpec as P

MESH = pl.DeviceIdType.MESH
LANES = 128
F32 = jnp.float32
BF16 = jnp.bfloat16


def lane_index(shape):
    return lax.broadcasted_iota(jnp.int32, shape, len(shape) - 1)


def aligned(start, step):
    return pl.multiple_of(start * step, step)


def kernel(
    nlon, nlat, rows, chans, owners, scale,
    fields_ref, cot_ref, one_ref, two_ref, north_map, north_code, south_map, south_code,
    out_ref, df_ref, g1_ref, g2_ref,
    stage, stage_two, fwide, gwide, hwide, dwide, slope, w_ref, wedge,
    send_a, recv_a, pole_a, send_b, recv_b, pole_b, send_c, recv_c, pole_c,
    acc_one, acc_two, rs_send, rs_recv, ar_send, ar_recv, ag_buf,
    near_send, near_recv, pole_send, pole_recv,
    rs_ssem, rs_rsem, ar_ssem, ar_rsem, ag_ssem, ag_rsem,
):
    lon = lax.axis_index("lon")
    lat = lax.axis_index("lat")
    west = lax.rem(lon + nlon - 1, nlon)
    east = lax.rem(lon + 1, nlon)
    has_north = lat > 0
    has_south = lat < nlat - 1
    at_top = lat == 0
    at_pole = jnp.logical_or(lat == 0, lat == nlat - 1)
    at_bottom = lat == nlat - 1
    lane = lane_index((chans, LANES))
    own_rows = pl.ds(0, LANES)
    ghost_cols = pl.ds(LANES, LANES)
    piece = ag_buf.shape[0] // owners

    def other(k, me, count):
        return lax.rem(me + k, count)

    barrier = pltpu.get_barrier_semaphore()

    def greet(lat_at, lon_at):
        pl.semaphore_signal(
            barrier, inc=1, device_id={"lon": lon_at, "lat": lat_at}, device_id_type=MESH
        )

    def greet_lon(k, c):
        greet(lat, other(k, lon, nlon))
        return c

    def greet_lat(k, c):
        greet(other(k, lat, nlat), lon)
        return c

    lax.fori_loop(1, nlon, greet_lon, 0)
    lax.fori_loop(1, nlat, greet_lat, 0)

    @pl.when(has_north)
    def _():
        greet(lat - 1, west)
        greet(lat - 1, east)

    @pl.when(has_south)
    def _():
        greet(lat + 1, west)
        greet(lat + 1, east)

    diagonals = 2 * has_north.astype(jnp.int32) + 2 * has_south.astype(jnp.int32)

    def put(src, dst, ssem, rsem, lat_at, lon_at):
        return pltpu.make_async_remote_copy(
            src_ref=src, dst_ref=dst, send_sem=ssem, recv_sem=rsem,
            device_id={"lon": lon_at, "lat": lat_at}, device_id_type=MESH,
        )

    def near_copies(x, send, recv):
        def one(part, slot, at, lat_at, lon_at):
            return put(
                send.at[part], recv.at[slot], near_send.at[x, at], near_recv.at[x, slot],
                lat_at, lon_at,
            )

        sides = [one(2, 1, 0, lat, west), one(2, 0, 1, lat, east)]
        up = [
            one(0, 7, 2, lat - 1, west), one(0, 6, 3, lat - 1, lon), one(0, 5, 4, lat - 1, east)
        ]
        down = [
            one(1, 4, 5, lat + 1, west), one(1, 3, 6, lat + 1, lon), one(1, 2, 7, lat + 1, east)
        ]
        return sides, up, down

    def pole_copy(x, part, send, pole, k):
        target = other(k, lon, nlon)
        return put(
            send.at[part], pole.at[lon], pole_send.at[x, k], pole_recv.at[x, lon], lat, target
        )

    def start_exchange(x, send, recv, pole):
        sides, up, down = near_copies(x, send, recv)

        def pole_start(part):
            pole[lon] = send[part]

            def step(k, c):
                pole_copy(x, part, send, pole, k).start()
                return c

            lax.fori_loop(1, nlon, step, 0)

        @pl.when(at_top)
        def _():
            pole_start(0)

        @pl.when(at_bottom)
        def _():
            pole_start(1)

        for copy in sides:
            copy.start()

        @pl.when(has_north)
        def _():
            for copy in up:
                copy.start()

        @pl.when(has_south)
        def _():
            for copy in down:
                copy.start()

    def finish_exchange(x, send, recv, pole):
        sides, up, down = near_copies(x, send, recv)

        def arrived(slot):
            put(
                send.at[0], recv.at[slot], near_send.at[x, 0], near_recv.at[x, slot], lat, lon
            ).wait_recv()

        for copy in sides:
            copy.wait_send()
        arrived(0)
        arrived(1)

        @pl.when(has_north)
        def _():
            for copy in up:
                copy.wait_send()
            for slot in (2, 3, 4):
                arrived(slot)

        @pl.when(has_south)
        def _():
            for copy in down:
                copy.wait_send()
            for slot in (5, 6, 7):
                arrived(slot)

        @pl.when(at_pole)
        def _():
            def step(k, c):
                pole_copy(x, 0, send, pole, k).wait_send()
                source = other(k, lon, nlon)
                put(
                    send.at[0], pole.at[source], pole_send.at[x, k], pole_recv.at[x, source],
                    lat, lon,
                ).wait_recv()
                return c

            lax.fori_loop(1, nlon, step, 0)

    def map_at(k):
        return jnp.where(at_top, north_map[k], south_map[k])

    def code_at(k):
        return jnp.where(at_top, north_code[k], south_code[k])

    def find_owner(k, c):
        hit = map_at(k) == lon
        return jnp.where(hit, k, c[0]), jnp.where(hit, code_at(k), c[1])

    rim_source, rim_code = lax.fori_loop(0, nlon, find_owner, (jnp.int32(0), jnp.int32(0)))

    def turned(row, code):
        i = lax.broadcasted_iota(jnp.int32, (LANES, LANES), 0)
        j = lax.broadcasted_iota(jnp.int32, (LANES, LANES), 1)
        match = (i + (2 * code - 1) * j) == (LANES - 1) * code
        turn = jnp.where(match, 1.0, 0.0).astype(BF16)
        return jnp.dot(row, turn, preferred_element_type=F32)

    def set_ghost_row(wide, row, left, mid, right):
        place = pl.ds(row * chans, chans)
        wide[place, own_rows] = mid.astype(BF16)
        wide[place, ghost_cols] = jnp.where(lane == 0, right.astype(F32), left.astype(F32)).astype(
            BF16
        )

    def set_ghost_cols(wide, from_west, from_east):
        merged = jnp.where(lane % 2 == 0, from_east.astype(F32), from_west.astype(F32))

        def step(h, c):
            place = pl.ds(aligned(h + 1, chans), chans)
            wide[place, ghost_cols] = pltpu.roll(merged, lax.rem(LANES - 2 * h, LANES), 1).astype(
                BF16
            )
            return c

        lax.fori_loop(0, rows, step, 0, unroll=32)

    def edges_into(send, part, wide, packed):
        top, bottom, side = (
            (send.at[i] if part is None else send.at[i, part]) for i in range(3)
        )
        top[...] = wide[pl.ds(chans, chans), own_rows]
        bottom[...] = wide[pl.ds(rows * chans, chans), own_rows]
        side[...] = packed.astype(BF16)

    def pack_edge(h, value, packed):
        keep = jnp.logical_or(lane == 2 * h, lane == lax.rem(2 * h + LANES - 1, LANES))
        return jnp.where(keep, pltpu.roll(value, 2 * h, 1), packed)

    def take_in(source, stage, wide, send, part):
        stage[...] = source[...].astype(F32)

        def step(h, packed):
            value = stage[pl.ds(h, chans, stride=rows), :]
            wide[pl.ds(aligned(h + 1, chans), chans), own_rows] = value.astype(BF16)
            return pack_edge(h, value, packed)

        packed = lax.fori_loop(0, rows, step, jnp.zeros((chans, LANES), F32), unroll=32)
        edges_into(send, part, wide, packed)

    def ghosts_forward(wide, recv, pole, part):
        def got(slot):
            return recv[slot] if part is None else recv[slot, part]

        def strip(k):
            index = map_at(k)
            row = pole[index] if part is None else pole[index, part]
            return turned(row, code_at(k))

        set_ghost_cols(wide, got(0), got(1))

        @pl.when(has_north)
        def _():
            set_ghost_row(wide, 0, got(2), got(3), got(4))

        @pl.when(has_south)
        def _():
            set_ghost_row(wide, rows + 1, got(5), got(6), got(7))

        @pl.when(at_top)
        def _():
            set_ghost_row(wide, 0, strip(west), strip(lon), strip(east))

        @pl.when(at_bottom)
        def _():
            set_ghost_row(wide, rows + 1, strip(west), strip(lon), strip(east))

    def ghosts_backward(wide, recv, pole, part):
        def got(slot):
            return recv[slot] if part is None else recv[slot, part]

        def rim(row):
            def strip(shift):
                index = lax.rem(rim_source + shift + nlon, nlon)
                return turned(pole[index] if part is None else pole[index, part], rim_code)

            before, mid, after = strip(-1), strip(0), strip(1)
            flip = rim_code == 1
            set_ghost_row(
                wide, row, jnp.where(flip, after, before), mid, jnp.where(flip, before, after)
            )

        set_ghost_cols(wide, got(0), got(1))

        @pl.when(has_north)
        def _():
            set_ghost_row(wide, 0, got(2), got(3), got(4))

        @pl.when(has_south)
        def _():
            set_ghost_row(wide, rows + 1, got(5), got(6), got(7))

        @pl.when(at_top)
        def _():
            rim(0)

        @pl.when(at_bottom)
        def _():
            rim(rows + 1)

    def weight_forms():
        def spot(shape, shift):
            i = lax.broadcasted_iota(jnp.int32, shape, 0)
            j = lax.broadcasted_iota(jnp.int32, shape, 1)
            return jnp.where(i + shift == j, 1.0, 0.0).astype(BF16)

        tall = 3 * chans
        for at, ref in ((0, one_ref), (1, two_ref)):
            total = jnp.zeros((tall, tall), F32)
            for r in range(3):
                total = total + jnp.dot(
                    ref[r * tall : (r + 1) * tall, :],
                    spot((chans, tall), r * chans),
                    preferred_element_type=F32,
                )
            w_ref[at] = total.astype(BF16)
            for s in range(3):
                blocks = [
                    ref[((2 - r) * 3 + 2 - s) * chans : ((2 - r) * 3 + 3 - s) * chans, :]
                    for r in range(3)
                ]
                w_ref[2 + at, s * chans : (s + 1) * chans, :] = lax.dot_general(
                    spot((chans, chans), 0),
                    jnp.concatenate(blocks, axis=0),
                    (((1,), (1,)), ((), ())),
                    preferred_element_type=F32,
                ).astype(BF16)

    def rim_weights():
        for kernel_at in range(2):
            base = w_ref[2 + kernel_at]
            for place in range(3):
                wedge[kernel_at * 3 + place] = base

            def replace(place, into, out_of):
                full = base.astype(F32)
                shown = lax.broadcasted_iota(jnp.int32, full.shape, 1) // chans == into
                width = full.shape[1]
                i = lax.broadcasted_iota(jnp.int32, (width, width), 0)
                j = lax.broadcasted_iota(jnp.int32, (width, width), 1)
                move = jnp.where(i - out_of * chans == j - into * chans, 1.0, 0.0).astype(BF16)
                moved = jnp.dot(base, move, preferred_element_type=F32)
                swapped = jnp.concatenate(
                    [moved[2 * chans :], moved[chans : 2 * chans], moved[:chans]], axis=0
                )
                chosen = jnp.where(rim_code == 1, swapped, moved)
                wedge[kernel_at * 3 + place] = jnp.where(shown, chosen, full).astype(BF16)

            @pl.when(at_top)
            def _():
                replace(0, 0, 2)

            @pl.when(at_bottom)
            def _():
                replace(2, 2, 0)

    def conv_row(weights, wide, h):
        window = wide[pl.ds(aligned(h, chans), 3 * chans), :]
        y = jnp.dot(weights, window, preferred_element_type=F32)
        left = jnp.where(lane == LANES - 1, y[:chans, LANES:], y[:chans, :LANES])
        right = jnp.where(lane == 0, y[2 * chans :, LANES:], y[2 * chans :, :LANES])
        return (
            pltpu.roll(left, 1, 1) + y[chans : 2 * chans, :LANES] + pltpu.roll(right, LANES - 1, 1)
        )

    def gradient(up_wide, wide, acc):
        group = 16

        def shifted(h):
            g = up_wide[pl.ds(aligned(h + 1, chans), chans), own_rows].astype(F32)
            ahead = pltpu.roll(g, LANES - 1, 1)
            behind = pltpu.roll(g, 1, 1)
            zero = jnp.zeros_like(g)
            first = jnp.concatenate(
                [jnp.where(lane != LANES - 1, ahead, zero), g, jnp.where(lane != 0, behind, zero)],
                axis=0,
            )
            second = jnp.concatenate(
                [jnp.where(lane == LANES - 1, ahead, zero), zero, jnp.where(lane == 0, behind, zero)],
                axis=0,
            )
            return [first.astype(BF16), second.astype(BF16)]

        def step(i, c):
            lefts, rights = [], []
            for u in range(group):
                h = i * group + u
                lefts += shifted(h)
                rights.append(wide[pl.ds(aligned(h, chans), 3 * chans), :])
            acc[:, : 3 * chans] += lax.dot_general(
                jnp.concatenate(lefts, axis=1),
                jnp.concatenate(rights, axis=1),
                (((1,), (1,)), ((), ())),
                preferred_element_type=F32,
            )
            return c

        acc[...] = jnp.zeros_like(acc)
        lax.fori_loop(0, rows // group, step, 0)

    take_in(fields_ref, stage, fwide, send_a, 0)
    take_in(cot_ref, stage_two, gwide, send_a, 1)
    pl.semaphore_wait(barrier, nlon - 1 + nlat - 1 + diagonals)
    start_exchange(0, send_a, recv_a, pole_a)
    weight_forms()
    rim_weights()
    finish_exchange(0, send_a, recv_a, pole_a)
    ghosts_forward(fwide, recv_a, pole_a, 0)
    ghosts_backward(gwide, recv_a, pole_a, 1)

    root = math.sqrt(2.0 / math.pi)

    def hidden_row(h, packed):
        u = conv_row(w_ref[0], fwide, h)
        square = u * u
        t = jnp.tanh(root * (u + 0.044715 * (square * u)))
        half = 0.5 * (1.0 + t)
        slope[pl.ds(aligned(h, chans), chans), :] = half + (0.5 * root) * u * (1.0 - t * t) * (
            1.0 + (3 * 0.044715) * square
        )
        value = u * half
        hwide[pl.ds(aligned(h + 1, chans), chans), own_rows] = value.astype(BF16)
        return pack_edge(h, value, packed)

    none = jnp.zeros((chans, LANES), F32)
    packed = lax.fori_loop(0, rows, hidden_row, none, unroll=32)
    edges_into(send_b, None, hwide, packed)
    start_exchange(1, send_b, recv_b, pole_b)

    def weights_at(kernel_at, h):
        place = jnp.where(h == 0, 0, jnp.where(h == rows - 1, 2, 1))
        return wedge[kernel_at * 3 + place]

    def back_row(h, packed):
        back = conv_row(weights_at(1, h), gwide, h)
        value = back * slope[pl.ds(aligned(h, chans), chans), :]
        dwide[pl.ds(aligned(h + 1, chans), chans), own_rows] = value.astype(BF16)
        return pack_edge(h, value, packed)

    packed = lax.fori_loop(0, rows, back_row, none, unroll=32)
    edges_into(send_c, None, dwide, packed)
    start_exchange(2, send_c, recv_c, pole_c)

    gradient(dwide, fwide, acc_one)
    finish_exchange(1, send_b, recv_b, pole_b)
    ghosts_forward(hwide, recv_b, pole_b, None)
    gradient(gwide, hwide, acc_two)

    tall = 3 * chans
    tall_lane = lane_index((tall, LANES))
    rs_send[pl.ds(0, tall), :] = acc_one[:, :LANES].astype(BF16)
    rs_send[pl.ds(tall, tall), :] = acc_two[:, :LANES].astype(BF16)
    rs_send[pl.ds(2 * tall, tall), :] = jnp.where(
        tall_lane < chans, acc_one[:, LANES:], pltpu.roll(acc_two[:, LANES:], chans, 1)
    ).astype(BF16)

    def rows_of(k):
        return pl.ds(aligned(k, piece), piece)

    def rs_copy(k):
        return put(
            rs_send.at[rows_of(k)], rs_recv.at[lon], rs_ssem.at[k], rs_rsem.at[lon], lat, k
        )

    def rs_start(k, c):
        @pl.when(k != lon)
        def _():
            rs_copy(k).start()

        return c

    lax.fori_loop(0, owners, rs_start, 0)

    @pl.when(lon < owners)
    def _():
        rs_recv[lon] = rs_send[rows_of(lon), :]

    def out_row(h, c):
        stage[pl.ds(h, chans, stride=rows), :] = conv_row(w_ref[1], hwide, h)
        return c

    lax.fori_loop(0, rows, out_row, 0, unroll=32)
    out_ref[...] = stage[...].astype(BF16)

    def ar_copy(k):
        return put(
            ar_send, ar_recv.at[lat], ar_ssem.at[k], ar_rsem.at[lat], other(k, lat, nlat), lon
        )

    @pl.when(lon < owners)
    def _():
        def wait(k, c):
            source = other(k, lon, nlon)
            put(
                rs_recv.at[lon], rs_recv.at[source], rs_ssem.at[0], rs_rsem.at[source], lat, lon
            ).wait_recv()
            return c

        lax.fori_loop(1, nlon, wait, 0)
        total = rs_recv[0].astype(F32)
        for k in range(1, nlon):
            total = total + rs_recv[k].astype(F32)
        ar_send[...] = total.astype(BF16)
        ar_recv[lat] = total.astype(BF16)

        def start(k, c):
            ar_copy(k).start()
            return c

        lax.fori_loop(1, nlat, start, 0)

    def rs_wait(k, c):
        @pl.when(k != lon)
        def _():
            rs_copy(k).wait_send()

        return c

    lax.fori_loop(0, owners, rs_wait, 0)

    finish_exchange(2, send_c, recv_c, pole_c)
    ghosts_backward(dwide, recv_c, pole_c, None)

    def df_row(h, c):
        stage[pl.ds(h, chans, stride=rows), :] = conv_row(weights_at(0, h), dwide, h)
        return c

    lax.fori_loop(0, rows, df_row, 0, unroll=32)
    df_ref[...] = stage[...].astype(BF16)

    def ag_copy(k):
        return put(
            ag_buf.at[rows_of(lon)], ag_buf.at[rows_of(lon)], ag_ssem.at[k], ag_rsem.at[lon],
            lat, other(k, lon, nlon),
        )

    @pl.when(lon < owners)
    def _():
        def wait(k, c):
            source = other(k, lat, nlat)
            ar_copy(k).wait_send()
            put(
                ar_send, ar_recv.at[source], ar_ssem.at[k], ar_rsem.at[source], lat, lon
            ).wait_recv()
            return c

        lax.fori_loop(1, nlat, wait, 0)
        total = ar_recv[0].astype(F32)
        for k in range(1, nlat):
            total = total + ar_recv[k].astype(F32)
        ag_buf[rows_of(lon), :] = total.astype(BF16)

        def start(k, c):
            ag_copy(k).start()
            return c

        lax.fori_loop(1, nlon, start, 0)

    def ag_wait(k, c):
        @pl.when(k != lon)
        def _():
            put(
                ag_buf.at[rows_of(k)], ag_buf.at[rows_of(k)], ag_ssem.at[0], ag_rsem.at[k],
                lat, lon,
            ).wait_recv()

        return c

    lax.fori_loop(0, owners, ag_wait, 0)

    @pl.when(lon < owners)
    def _():
        def wait(k, c):
            ag_copy(k).wait_send()
            return c

        lax.fori_loop(1, nlon, wait, 0)

    last = ag_buf[pl.ds(2 * tall, tall), :].astype(F32) * scale
    last_turned = pltpu.roll(last, chans, 1)
    for which, ref in ((0, g1_ref), (1, g2_ref)):
        block = ag_buf[pl.ds(which * tall, tall), :].astype(F32) * scale
        turned_block = pltpu.roll(block, chans, 1)
        for s in range(3):
            cut = slice(s * chans, (s + 1) * chans)
            ref[0, s] = block[cut, :chans]
            ref[1, s] = turned_block[cut, :chans]
            ref[2, s] = (last if which == 0 else last_turned)[cut, :chans]


def on_device(
    nlon, nlat, fields_in, weight_one, weight_two, cotangent,
    north_map, north_code, south_map, south_code,
):
    chans, rows, cols = fields_in.shape
    scale = 1.0 / math.sqrt(float(rows * cols * nlon * nlat))
    tall = 3 * chans
    total_rows = 3 * tall
    owners = max(k for k in range(1, nlon + 1) if total_rows % (16 * k) == 0)
    piece = total_rows // owners
    vmem = pl.BlockSpec(memory_space=pltpu.VMEM)
    smem = pl.BlockSpec(memory_space=pltpu.SMEM)
    wide = pltpu.VMEM(((rows + 2) * chans, 2 * LANES), BF16)
    edge = (chans, LANES)
    dma = pltpu.SemaphoreType.DMA
    scratch = [
        pltpu.VMEM((chans * rows, LANES), F32), pltpu.VMEM((chans * rows, LANES), F32),
        wide, wide, wide, wide,
        pltpu.VMEM((chans * rows, LANES), F32),
        pltpu.VMEM((4, tall, tall), BF16),
        pltpu.VMEM((6, tall, tall), BF16),
        pltpu.VMEM((3, 2) + edge, BF16), pltpu.VMEM((8, 2) + edge, BF16),
        pltpu.VMEM((nlon, 2) + edge, BF16),
        pltpu.VMEM((3,) + edge, BF16), pltpu.VMEM((8,) + edge, BF16),
        pltpu.VMEM((nlon,) + edge, BF16),
        pltpu.VMEM((3,) + edge, BF16), pltpu.VMEM((8,) + edge, BF16),
        pltpu.VMEM((nlon,) + edge, BF16),
        pltpu.VMEM((tall, 2 * LANES), F32), pltpu.VMEM((tall, 2 * LANES), F32),
        pltpu.VMEM((total_rows, LANES), BF16), pltpu.VMEM((nlon, piece, LANES), BF16),
        pltpu.VMEM((piece, LANES), BF16), pltpu.VMEM((nlat, piece, LANES), BF16),
        pltpu.VMEM((total_rows, LANES), BF16),
        dma((3, 8)), dma((3, 8)), dma((3, nlon)), dma((3, nlon)),
        dma((nlon,)), dma((nlon,)), dma((nlat,)), dma((nlat,)), dma((nlon,)), dma((nlon,)),
    ]
    output, d_fields, grad_one, grad_two = pl.pallas_call(
        functools.partial(kernel, nlon, nlat, rows, chans, owners, scale),
        out_shape=(
            jax.ShapeDtypeStruct((chans * rows, cols), BF16),
            jax.ShapeDtypeStruct((chans * rows, cols), BF16),
            jax.ShapeDtypeStruct((3, 3, chans, chans), F32),
            jax.ShapeDtypeStruct((3, 3, chans, chans), F32),
        ),
        in_specs=[vmem, vmem, vmem, vmem, smem, smem, smem, smem],
        out_specs=(vmem, vmem, vmem, vmem),
        scratch_shapes=scratch,
        compiler_params=pltpu.CompilerParams(
            collective_id=0, has_side_effects=True, vmem_limit_bytes=48 * 1024 * 1024
        ),
    )(
        fields_in.reshape(chans * rows, cols), cotangent.reshape(chans * rows, cols),
        weight_one.reshape(9 * chans, chans), weight_two.reshape(9 * chans, chans),
        north_map, north_code, south_map, south_code,
    )
    shape = (chans, rows, cols)
    return (output.reshape(shape), d_fields.reshape(shape), grad_one, grad_two)


def solution(mesh):
    placed = (P(None, "lat", "lon"), P(), P(), P(None, "lat", "lon"), P(), P(), P(), P())
    return jax.shard_map(
        functools.partial(on_device, mesh.shape["lon"], mesh.shape["lat"]),
        mesh=mesh,
        in_specs=placed,
        out_specs=(P(None, "lat", "lon"), P(None, "lat", "lon"), P(), P()),
        check_vma=False,
    )
```

```python
import functools
import math

import jax
import jax.numpy as jnp
from jax import lax
from jax.experimental import pallas as pl
from jax.experimental.pallas import tpu as pltpu
from jax.sharding import PartitionSpec as P

MESH = pl.DeviceIdType.MESH
LANES = 128
F32 = jnp.float32
BF16 = jnp.bfloat16
NT = (((1,), (1,)), ((), ()))
FIELDS, COT, HIDDEN, DPRE = range(4)


def aligned(start, step):
    return pl.multiple_of(start * step, step)


def kernel(
    nlon, nlat, planes, rows, chans, owners, scale,
    fields_hbm, cot_hbm, one_hbm, two_hbm, north_map, north_code, south_map, south_code,
    out_hbm, df_hbm, g1_ref, g2_ref,
    fields_in, cot_in, one_ref, two_ref, out_buf, df_buf,
    stage, stage_two, fwide, gwide, hwide, dwide, slope, w_ref, wedge, rim_row,
    send, recv, pole_f, pole_c, pole_h, pole_d, acc_one, acc_two, sums,
    rs_send, rs_recv, ar_send, ar_recv, ag_buf,
    local_sem, near_send, near_recv, pole_send, pole_recv,
    rs_ssem, rs_rsem, ar_ssem, ar_rsem, ag_ssem, ag_rsem,
):
    lon = lax.axis_index("lon")
    lat = lax.axis_index("lat")
    depth = nlat // planes
    plane = lax.div(lat, depth)
    z = lax.rem(lat, depth)
    group = nlon * planes
    mine = lon + nlon * plane
    west = lax.rem(lon + nlon - 1, nlon)
    east = lax.rem(lon + 1, nlon)
    has_north = lat > 0
    has_south = lat < nlat - 1
    at_top = lat == 0
    at_bottom = lat == nlat - 1
    at_pole = jnp.logical_or(at_top, at_bottom)
    tall = 3 * chans
    lane = lax.broadcasted_iota(jnp.int32, (chans, LANES), 1)
    own = pl.ds(0, LANES)
    ghost_cols = pl.ds(LANES, LANES)
    piece = 3 * tall // owners

    def in_group(g):
        return lax.div(g, nlon) * depth + z, lax.rem(g, nlon)

    def group_peer(k):
        return lax.rem(mine + k, group)

    def along_z(k):
        return plane * depth + lax.rem(z + k, depth), lon

    spread_owners = group % 4 == 0 and owners == group // 4 * 3

    def owner_at(j):
        return lax.div(j, 3) * 4 + lax.rem(j, 3) if spread_owners else j

    if spread_owners:
        owns = lax.rem(mine, 4) < 3
        own_piece = lax.div(mine, 4) * 3 + lax.rem(mine, 4)
    else:
        owns = mine < owners
        own_piece = mine

    barrier = pltpu.get_barrier_semaphore()

    def greet(place):
        pl.semaphore_signal(
            barrier, inc=1, device_id={"lat": place[0], "lon": place[1]}, device_id_type=MESH
        )

    def greet_group(k, c):
        greet(in_group(group_peer(k)))
        return c

    def greet_z(k, c):
        greet(along_z(k))
        return c

    @pl.when(has_north)
    def _():
        for at in (west, lon, east):
            greet((lat - 1, at))

    @pl.when(has_south)
    def _():
        for at in (west, lon, east):
            greet((lat + 1, at))

    lax.fori_loop(1, group, greet_group, 0)
    lax.fori_loop(1, depth, greet_z, 0)
    beside = 3 * has_north.astype(jnp.int32) + 3 * has_south.astype(jnp.int32)

    loads = [
        pltpu.make_async_copy(source, target, local_sem.at[i])
        for i, (source, target) in enumerate(
            [(fields_hbm, fields_in), (cot_hbm, cot_in), (one_hbm, one_ref), (two_hbm, two_ref)]
        )
    ]
    for load in loads:
        load.start()

    def put(src, dst, ssem, rsem, place):
        return pltpu.make_async_remote_copy(
            src_ref=src, dst_ref=dst, send_sem=ssem, recv_sem=rsem,
            device_id={"lat": place[0], "lon": place[1]}, device_id_type=MESH,
        )

    here = (lat, lon)
    pole = (pole_f, pole_c, pole_h, pole_d)

    def near_copies(x):
        def one(part, slot, at, place):
            return put(
                send.at[x, part], recv.at[x, slot], near_send.at[x, at], near_recv.at[x, slot],
                place,
            )

        sides = [one(2, 1, 0, (lat, west)), one(2, 0, 1, (lat, east))]
        up = [
            one(0, 7, 2, (lat - 1, west)), one(0, 6, 3, (lat - 1, lon)), one(0, 5, 4, (lat - 1, east))
        ]
        down = [
            one(1, 4, 5, (lat + 1, west)), one(1, 3, 6, (lat + 1, lon)), one(1, 2, 7, (lat + 1, east))
        ]
        return sides, up, down

    def pole_copy(x, part, k):
        return put(
            send.at[x, part], pole[x].at[lon], pole_send.at[x, k], pole_recv.at[x, lon],
            (lat, lax.rem(lon + k, nlon)),
        )

    def start_exchange(x):
        sides, up, down = near_copies(x)
        for copy in sides:
            copy.start()

        @pl.when(has_north)
        def _():
            for copy in up:
                copy.start()

        @pl.when(has_south)
        def _():
            for copy in down:
                copy.start()

        def pole_start(part):
            def step(k, c):
                pole_copy(x, part, k).start()
                return c

            lax.fori_loop(1, nlon, step, 0)
            pole[x][lon] = send[x, part]

        @pl.when(at_top)
        def _():
            pole_start(0)

        @pl.when(at_bottom)
        def _():
            pole_start(1)

    def arrived(x, slot):
        put(
            send.at[x, 0], recv.at[x, slot], near_send.at[x, 0], near_recv.at[x, slot], here
        ).wait_recv()

    def wait_rows(x):
        @pl.when(has_north)
        def _():
            for slot in (2, 3, 4):
                arrived(x, slot)

        @pl.when(has_south)
        def _():
            for slot in (5, 6, 7):
                arrived(x, slot)

        @pl.when(at_pole)
        def _():
            def step(k, c):
                source = lax.rem(lon + k, nlon)
                put(
                    send.at[x, 0], pole[x].at[source], pole_send.at[x, k],
                    pole_recv.at[x, source], here,
                ).wait_recv()
                return c

            lax.fori_loop(1, nlon, step, 0)

    def wait_sent(x):
        sides, up, down = near_copies(x)
        for copy in sides:
            copy.wait_send()

        @pl.when(has_north)
        def _():
            for copy in up:
                copy.wait_send()

        @pl.when(has_south)
        def _():
            for copy in down:
                copy.wait_send()

        @pl.when(at_pole)
        def _():
            def step(k, c):
                pole_copy(x, 0, k).wait_send()
                return c

            lax.fori_loop(1, nlon, step, 0)

    def map_at(k):
        return jnp.where(at_top, north_map[k], south_map[k])

    def code_at(k):
        return jnp.where(at_top, north_code[k], south_code[k])

    def find_owner(k, c):
        hit = map_at(k) == lon
        return jnp.where(hit, k, c[0]), jnp.where(hit, code_at(k), c[1])

    rim_source, rim_code = lax.fori_loop(0, nlon, find_owner, (jnp.int32(0), jnp.int32(0)))

    def turned(row, code):
        i = lax.broadcasted_iota(jnp.int32, (LANES, LANES), 0)
        j = lax.broadcasted_iota(jnp.int32, (LANES, LANES), 1)
        match = (i + (2 * code - 1) * j) == (LANES - 1) * code
        turn = jnp.where(match, 1.0, 0.0).astype(BF16)
        return jnp.dot(row, turn, preferred_element_type=F32)

    def set_ghost_row(wide, row, left, mid, right):
        place = pl.ds(row * chans, chans)
        wide[place, own] = mid.astype(BF16)
        wide[place, ghost_cols] = jnp.where(lane == 0, right.astype(F32), left.astype(F32)).astype(
            BF16
        )

    def set_ghost_cols(x, wide):
        arrived(x, 0)
        arrived(x, 1)
        merged = jnp.where(lane % 2 == 0, recv[x, 1].astype(F32), recv[x, 0].astype(F32))

        def step(h, c):
            place = pl.ds(aligned(h + 1, chans), chans)
            wide[place, ghost_cols] = pltpu.roll(merged, lax.rem(LANES - 2 * h, LANES), 1).astype(
                BF16
            )
            return c

        lax.fori_loop(0, rows, step, 0, unroll=rows)

    def pack_edge(h, value, packed):
        keep = jnp.logical_or(lane == 2 * h, lane == lax.rem(2 * h + LANES - 1, LANES))
        return jnp.where(keep, pltpu.roll(value, 2 * h, 1), packed)

    def send_edges(x, wide, packed):
        send[x, 0] = wide[pl.ds(chans, chans), own]
        send[x, 1] = wide[pl.ds(rows * chans, chans), own]
        send[x, 2] = packed.astype(BF16)
        start_exchange(x)

    none = jnp.zeros((chans, LANES), F32)

    def take_in(source, stage, wide):
        stage[...] = source[...].astype(F32)

        def step(h, packed):
            value = stage[pl.ds(h, chans, stride=rows), :]
            wide[pl.ds(aligned(h + 1, chans), chans), own] = value.astype(BF16)
            return pack_edge(h, value, packed)

        return lax.fori_loop(0, rows, step, none, unroll=rows)

    def set_ghost_rows(x, wide, forward):
        wait_rows(x)

        @pl.when(has_north)
        def _():
            set_ghost_row(wide, 0, recv[x, 2], recv[x, 3], recv[x, 4])

        @pl.when(has_south)
        def _():
            set_ghost_row(wide, rows + 1, recv[x, 5], recv[x, 6], recv[x, 7])

        def across(row):
            if forward:
                strips = [turned(pole[x][map_at(k)], code_at(k)) for k in (west, lon, east)]
                set_ghost_row(wide, row, *strips)
                return
            before, mid, after = [
                turned(pole[x][lax.rem(rim_source + shift, nlon)], rim_code)
                for shift in (nlon - 1, 0, 1)
            ]
            flip = rim_code == 1
            set_ghost_row(
                wide, row, jnp.where(flip, after, before), mid, jnp.where(flip, before, after)
            )

        @pl.when(at_top)
        def _():
            across(0)

        @pl.when(at_bottom)
        def _():
            across(rows + 1)

    def weight_forms():
        def spot(shape, shift):
            i = lax.broadcasted_iota(jnp.int32, shape, 0)
            j = lax.broadcasted_iota(jnp.int32, shape, 1)
            return jnp.where(i + shift == j, 1.0, 0.0).astype(BF16)

        for at, ref in ((0, one_ref), (1, two_ref)):
            total = jnp.zeros((tall, tall), F32)
            for r in range(3):
                total = total + jnp.dot(
                    ref[r * tall : (r + 1) * tall, :],
                    spot((chans, tall), r * chans),
                    preferred_element_type=F32,
                )
            w_ref[at] = total.astype(BF16)
            for s in range(3):
                blocks = [
                    ref[((2 - r) * 3 + 2 - s) * chans : ((2 - r) * 3 + 3 - s) * chans, :]
                    for r in range(3)
                ]
                w_ref[2 + at, s * chans : (s + 1) * chans, :] = lax.dot_general(
                    spot((chans, chans), 0),
                    jnp.concatenate(blocks, axis=0),
                    NT,
                    preferred_element_type=F32,
                ).astype(BF16)

    def rim_weights():
        for kernel_at in range(2):
            base = w_ref[2 + kernel_at]
            for place in range(3):
                wedge[kernel_at * 3 + place] = base

            def replace(place, into, out_of):
                full = base.astype(F32)
                shown = lax.broadcasted_iota(jnp.int32, full.shape, 1) // chans == into
                i = lax.broadcasted_iota(jnp.int32, full.shape, 0)
                j = lax.broadcasted_iota(jnp.int32, full.shape, 1)
                move = jnp.where(i - out_of * chans == j - into * chans, 1.0, 0.0).astype(BF16)
                moved = jnp.dot(base, move, preferred_element_type=F32)
                swapped = jnp.concatenate(
                    [moved[2 * chans :], moved[chans : 2 * chans], moved[:chans]], axis=0
                )
                chosen = jnp.where(rim_code == 1, swapped, moved)
                wedge[kernel_at * 3 + place] = jnp.where(shown, chosen, full).astype(BF16)

            @pl.when(at_top)
            def _():
                replace(0, 0, 2)

            @pl.when(at_bottom)
            def _():
                replace(2, 2, 0)

    def conv_row(weights, wide, h):
        window = wide[pl.ds(aligned(h, chans), tall), :]
        y = jnp.dot(weights, window, preferred_element_type=F32)
        left = jnp.where(lane == LANES - 1, y[:chans, LANES:], y[:chans, :LANES])
        right = jnp.where(lane == 0, y[2 * chans :, LANES:], y[2 * chans :, :LANES])
        return (
            pltpu.roll(left, 1, 1) + y[chans : 2 * chans, :LANES] + pltpu.roll(right, LANES - 1, 1)
        )

    def shifted(wide, h):
        g = wide[pl.ds(aligned(h + 1, chans), chans), own].astype(F32)
        ahead = pltpu.roll(g, LANES - 1, 1)
        behind = pltpu.roll(g, 1, 1)
        zero = jnp.zeros_like(g)
        first = jnp.concatenate(
            [jnp.where(lane != LANES - 1, ahead, zero), g, jnp.where(lane != 0, behind, zero)],
            axis=0,
        )
        second = jnp.concatenate(
            [jnp.where(lane == LANES - 1, ahead, zero), zero, jnp.where(lane == 0, behind, zero)],
            axis=0,
        )
        return [first.astype(BF16), second.astype(BF16)]

    def gradient(shift_wide, window_wide, acc, shifted_first):
        count = min(16, rows)

        def step(i, c):
            moved, windows = [], []
            for u in range(count):
                h = i * count + u
                moved += shifted(shift_wide, h)
                windows.append(window_wide[pl.ds(aligned(h, chans), tall), :])
            moved, windows = jnp.concatenate(moved, axis=1), jnp.concatenate(windows, axis=1)
            a, b = (moved, windows) if shifted_first else (windows, moved)
            acc[:, :tall] += lax.dot_general(a, b, NT, preferred_element_type=F32)
            return c

        acc[...] = jnp.zeros_like(acc)
        lax.fori_loop(0, rows // count, step, 0)

    def all_rows(row, x, wide, forward):
        set_ghost_cols(x, wide)
        carry = lax.fori_loop(1, rows - 1, row, none, unroll=rows - 2)
        set_ghost_rows(x, wide, forward)
        return lax.fori_loop(0, 2, lambda k, c: row(k * (rows - 1), c), carry, unroll=2)

    loads[0].wait()
    packed = take_in(fields_in, stage, fwide)
    pl.semaphore_wait(barrier, group - 1 + depth - 1 + beside)
    send_edges(FIELDS, fwide, packed)
    loads[1].wait()
    packed = take_in(cot_in, stage_two, gwide)
    send_edges(COT, gwide, packed)
    loads[2].wait()
    loads[3].wait()
    weight_forms()
    rim_weights()

    root = math.sqrt(2.0 / math.pi)

    def hidden_row(h, packed):
        u = conv_row(w_ref[0], fwide, h)
        square = u * u
        t = jnp.tanh(root * (u + 0.044715 * (square * u)))
        half = 0.5 * (1.0 + t)
        slope[pl.ds(aligned(h, chans), chans), :] = half + (0.5 * root) * u * (1.0 - t * t) * (
            1.0 + (3 * 0.044715) * square
        )
        value = u * half
        hwide[pl.ds(aligned(h + 1, chans), chans), own] = value.astype(BF16)
        return pack_edge(h, value, packed)

    packed = all_rows(hidden_row, FIELDS, fwide, True)
    send_edges(HIDDEN, hwide, packed)

    def weights_at(kernel_at, h):
        place = jnp.where(h == 0, 0, jnp.where(h == rows - 1, 2, 1))
        return wedge[kernel_at * 3 + place]

    def back_row(h, packed):
        back = conv_row(weights_at(1, h), gwide, h)
        value = back * slope[pl.ds(aligned(h, chans), chans), :]
        dwide[pl.ds(aligned(h + 1, chans), chans), own] = value.astype(BF16)
        return pack_edge(h, value, packed)

    packed = all_rows(back_row, COT, gwide, False)
    send_edges(DPRE, dwide, packed)

    gradient(dwide, fwide, acc_one, True)

    def set_aside(row):
        place = pl.ds(row * chans, chans)
        rim_row[...] = gwide[place, :]
        gwide[place, :] = jnp.zeros((chans, 2 * LANES), BF16)

    def credit(h, block):
        first, second = shifted(hwide, h)
        moved = jnp.concatenate([first, second], axis=1).astype(F32)
        swapped = jnp.concatenate(
            [moved[2 * chans :], moved[chans : 2 * chans], moved[:chans]], axis=0
        )
        chosen = jnp.where(rim_code == 1, swapped, moved).astype(BF16)
        acc_two[pl.ds(block * chans, chans), :tall] += lax.dot_general(
            rim_row[...], chosen, NT, preferred_element_type=F32
        )

    @pl.when(at_top)
    def _():
        set_aside(0)

    @pl.when(at_bottom)
    def _():
        set_aside(rows + 1)

    gradient(hwide, gwide, acc_two, False)

    @pl.when(at_top)
    def _():
        credit(0, 2)

    @pl.when(at_bottom)
    def _():
        credit(rows - 1, 0)

    sums[pl.ds(0, tall), :] = acc_one[:, :LANES]
    sums[pl.ds(tall, tall), :] = acc_two[:, :LANES]
    half_lane = lax.broadcasted_iota(jnp.int32, (tall, LANES), 1) < chans
    sums[pl.ds(2 * tall, tall), :] = jnp.where(
        half_lane, acc_one[:, LANES:], pltpu.roll(acc_two[:, LANES:], chans, 1)
    )
    for j in range(owners):
        rs_send[j] = sums[pl.ds(j * piece, piece), :].astype(BF16)

    def rs_copy(j):
        return put(
            rs_send.at[j], rs_recv.at[mine], rs_ssem.at[j], rs_rsem.at[mine], in_group(owner_at(j))
        )

    def rs_start(j, c):
        @pl.when(owner_at(j) != mine)
        def _():
            rs_copy(j).start()

        return c

    lax.fori_loop(0, owners, rs_start, 0)

    @pl.when(owns)
    def _():
        rs_recv[mine] = rs_send[own_piece]

    set_ghost_cols(HIDDEN, hwide)
    set_ghost_rows(HIDDEN, hwide, True)

    def out_row(h, c):
        stage[pl.ds(h, chans, stride=rows), :] = conv_row(w_ref[1], hwide, h)
        return c

    lax.fori_loop(0, rows, out_row, 0, unroll=rows)
    out_buf[...] = stage[...].astype(BF16)
    out_copy = pltpu.make_async_copy(out_buf, out_hbm, local_sem.at[4])
    out_copy.start()

    def ar_copy(k):
        return put(ar_send, ar_recv.at[z], ar_ssem.at[k], ar_rsem.at[z], along_z(k))

    @pl.when(owns)
    def _():
        def wait(k, c):
            source = group_peer(k)
            put(
                rs_recv.at[mine], rs_recv.at[source], rs_ssem.at[0], rs_rsem.at[source], here
            ).wait_recv()
            return c

        lax.fori_loop(1, group, wait, 0)
        total = rs_recv[0].astype(F32)
        for k in range(1, group):
            total = total + rs_recv[k].astype(F32)
        ar_send[...] = total.astype(BF16)
        ar_recv[z] = total.astype(BF16)

        def start(k, c):
            ar_copy(k).start()
            return c

        lax.fori_loop(1, depth, start, 0)

    set_ghost_cols(DPRE, dwide)
    set_ghost_rows(DPRE, dwide, False)

    def df_row(h, c):
        stage_two[pl.ds(h, chans, stride=rows), :] = conv_row(weights_at(0, h), dwide, h)
        return c

    lax.fori_loop(0, rows, df_row, 0, unroll=rows)
    df_buf[...] = stage_two[...].astype(BF16)
    df_copy = pltpu.make_async_copy(df_buf, df_hbm, local_sem.at[5])
    df_copy.start()

    def ag_copy(k):
        return put(
            ag_buf.at[own_piece], ag_buf.at[own_piece], ag_ssem.at[k], ag_rsem.at[own_piece],
            in_group(group_peer(k)),
        )

    @pl.when(owns)
    def _():
        def wait(k, c):
            source = lax.rem(z + k, depth)
            put(ar_send, ar_recv.at[source], ar_ssem.at[k], ar_rsem.at[source], here).wait_recv()
            return c

        lax.fori_loop(1, depth, wait, 0)
        total = ar_recv[0].astype(F32)
        for k in range(1, depth):
            total = total + ar_recv[k].astype(F32)
        ag_buf[own_piece] = total.astype(BF16)

        def start(k, c):
            ag_copy(k).start()
            return c

        lax.fori_loop(1, group, start, 0)

    for x in range(4):
        wait_sent(x)

    def rs_sent(j, c):
        @pl.when(owner_at(j) != mine)
        def _():
            rs_copy(j).wait_send()

        return c

    lax.fori_loop(0, owners, rs_sent, 0)

    @pl.when(owns)
    def _():
        def sent(k, c):
            ar_copy(k).wait_send()
            return c

        lax.fori_loop(1, depth, sent, 0)

    def ag_wait(j, c):
        @pl.when(owner_at(j) != mine)
        def _():
            put(ag_buf.at[j], ag_buf.at[j], ag_ssem.at[0], ag_rsem.at[j], here).wait_recv()

        return c

    lax.fori_loop(0, owners, ag_wait, 0)
    for j in range(owners):
        sums[pl.ds(j * piece, piece), :] = ag_buf[j].astype(F32) * scale
    one, two, rest = (sums[pl.ds(i * tall, tall), :] for i in range(3))
    one_parts = (one, pltpu.roll(one, chans, 1), rest)
    two_parts = (two, pltpu.roll(two, chans, 1), pltpu.roll(rest, chans, 1))
    for a in range(3):
        cut = slice(a * chans, (a + 1) * chans)
        for b in range(3):
            g1_ref[b, a] = one_parts[b][cut, :chans]
            g2_ref[2 - a, 2 - b] = two_parts[b][cut, :chans]

    @pl.when(owns)
    def _():
        def sent(k, c):
            ag_copy(k).wait_send()
            return c

        lax.fori_loop(1, group, sent, 0)

    out_copy.wait()
    df_copy.wait()


def on_device(
    nlon, nlat, fields_in, weight_one, weight_two, cotangent,
    north_map, north_code, south_map, south_code,
):
    chans, rows, cols = fields_in.shape
    scale = 1.0 / math.sqrt(float(rows * cols * nlon * nlat))
    tall = 3 * chans
    planes = 2 if nlat % 2 == 0 else 1
    group, depth = nlon * planes, nlat // planes
    owners = max(k for k in range(1, group + 1) if 3 * tall % (8 * k) == 0)
    piece = 3 * tall // owners
    vmem = pl.BlockSpec(memory_space=pltpu.VMEM)
    smem = pl.BlockSpec(memory_space=pltpu.SMEM)
    hbm = pl.BlockSpec(memory_space=pltpu.HBM)
    wide = pltpu.VMEM(((rows + 2) * chans, 2 * LANES), BF16)
    flat16 = pltpu.VMEM((chans * rows, LANES), BF16)
    flat32 = pltpu.VMEM((chans * rows, LANES), F32)
    polar = pltpu.VMEM((nlon, chans, LANES), BF16)
    dma = pltpu.SemaphoreType.DMA
    scratch = [
        flat16, flat16,
        pltpu.VMEM((9 * chans, chans), BF16), pltpu.VMEM((9 * chans, chans), BF16),
        flat16, flat16, flat32, flat32, wide, wide, wide, wide, flat32,
        pltpu.VMEM((4, tall, tall), BF16), pltpu.VMEM((6, tall, tall), BF16),
        pltpu.VMEM((chans, 2 * LANES), BF16),
        pltpu.VMEM((4, 3, chans, LANES), BF16), pltpu.VMEM((4, 8, chans, LANES), BF16),
        polar, polar, polar, polar,
        pltpu.VMEM((tall, 2 * LANES), F32), pltpu.VMEM((tall, 2 * LANES), F32),
        pltpu.VMEM((3 * tall, LANES), F32),
        pltpu.VMEM((owners, piece, LANES), BF16), pltpu.VMEM((group, piece, LANES), BF16),
        pltpu.VMEM((piece, LANES), BF16), pltpu.VMEM((depth, piece, LANES), BF16),
        pltpu.VMEM((owners, piece, LANES), BF16),
        dma((6,)), dma((4, 8)), dma((4, 8)), dma((4, nlon)), dma((4, nlon)),
        dma((owners,)), dma((group,)), dma((depth,)), dma((depth,)),
        dma((group,)), dma((owners,)),
    ]
    output, d_fields, grad_one, grad_two = pl.pallas_call(
        functools.partial(kernel, nlon, nlat, planes, rows, chans, owners, scale),
        out_shape=(
            jax.ShapeDtypeStruct((chans * rows, cols), BF16),
            jax.ShapeDtypeStruct((chans * rows, cols), BF16),
            jax.ShapeDtypeStruct((3, 3, chans, chans), F32),
            jax.ShapeDtypeStruct((3, 3, chans, chans), F32),
        ),
        in_specs=[hbm, hbm, hbm, hbm, smem, smem, smem, smem],
        out_specs=(hbm, hbm, vmem, vmem),
        scratch_shapes=scratch,
        compiler_params=pltpu.CompilerParams(
            collective_id=0, has_side_effects=True, vmem_limit_bytes=48 * 1024 * 1024
        ),
    )(
        fields_in.reshape(chans * rows, cols), cotangent.reshape(chans * rows, cols),
        weight_one.reshape(9 * chans, chans), weight_two.reshape(9 * chans, chans),
        north_map, north_code, south_map, south_code,
    )
    shape = (chans, rows, cols)
    return (output.reshape(shape), d_fields.reshape(shape), grad_one, grad_two)


def solution(mesh):
    placed = (P(None, "lat", "lon"), P(), P(), P(None, "lat", "lon"), P(), P(), P(), P())
    return jax.shard_map(
        functools.partial(on_device, mesh.shape["lon"], mesh.shape["lat"]),
        mesh=mesh,
        in_specs=placed,
        out_specs=(P(None, "lat", "lon"), P(None, "lat", "lon"), P(), P()),
        check_vma=False,
    )
```

```python
import functools
import math

import jax
import jax.numpy as jnp
from jax import lax
from jax.experimental import pallas as pl
from jax.experimental.pallas import tpu as pltpu
from jax.sharding import PartitionSpec as P

MESH = pl.DeviceIdType.MESH
LANES = 128
F32 = jnp.float32
BF16 = jnp.bfloat16
NT = (((1,), (1,)), ((), ()))
FIELDS, COT, HIDDEN, DPRE = range(4)
VMEM_BYTES = 48 * 1024 * 1024


def aligned(start, step):
    return pl.multiple_of(start * step, step)


def kernel(
    nlon, nlat, planes, rows, chans, owners, scale,
    fields_hbm, cot_hbm, one_hbm, two_hbm, north_map, north_code, south_map, south_code,
    out_ref, df_ref, g1_ref, g2_ref,
    fields_in, cot_in, one_ref, two_ref,
    stage, stage_two, fwide, gwide, hwide, dwide, slope, w_ref, wedge, rim_row,
    send, recv, pole_f, pole_c, pole_h, pole_d, acc_one, acc_two, sums,
    rs_send, rs_recv, ar_send, ar_recv, ag_buf,
    local_sem, near_send, near_recv, pole_send, pole_recv,
    rs_ssem, rs_rsem, ar_ssem, ar_rsem, ag_ssem, ag_rsem,
):
    lon = lax.axis_index("lon")
    lat = lax.axis_index("lat")
    depth = nlat // planes
    plane = lax.div(lat, depth)
    z = lax.rem(lat, depth)
    group = nlon * planes
    mine = lon + nlon * plane
    west = lax.rem(lon + nlon - 1, nlon)
    east = lax.rem(lon + 1, nlon)
    has_north = lat > 0
    has_south = lat < nlat - 1
    at_top = lat == 0
    at_bottom = lat == nlat - 1
    at_pole = jnp.logical_or(at_top, at_bottom)
    tall = 3 * chans
    lane = lax.broadcasted_iota(jnp.int32, (chans, LANES), 1)
    own = pl.ds(0, LANES)
    ghost_cols = pl.ds(LANES, LANES)
    piece = 3 * tall // owners

    def in_group(g):
        return lax.div(g, nlon) * depth + z, lax.rem(g, nlon)

    def group_peer(k):
        return lax.rem(mine + k, group)

    def along_z(k):
        return plane * depth + lax.rem(z + k, depth), lon

    spread_owners = group % 4 == 0 and owners == group // 4 * 3

    def owner_at(j):
        return lax.div(j, 3) * 4 + lax.rem(j, 3) if spread_owners else j

    if spread_owners:
        owns = lax.rem(mine, 4) < 3
        own_piece = lax.div(mine, 4) * 3 + lax.rem(mine, 4)
    else:
        owns = mine < owners
        own_piece = mine

    barrier = pltpu.get_barrier_semaphore()

    def greet(place):
        pl.semaphore_signal(
            barrier, inc=1, device_id={"lat": place[0], "lon": place[1]}, device_id_type=MESH
        )

    def greet_group(k, c):
        greet(in_group(group_peer(k)))
        return c

    def greet_z(k, c):
        greet(along_z(k))
        return c

    @pl.when(has_north)
    def _():
        for at in (west, lon, east):
            greet((lat - 1, at))

    @pl.when(has_south)
    def _():
        for at in (west, lon, east):
            greet((lat + 1, at))

    lax.fori_loop(1, group, greet_group, 0)
    lax.fori_loop(1, depth, greet_z, 0)
    beside = 3 * has_north.astype(jnp.int32) + 3 * has_south.astype(jnp.int32)

    loads = [
        pltpu.make_async_copy(source, target, local_sem.at[i])
        for i, (source, target) in enumerate(
            [(fields_hbm, fields_in), (cot_hbm, cot_in), (one_hbm, one_ref), (two_hbm, two_ref)]
        )
    ]
    for load in loads:
        load.start()

    def put(src, dst, ssem, rsem, place):
        return pltpu.make_async_remote_copy(
            src_ref=src, dst_ref=dst, send_sem=ssem, recv_sem=rsem,
            device_id={"lat": place[0], "lon": place[1]}, device_id_type=MESH,
        )

    here = (lat, lon)
    pole = (pole_f, pole_c, pole_h, pole_d)

    def near_copies(x):
        def one(part, slot, at, place):
            return put(
                send.at[x, part], recv.at[x, slot], near_send.at[x, at], near_recv.at[x, slot],
                place,
            )

        sides = [one(2, 1, 0, (lat, west)), one(2, 0, 1, (lat, east))]
        up = [
            one(0, 7, 2, (lat - 1, west)), one(0, 6, 3, (lat - 1, lon)), one(0, 5, 4, (lat - 1, east))
        ]
        down = [
            one(1, 4, 5, (lat + 1, west)), one(1, 3, 6, (lat + 1, lon)), one(1, 2, 7, (lat + 1, east))
        ]
        return sides, up, down

    def pole_copy(x, part, k):
        return put(
            send.at[x, part], pole[x].at[lon], pole_send.at[x, k], pole_recv.at[x, lon],
            (lat, lax.rem(lon + k, nlon)),
        )

    def start_exchange(x):
        sides, up, down = near_copies(x)
        for copy in sides:
            copy.start()

        @pl.when(has_north)
        def _():
            for copy in up:
                copy.start()

        @pl.when(has_south)
        def _():
            for copy in down:
                copy.start()

        def pole_start(part):
            def step(k, c):
                pole_copy(x, part, k).start()
                return c

            lax.fori_loop(1, nlon, step, 0)
            pole[x][lon] = send[x, part]

        @pl.when(at_top)
        def _():
            pole_start(0)

        @pl.when(at_bottom)
        def _():
            pole_start(1)

    def arrived(x, slot):
        put(
            send.at[x, 0], recv.at[x, slot], near_send.at[x, 0], near_recv.at[x, slot], here
        ).wait_recv()

    def wait_rows(x):
        @pl.when(has_north)
        def _():
            for slot in (2, 3, 4):
                arrived(x, slot)

        @pl.when(has_south)
        def _():
            for slot in (5, 6, 7):
                arrived(x, slot)

        @pl.when(at_pole)
        def _():
            def step(k, c):
                source = lax.rem(lon + k, nlon)
                put(
                    send.at[x, 0], pole[x].at[source], pole_send.at[x, k],
                    pole_recv.at[x, source], here,
                ).wait_recv()
                return c

            lax.fori_loop(1, nlon, step, 0)

    def wait_sent(x):
        sides, up, down = near_copies(x)
        for copy in sides:
            copy.wait_send()

        @pl.when(has_north)
        def _():
            for copy in up:
                copy.wait_send()

        @pl.when(has_south)
        def _():
            for copy in down:
                copy.wait_send()

        @pl.when(at_pole)
        def _():
            def step(k, c):
                pole_copy(x, 0, k).wait_send()
                return c

            lax.fori_loop(1, nlon, step, 0)

    def map_at(k):
        return jnp.where(at_top, north_map[k], south_map[k])

    def code_at(k):
        return jnp.where(at_top, north_code[k], south_code[k])

    def find_owner(k, c):
        hit = map_at(k) == lon
        return jnp.where(hit, k, c[0]), jnp.where(hit, code_at(k), c[1])

    rim_source, rim_code = lax.fori_loop(0, nlon, find_owner, (jnp.int32(0), jnp.int32(0)))

    def turned(row, code):
        i = lax.broadcasted_iota(jnp.int32, (LANES, LANES), 0)
        j = lax.broadcasted_iota(jnp.int32, (LANES, LANES), 1)
        match = (i + (2 * code - 1) * j) == (LANES - 1) * code
        turn = jnp.where(match, 1.0, 0.0).astype(BF16)
        return jnp.dot(row, turn, preferred_element_type=F32)

    def set_ghost_row(wide, row, left, mid, right):
        place = pl.ds(row * chans, chans)
        wide[place, own] = mid.astype(BF16)
        wide[place, ghost_cols] = jnp.where(lane == 0, right.astype(F32), left.astype(F32)).astype(
            BF16
        )

    def set_ghost_cols(x, wide):
        arrived(x, 0)
        arrived(x, 1)
        merged = jnp.where(lane % 2 == 0, recv[x, 1].astype(F32), recv[x, 0].astype(F32))

        def step(h, c):
            place = pl.ds(aligned(h + 1, chans), chans)
            wide[place, ghost_cols] = pltpu.roll(merged, lax.rem(LANES - 2 * h, LANES), 1).astype(
                BF16
            )
            return c

        lax.fori_loop(0, rows, step, 0, unroll=rows)

    def pack_edge(h, value, packed):
        keep = jnp.logical_or(lane == 2 * h, lane == lax.rem(2 * h + LANES - 1, LANES))
        return jnp.where(keep, pltpu.roll(value, 2 * h, 1), packed)

    def send_edges(x, wide, packed):
        send[x, 0] = wide[pl.ds(chans, chans), own]
        send[x, 1] = wide[pl.ds(rows * chans, chans), own]
        send[x, 2] = packed.astype(BF16)
        start_exchange(x)

    none = jnp.zeros((chans, LANES), F32)

    def take_in(source, stage, wide):
        stage[...] = source[...].astype(F32)

        def step(h, packed):
            value = stage[pl.ds(h, chans, stride=rows), :]
            wide[pl.ds(aligned(h + 1, chans), chans), own] = value.astype(BF16)
            return pack_edge(h, value, packed)

        return lax.fori_loop(0, rows, step, none, unroll=rows)

    def set_ghost_rows(x, wide, forward):
        wait_rows(x)

        @pl.when(has_north)
        def _():
            set_ghost_row(wide, 0, recv[x, 2], recv[x, 3], recv[x, 4])

        @pl.when(has_south)
        def _():
            set_ghost_row(wide, rows + 1, recv[x, 5], recv[x, 6], recv[x, 7])

        def across(row):
            if forward:
                strips = [turned(pole[x][map_at(k)], code_at(k)) for k in (west, lon, east)]
                set_ghost_row(wide, row, *strips)
                return
            before, mid, after = [
                turned(pole[x][lax.rem(rim_source + shift, nlon)], rim_code)
                for shift in (nlon - 1, 0, 1)
            ]
            flip = rim_code == 1
            set_ghost_row(
                wide, row, jnp.where(flip, after, before), mid, jnp.where(flip, before, after)
            )

        @pl.when(at_top)
        def _():
            across(0)

        @pl.when(at_bottom)
        def _():
            across(rows + 1)

    def weight_forms():
        def spot(shape, shift):
            i = lax.broadcasted_iota(jnp.int32, shape, 0)
            j = lax.broadcasted_iota(jnp.int32, shape, 1)
            return jnp.where(i + shift == j, 1.0, 0.0).astype(BF16)

        for at, ref in ((0, one_ref), (1, two_ref)):
            total = jnp.zeros((tall, tall), F32)
            for r in range(3):
                total = total + jnp.dot(
                    ref[r * tall : (r + 1) * tall, :],
                    spot((chans, tall), r * chans),
                    preferred_element_type=F32,
                )
            w_ref[at] = total.astype(BF16)
            for s in range(3):
                blocks = [
                    ref[((2 - r) * 3 + 2 - s) * chans : ((2 - r) * 3 + 3 - s) * chans, :]
                    for r in range(3)
                ]
                w_ref[2 + at, s * chans : (s + 1) * chans, :] = lax.dot_general(
                    spot((chans, chans), 0),
                    jnp.concatenate(blocks, axis=0),
                    NT,
                    preferred_element_type=F32,
                ).astype(BF16)

    def rim_weights():
        for kernel_at in range(2):
            base = w_ref[2 + kernel_at]
            for place in range(3):
                wedge[kernel_at * 3 + place] = base

            def replace(place, into, out_of):
                full = base.astype(F32)
                shown = lax.broadcasted_iota(jnp.int32, full.shape, 1) // chans == into
                i = lax.broadcasted_iota(jnp.int32, full.shape, 0)
                j = lax.broadcasted_iota(jnp.int32, full.shape, 1)
                move = jnp.where(i - out_of * chans == j - into * chans, 1.0, 0.0).astype(BF16)
                moved = jnp.dot(base, move, preferred_element_type=F32)
                swapped = jnp.concatenate(
                    [moved[2 * chans :], moved[chans : 2 * chans], moved[:chans]], axis=0
                )
                chosen = jnp.where(rim_code == 1, swapped, moved)
                wedge[kernel_at * 3 + place] = jnp.where(shown, chosen, full).astype(BF16)

            @pl.when(at_top)
            def _():
                replace(0, 0, 2)

            @pl.when(at_bottom)
            def _():
                replace(2, 2, 0)

    def conv_row(weights, wide, h):
        window = wide[pl.ds(aligned(h, chans), tall), :]
        y = jnp.dot(weights, window, preferred_element_type=F32)
        left = jnp.where(lane == LANES - 1, y[:chans, LANES:], y[:chans, :LANES])
        right = jnp.where(lane == 0, y[2 * chans :, LANES:], y[2 * chans :, :LANES])
        return (
            pltpu.roll(left, 1, 1) + y[chans : 2 * chans, :LANES] + pltpu.roll(right, LANES - 1, 1)
        )

    def shifted(wide, h):
        g = wide[pl.ds(aligned(h + 1, chans), chans), own].astype(F32)
        ahead = pltpu.roll(g, LANES - 1, 1)
        behind = pltpu.roll(g, 1, 1)
        zero = jnp.zeros_like(g)
        first = jnp.concatenate(
            [jnp.where(lane != LANES - 1, ahead, zero), g, jnp.where(lane != 0, behind, zero)],
            axis=0,
        )
        second = jnp.concatenate(
            [jnp.where(lane == LANES - 1, ahead, zero), zero, jnp.where(lane == 0, behind, zero)],
            axis=0,
        )
        return [first.astype(BF16), second.astype(BF16)]

    def gradient(shift_wide, window_wide, acc, shifted_first):
        count = min(16, rows)

        def step(i, c):
            moved, windows = [], []
            for u in range(count):
                h = i * count + u
                moved += shifted(shift_wide, h)
                windows.append(window_wide[pl.ds(aligned(h, chans), tall), :])
            moved, windows = jnp.concatenate(moved, axis=1), jnp.concatenate(windows, axis=1)
            a, b = (moved, windows) if shifted_first else (windows, moved)
            acc[:, :tall] += lax.dot_general(a, b, NT, preferred_element_type=F32)
            return c

        acc[...] = jnp.zeros_like(acc)
        lax.fori_loop(0, rows // count, step, 0)

    def all_rows(row, x, wide, forward):
        set_ghost_cols(x, wide)
        carry = lax.fori_loop(1, rows - 1, row, none, unroll=rows - 2)
        set_ghost_rows(x, wide, forward)
        return lax.fori_loop(0, 2, lambda k, c: row(k * (rows - 1), c), carry, unroll=2)

    loads[0].wait()
    packed = take_in(fields_in, stage, fwide)
    pl.semaphore_wait(barrier, group - 1 + depth - 1 + beside)
    send_edges(FIELDS, fwide, packed)
    loads[1].wait()
    packed = take_in(cot_in, stage_two, gwide)
    send_edges(COT, gwide, packed)
    loads[2].wait()
    loads[3].wait()
    weight_forms()
    rim_weights()

    root = math.sqrt(2.0 / math.pi)

    def hidden_row(h, packed):
        u = conv_row(w_ref[0], fwide, h)
        square = u * u
        t = jnp.tanh(root * (u + 0.044715 * (square * u)))
        half = 0.5 * (1.0 + t)
        slope[pl.ds(aligned(h, chans), chans), :] = half + (0.5 * root) * u * (1.0 - t * t) * (
            1.0 + (3 * 0.044715) * square
        )
        value = u * half
        hwide[pl.ds(aligned(h + 1, chans), chans), own] = value.astype(BF16)
        return pack_edge(h, value, packed)

    packed = all_rows(hidden_row, FIELDS, fwide, True)
    send_edges(HIDDEN, hwide, packed)

    def weights_at(kernel_at, h):
        place = jnp.where(h == 0, 0, jnp.where(h == rows - 1, 2, 1))
        return wedge[kernel_at * 3 + place]

    def back_row(h, packed):
        back = conv_row(weights_at(1, h), gwide, h)
        value = back * slope[pl.ds(aligned(h, chans), chans), :]
        dwide[pl.ds(aligned(h + 1, chans), chans), own] = value.astype(BF16)
        return pack_edge(h, value, packed)

    packed = all_rows(back_row, COT, gwide, False)
    send_edges(DPRE, dwide, packed)

    gradient(dwide, fwide, acc_one, True)

    def set_aside(row):
        place = pl.ds(row * chans, chans)
        rim_row[...] = gwide[place, :]
        gwide[place, :] = jnp.zeros((chans, 2 * LANES), BF16)

    def credit(h, block):
        first, second = shifted(hwide, h)
        moved = jnp.concatenate([first, second], axis=1).astype(F32)
        swapped = jnp.concatenate(
            [moved[2 * chans :], moved[chans : 2 * chans], moved[:chans]], axis=0
        )
        chosen = jnp.where(rim_code == 1, swapped, moved).astype(BF16)
        acc_two[pl.ds(block * chans, chans), :tall] += lax.dot_general(
            rim_row[...], chosen, NT, preferred_element_type=F32
        )

    @pl.when(at_top)
    def _():
        set_aside(0)

    @pl.when(at_bottom)
    def _():
        set_aside(rows + 1)

    gradient(hwide, gwide, acc_two, False)

    @pl.when(at_top)
    def _():
        credit(0, 2)

    @pl.when(at_bottom)
    def _():
        credit(rows - 1, 0)

    sums[pl.ds(0, tall), :] = acc_one[:, :LANES]
    sums[pl.ds(tall, tall), :] = acc_two[:, :LANES]
    half_lane = lax.broadcasted_iota(jnp.int32, (tall, LANES), 1) < chans
    sums[pl.ds(2 * tall, tall), :] = jnp.where(
        half_lane, acc_one[:, LANES:], pltpu.roll(acc_two[:, LANES:], chans, 1)
    )
    for j in range(owners):
        rs_send[j] = sums[pl.ds(j * piece, piece), :].astype(BF16)

    def rs_copy(j):
        return put(
            rs_send.at[j], rs_recv.at[mine], rs_ssem.at[j], rs_rsem.at[mine], in_group(owner_at(j))
        )

    def rs_start(j, c):
        @pl.when(owner_at(j) != mine)
        def _():
            rs_copy(j).start()

        return c

    lax.fori_loop(0, owners, rs_start, 0)

    @pl.when(owns)
    def _():
        rs_recv[mine] = rs_send[own_piece]

    set_ghost_cols(HIDDEN, hwide)
    set_ghost_rows(HIDDEN, hwide, True)

    def out_row(h, c):
        stage[pl.ds(h, chans, stride=rows), :] = conv_row(w_ref[1], hwide, h)
        return c

    lax.fori_loop(0, rows, out_row, 0, unroll=rows)
    out_ref[...] = stage[...].astype(BF16)

    def ar_copy(k):
        return put(ar_send, ar_recv.at[z], ar_ssem.at[k], ar_rsem.at[z], along_z(k))

    @pl.when(owns)
    def _():
        def wait(k, c):
            source = group_peer(k)
            put(
                rs_recv.at[mine], rs_recv.at[source], rs_ssem.at[0], rs_rsem.at[source], here
            ).wait_recv()
            return c

        lax.fori_loop(1, group, wait, 0)
        total = rs_recv[0].astype(F32)
        for k in range(1, group):
            total = total + rs_recv[k].astype(F32)
        ar_send[...] = total.astype(BF16)
        ar_recv[z] = total.astype(BF16)

        def start(k, c):
            ar_copy(k).start()
            return c

        lax.fori_loop(1, depth, start, 0)

    set_ghost_cols(DPRE, dwide)
    set_ghost_rows(DPRE, dwide, False)

    def df_row(h, c):
        stage_two[pl.ds(h, chans, stride=rows), :] = conv_row(weights_at(0, h), dwide, h)
        return c

    lax.fori_loop(0, rows, df_row, 0, unroll=rows)
    df_ref[...] = stage_two[...].astype(BF16)

    def ag_copy(k):
        return put(
            ag_buf.at[own_piece], ag_buf.at[own_piece], ag_ssem.at[k], ag_rsem.at[own_piece],
            in_group(group_peer(k)),
        )

    @pl.when(owns)
    def _():
        def wait(k, c):
            source = lax.rem(z + k, depth)
            put(ar_send, ar_recv.at[source], ar_ssem.at[k], ar_rsem.at[source], here).wait_recv()
            return c

        lax.fori_loop(1, depth, wait, 0)
        total = ar_recv[0].astype(F32)
        for k in range(1, depth):
            total = total + ar_recv[k].astype(F32)
        ag_buf[own_piece] = total.astype(BF16)

        def start(k, c):
            ag_copy(k).start()
            return c

        lax.fori_loop(1, group, start, 0)

    for x in range(4):
        wait_sent(x)

    def rs_sent(j, c):
        @pl.when(owner_at(j) != mine)
        def _():
            rs_copy(j).wait_send()

        return c

    lax.fori_loop(0, owners, rs_sent, 0)

    @pl.when(owns)
    def _():
        def sent(k, c):
            ar_copy(k).wait_send()
            return c

        lax.fori_loop(1, depth, sent, 0)

    def ag_wait(j, c):
        @pl.when(owner_at(j) != mine)
        def _():
            put(ag_buf.at[j], ag_buf.at[j], ag_ssem.at[0], ag_rsem.at[j], here).wait_recv()

        return c

    lax.fori_loop(0, owners, ag_wait, 0)
    for j in range(owners):
        sums[pl.ds(j * piece, piece), :] = ag_buf[j].astype(F32) * scale
    one, two, rest = (sums[pl.ds(i * tall, tall), :] for i in range(3))
    one_parts = (one, pltpu.roll(one, chans, 1), rest)
    two_parts = (two, pltpu.roll(two, chans, 1), pltpu.roll(rest, chans, 1))
    for a in range(3):
        cut = slice(a * chans, (a + 1) * chans)
        for b in range(3):
            g1_ref[b, a] = one_parts[b][cut, :chans]
            g2_ref[2 - a, 2 - b] = two_parts[b][cut, :chans]

    @pl.when(owns)
    def _():
        def sent(k, c):
            ag_copy(k).wait_send()
            return c

        lax.fori_loop(1, group, sent, 0)


def hand_over(*refs):
    count = (len(refs) - 1) // 2
    sems = refs[-1]
    copies = [
        pltpu.make_async_copy(refs[i], refs[count + i], sems.at[i]) for i in range(count)
    ]
    for copy in copies:
        copy.start()
    for copy in copies:
        copy.wait()


def on_device(
    nlon, nlat, fields_in, weight_one, weight_two, cotangent,
    north_map, north_code, south_map, south_code,
):
    chans, rows, cols = fields_in.shape
    scale = 1.0 / math.sqrt(float(rows * cols * nlon * nlat))
    tall = 3 * chans
    planes = 2 if nlat % 2 == 0 else 1
    group, depth = nlon * planes, nlat // planes
    owners = max(k for k in range(1, group + 1) if 3 * tall % (8 * k) == 0)
    piece = 3 * tall // owners
    vmem = pl.BlockSpec(memory_space=pltpu.VMEM)
    smem = pl.BlockSpec(memory_space=pltpu.SMEM)
    hbm = pl.BlockSpec(memory_space=pltpu.HBM)
    wide = pltpu.VMEM(((rows + 2) * chans, 2 * LANES), BF16)
    flat16 = pltpu.VMEM((chans * rows, LANES), BF16)
    flat32 = pltpu.VMEM((chans * rows, LANES), F32)
    polar = pltpu.VMEM((nlon, chans, LANES), BF16)
    dma = pltpu.SemaphoreType.DMA

    def in_hbm(x):
        return pltpu.with_memory_space_constraint(x, pltpu.HBM)

    scratch = [
        flat16, flat16,
        pltpu.VMEM((9 * chans, chans), BF16), pltpu.VMEM((9 * chans, chans), BF16),
        flat32, flat32, wide, wide, wide, wide, flat32,
        pltpu.VMEM((4, tall, tall), BF16), pltpu.VMEM((6, tall, tall), BF16),
        pltpu.VMEM((chans, 2 * LANES), BF16),
        pltpu.VMEM((4, 3, chans, LANES), BF16), pltpu.VMEM((4, 8, chans, LANES), BF16),
        polar, polar, polar, polar,
        pltpu.VMEM((tall, 2 * LANES), F32), pltpu.VMEM((tall, 2 * LANES), F32),
        pltpu.VMEM((3 * tall, LANES), F32),
        pltpu.VMEM((owners, piece, LANES), BF16), pltpu.VMEM((group, piece, LANES), BF16),
        pltpu.VMEM((piece, LANES), BF16), pltpu.VMEM((depth, piece, LANES), BF16),
        pltpu.VMEM((owners, piece, LANES), BF16),
        dma((4,)), dma((4, 8)), dma((4, 8)), dma((4, nlon)), dma((4, nlon)),
        dma((owners,)), dma((group,)), dma((depth,)), dma((depth,)),
        dma((group,)), dma((owners,)),
    ]
    results = pl.pallas_call(
        functools.partial(kernel, nlon, nlat, planes, rows, chans, owners, scale),
        out_shape=(
            pltpu.VMEM((chans * rows, cols), BF16),
            pltpu.VMEM((chans * rows, cols), BF16),
            pltpu.VMEM((3, 3, chans, chans), F32),
            pltpu.VMEM((3, 3, chans, chans), F32),
        ),
        in_specs=[hbm, hbm, hbm, hbm, smem, smem, smem, smem],
        out_specs=(vmem, vmem, vmem, vmem),
        scratch_shapes=scratch,
        compiler_params=pltpu.CompilerParams(
            collective_id=0, has_side_effects=True, vmem_limit_bytes=VMEM_BYTES
        ),
    )(
        in_hbm(fields_in.reshape(chans * rows, cols)), in_hbm(cotangent.reshape(chans * rows, cols)),
        in_hbm(weight_one.reshape(9 * chans, chans)), in_hbm(weight_two.reshape(9 * chans, chans)),
        north_map, north_code, south_map, south_code,
    )
    output, d_fields, grad_one, grad_two = pl.pallas_call(
        hand_over,
        out_shape=tuple(jax.ShapeDtypeStruct(x.shape, x.dtype) for x in results),
        in_specs=[vmem] * 4,
        out_specs=(hbm,) * 4,
        scratch_shapes=[dma((4,))],
    )(*[pltpu.with_memory_space_constraint(x, pltpu.VMEM) for x in results])
    shape = (chans, rows, cols)
    return (output.reshape(shape), d_fields.reshape(shape), grad_one, grad_two)


def solution(mesh):
    placed = (P(None, "lat", "lon"), P(), P(), P(None, "lat", "lon"), P(), P(), P(), P())
    return jax.shard_map(
        functools.partial(on_device, mesh.shape["lon"], mesh.shape["lat"]),
        mesh=mesh,
        in_specs=placed,
        out_specs=(P(None, "lat", "lon"), P(None, "lat", "lon"), P(), P()),
        check_vma=False,
    )
```

```python
import functools
import math

import jax
import jax.numpy as jnp
from jax import lax
from jax.experimental import pallas as pl
from jax.experimental.pallas import tpu as pltpu
from jax.sharding import PartitionSpec as P

MESH = pl.DeviceIdType.MESH
LANES = 128
F32 = jnp.float32
BF16 = jnp.bfloat16
NT = (((1,), (1,)), ((), ()))
FIELDS, COT, HIDDEN, DPRE = range(4)
VMEM_BYTES = 48 * 1024 * 1024


def aligned(start, step):
    return pl.multiple_of(start * step, step)


def kernel(
    nlon, nlat, planes, rows, chans, owners, scale,
    fields_hbm, cot_hbm, one_hbm, two_hbm, north_map, north_code, south_map, south_code,
    out_ref, df_ref, g1_ref, g2_ref,
    fields_in, cot_in, one_ref, two_ref,
    stage, stage_two, fwide, gwide, hwide, dwide, slope, w_ref, wedge, rim_row,
    send, recv, pole_f, pole_c, pole_h, pole_d, acc_one, acc_two, sums,
    rs_send, rs_recv, ar_send, ar_recv, ag_buf,
    local_sem, near_send, near_recv, pole_send, pole_recv, hand_send, hand_recv,
    rs_ssem, rs_rsem, ar_ssem, ar_rsem, ag_ssem, ag_rsem,
):
    lon = lax.axis_index("lon")
    lat = lax.axis_index("lat")
    depth = nlat // planes
    plane = lax.div(lat, depth)
    z = lax.rem(lat, depth)
    group = nlon * planes
    mine = lon + nlon * plane
    west = lax.rem(lon + nlon - 1, nlon)
    east = lax.rem(lon + 1, nlon)
    has_north = lat > 0
    has_south = lat < nlat - 1
    at_top = lat == 0
    at_bottom = lat == nlat - 1
    at_pole = jnp.logical_or(at_top, at_bottom)
    tall = 3 * chans
    lane = lax.broadcasted_iota(jnp.int32, (chans, LANES), 1)
    own = pl.ds(0, LANES)
    ghost_cols = pl.ds(LANES, LANES)
    piece = 3 * tall // owners

    def in_group(g):
        return lax.div(g, nlon) * depth + z, lax.rem(g, nlon)

    def group_peer(k):
        return lax.rem(mine + k, group)

    def along_z(k):
        return plane * depth + lax.rem(z + k, depth), lon

    spread_owners = group % 4 == 0 and owners == group // 4 * 3

    def owner_at(j):
        return lax.div(j, 3) * 4 + lax.rem(j, 3) if spread_owners else j

    if spread_owners:
        owns = lax.rem(mine, 4) < 3
        own_piece = lax.div(mine, 4) * 3 + lax.rem(mine, 4)
    else:
        owns = mine < owners
        own_piece = mine

    barrier = pltpu.get_barrier_semaphore()

    def greet(place):
        pl.semaphore_signal(
            barrier, inc=1, device_id={"lat": place[0], "lon": place[1]}, device_id_type=MESH
        )

    def greet_group(k, c):
        greet(in_group(group_peer(k)))
        return c

    def greet_z(k, c):
        greet(along_z(k))
        return c

    @pl.when(has_north)
    def _():
        for at in (west, lon, east):
            greet((lat - 1, at))

    @pl.when(has_south)
    def _():
        for at in (west, lon, east):
            greet((lat + 1, at))

    lax.fori_loop(1, group, greet_group, 0)
    lax.fori_loop(1, depth, greet_z, 0)
    beside = 3 * has_north.astype(jnp.int32) + 3 * has_south.astype(jnp.int32)

    loads = [
        pltpu.make_async_copy(source, target, local_sem.at[i])
        for i, (source, target) in enumerate(
            [(fields_hbm, fields_in), (cot_hbm, cot_in), (one_hbm, one_ref), (two_hbm, two_ref)]
        )
    ]
    for load in loads:
        load.start()

    def put(src, dst, ssem, rsem, place):
        return pltpu.make_async_remote_copy(
            src_ref=src, dst_ref=dst, send_sem=ssem, recv_sem=rsem,
            device_id={"lat": place[0], "lon": place[1]}, device_id_type=MESH,
        )

    here = (lat, lon)
    pole = (pole_f, pole_c, pole_h, pole_d)

    def near_copies(x):
        def one(part, slot, at, place):
            return put(
                send.at[x, part], recv.at[x, slot], near_send.at[x, at], near_recv.at[x, slot],
                place,
            )

        sides = [one(2, 1, 0, (lat, west)), one(2, 0, 1, (lat, east))]
        up = [
            one(0, 7, 2, (lat - 1, west)), one(0, 6, 3, (lat - 1, lon)), one(0, 5, 4, (lat - 1, east))
        ]
        down = [
            one(1, 4, 5, (lat + 1, west)), one(1, 3, 6, (lat + 1, lon)), one(1, 2, 7, (lat + 1, east))
        ]
        return sides, up, down

    half = nlon // 2
    core = lax.rem(lon, 2)
    chip = lax.div(lon, 2)
    sibling = (lat, lon + 1 - 2 * core)

    def strip_at(k):
        return lax.rem(k, 2) * half + lax.div(k, 2)

    def pole_copy(x, part, k):
        return put(
            send.at[x, part], pole[x].at[core * half + chip], pole_send.at[x, k],
            pole_recv.at[x, chip], (lat, lax.rem(lon + 2 * k, nlon)),
        )

    def hand_on(x, at):
        block = pole[x].at[pl.ds(at * half, half)]
        return put(block, block, hand_send.at[x], hand_recv.at[x], sibling)

    def forward_poles(x):
        @pl.when(at_pole)
        def _():
            def step(k, c):
                source = lax.rem(chip + k, half)
                put(
                    send.at[x, 0], pole[x].at[core * half + source], pole_send.at[x, k],
                    pole_recv.at[x, source], here,
                ).wait_recv()
                return c

            lax.fori_loop(1, half, step, 0)
            hand_on(x, core).start()

    def start_exchange(x):
        sides, up, down = near_copies(x)
        for copy in sides:
            copy.start()

        @pl.when(has_north)
        def _():
            for copy in up:
                copy.start()

        @pl.when(has_south)
        def _():
            for copy in down:
                copy.start()

        def pole_start(part):
            def step(k, c):
                pole_copy(x, part, k).start()
                return c

            lax.fori_loop(1, half, step, 0)
            pole[x][core * half + chip] = send[x, part]

        @pl.when(at_top)
        def _():
            pole_start(0)

        @pl.when(at_bottom)
        def _():
            pole_start(1)

    def arrived(x, slot):
        put(
            send.at[x, 0], recv.at[x, slot], near_send.at[x, 0], near_recv.at[x, slot], here
        ).wait_recv()

    def wait_rows(x):
        @pl.when(has_north)
        def _():
            for slot in (2, 3, 4):
                arrived(x, slot)

        @pl.when(has_south)
        def _():
            for slot in (5, 6, 7):
                arrived(x, slot)

        @pl.when(at_pole)
        def _():
            hand_on(x, 1 - core).wait_recv()

    def wait_sent(x):
        sides, up, down = near_copies(x)
        for copy in sides:
            copy.wait_send()

        @pl.when(has_north)
        def _():
            for copy in up:
                copy.wait_send()

        @pl.when(has_south)
        def _():
            for copy in down:
                copy.wait_send()

        @pl.when(at_pole)
        def _():
            def step(k, c):
                pole_copy(x, 0, k).wait_send()
                return c

            lax.fori_loop(1, half, step, 0)
            hand_on(x, core).wait_send()

    def map_at(k):
        return jnp.where(at_top, north_map[k], south_map[k])

    def code_at(k):
        return jnp.where(at_top, north_code[k], south_code[k])

    def find_owner(k, c):
        hit = map_at(k) == lon
        return jnp.where(hit, k, c[0]), jnp.where(hit, code_at(k), c[1])

    rim_source, rim_code = lax.fori_loop(0, nlon, find_owner, (jnp.int32(0), jnp.int32(0)))

    def turned(row, code):
        i = lax.broadcasted_iota(jnp.int32, (LANES, LANES), 0)
        j = lax.broadcasted_iota(jnp.int32, (LANES, LANES), 1)
        match = (i + (2 * code - 1) * j) == (LANES - 1) * code
        turn = jnp.where(match, 1.0, 0.0).astype(BF16)
        return jnp.dot(row, turn, preferred_element_type=F32)

    def set_ghost_row(wide, row, left, mid, right):
        place = pl.ds(row * chans, chans)
        wide[place, own] = mid.astype(BF16)
        wide[place, ghost_cols] = jnp.where(lane == 0, right.astype(F32), left.astype(F32)).astype(
            BF16
        )

    def set_ghost_cols(x, wide):
        arrived(x, 0)
        arrived(x, 1)
        merged = jnp.where(lane % 2 == 0, recv[x, 1].astype(F32), recv[x, 0].astype(F32))

        def step(h, c):
            place = pl.ds(aligned(h + 1, chans), chans)
            wide[place, ghost_cols] = pltpu.roll(merged, lax.rem(LANES - 2 * h, LANES), 1).astype(
                BF16
            )
            return c

        lax.fori_loop(0, rows, step, 0, unroll=rows)

    def pack_edge(h, value, packed):
        keep = jnp.logical_or(lane == 2 * h, lane == lax.rem(2 * h + LANES - 1, LANES))
        return jnp.where(keep, pltpu.roll(value, 2 * h, 1), packed)

    def set_edges(x, wide, packed):
        send[x, 0] = wide[pl.ds(chans, chans), own]
        send[x, 1] = wide[pl.ds(rows * chans, chans), own]
        send[x, 2] = packed.astype(BF16)

    none = jnp.zeros((chans, LANES), F32)

    def take_in(source, stage, wide):
        stage[...] = source[...].astype(F32)

        def step(h, packed):
            value = stage[pl.ds(h, chans, stride=rows), :]
            wide[pl.ds(aligned(h + 1, chans), chans), own] = value.astype(BF16)
            return pack_edge(h, value, packed)

        return lax.fori_loop(0, rows, step, none, unroll=rows)

    def set_ghost_rows(x, wide, forward):
        wait_rows(x)

        @pl.when(has_north)
        def _():
            set_ghost_row(wide, 0, recv[x, 2], recv[x, 3], recv[x, 4])

        @pl.when(has_south)
        def _():
            set_ghost_row(wide, rows + 1, recv[x, 5], recv[x, 6], recv[x, 7])

        def across(row):
            if forward:
                strips = [turned(pole[x][strip_at(map_at(k))], code_at(k)) for k in (west, lon, east)]
                set_ghost_row(wide, row, *strips)
                return
            before, mid, after = [
                turned(pole[x][strip_at(lax.rem(rim_source + shift, nlon))], rim_code)
                for shift in (nlon - 1, 0, 1)
            ]
            flip = rim_code == 1
            set_ghost_row(
                wide, row, jnp.where(flip, after, before), mid, jnp.where(flip, before, after)
            )

        @pl.when(at_top)
        def _():
            across(0)

        @pl.when(at_bottom)
        def _():
            across(rows + 1)

    def weight_forms():
        def spot(shape, shift):
            i = lax.broadcasted_iota(jnp.int32, shape, 0)
            j = lax.broadcasted_iota(jnp.int32, shape, 1)
            return jnp.where(i + shift == j, 1.0, 0.0).astype(BF16)

        for at, ref in ((0, one_ref), (1, two_ref)):
            total = jnp.zeros((tall, tall), F32)
            for r in range(3):
                total = total + jnp.dot(
                    ref[r * tall : (r + 1) * tall, :],
                    spot((chans, tall), r * chans),
                    preferred_element_type=F32,
                )
            w_ref[at] = total.astype(BF16)
            for s in range(3):
                blocks = [
                    ref[((2 - r) * 3 + 2 - s) * chans : ((2 - r) * 3 + 3 - s) * chans, :]
                    for r in range(3)
                ]
                w_ref[2 + at, s * chans : (s + 1) * chans, :] = lax.dot_general(
                    spot((chans, chans), 0),
                    jnp.concatenate(blocks, axis=0),
                    NT,
                    preferred_element_type=F32,
                ).astype(BF16)

    def rim_weights():
        for kernel_at in range(2):
            base = w_ref[2 + kernel_at]
            for place in range(3):
                wedge[kernel_at * 3 + place] = base

            def replace(place, into, out_of):
                full = base.astype(F32)
                shown = lax.broadcasted_iota(jnp.int32, full.shape, 1) // chans == into
                i = lax.broadcasted_iota(jnp.int32, full.shape, 0)
                j = lax.broadcasted_iota(jnp.int32, full.shape, 1)
                move = jnp.where(i - out_of * chans == j - into * chans, 1.0, 0.0).astype(BF16)
                moved = jnp.dot(base, move, preferred_element_type=F32)
                swapped = jnp.concatenate(
                    [moved[2 * chans :], moved[chans : 2 * chans], moved[:chans]], axis=0
                )
                chosen = jnp.where(rim_code == 1, swapped, moved)
                wedge[kernel_at * 3 + place] = jnp.where(shown, chosen, full).astype(BF16)

            @pl.when(at_top)
            def _():
                replace(0, 0, 2)

            @pl.when(at_bottom)
            def _():
                replace(2, 2, 0)

    def conv_row(weights, wide, h):
        window = wide[pl.ds(aligned(h, chans), tall), :]
        y = jnp.dot(weights, window, preferred_element_type=F32)
        left = jnp.where(lane == LANES - 1, y[:chans, LANES:], y[:chans, :LANES])
        right = jnp.where(lane == 0, y[2 * chans :, LANES:], y[2 * chans :, :LANES])
        return (
            pltpu.roll(left, 1, 1) + y[chans : 2 * chans, :LANES] + pltpu.roll(right, LANES - 1, 1)
        )

    def shifted(wide, h):
        g = wide[pl.ds(aligned(h + 1, chans), chans), own].astype(F32)
        ahead = pltpu.roll(g, LANES - 1, 1)
        behind = pltpu.roll(g, 1, 1)
        zero = jnp.zeros_like(g)
        first = jnp.concatenate(
            [jnp.where(lane != LANES - 1, ahead, zero), g, jnp.where(lane != 0, behind, zero)],
            axis=0,
        )
        second = jnp.concatenate(
            [jnp.where(lane == LANES - 1, ahead, zero), zero, jnp.where(lane == 0, behind, zero)],
            axis=0,
        )
        return [first.astype(BF16), second.astype(BF16)]

    def gradient(shift_wide, window_wide, acc, shifted_first, hs):
        moved, windows = [], []
        for h in hs:
            moved += shifted(shift_wide, h)
            windows.append(window_wide[pl.ds(aligned(h, chans), tall), :])
        moved, windows = jnp.concatenate(moved, axis=1), jnp.concatenate(windows, axis=1)
        a, b = (moved, windows) if shifted_first else (windows, moved)
        acc[:, :tall] += lax.dot_general(a, b, NT, preferred_element_type=F32)

    def inner_gradient(shift_wide, window_wide, acc, shifted_first):
        count = (rows - 2) // 2

        def step(i, c):
            first = 1 + i * count
            gradient(
                shift_wide, window_wide, acc, shifted_first, [first + u for u in range(count)]
            )
            return c

        acc[...] = jnp.zeros_like(acc)
        lax.fori_loop(0, 2, step, 0)

    ends = (0, rows - 1)

    def inner_rows(row, carry):
        return lax.fori_loop(1, rows - 1, row, carry, unroll=rows - 2)

    def end_rows(row, carry):
        for h in ends:
            carry = row(h, carry)
        return carry

    loads[0].wait()
    packed = take_in(fields_in, stage, fwide)
    set_edges(FIELDS, fwide, packed)
    pl.semaphore_wait(barrier, group - 1 + depth - 1 + beside)
    start_exchange(FIELDS)
    loads[1].wait()
    packed = take_in(cot_in, stage_two, gwide)
    set_edges(COT, gwide, packed)
    start_exchange(COT)
    loads[2].wait()
    loads[3].wait()
    weight_forms()
    rim_weights()

    root = math.sqrt(2.0 / math.pi)

    def hidden_row(h, packed):
        u = conv_row(w_ref[0], fwide, h)
        square = u * u
        t = jnp.tanh(root * (u + 0.044715 * (square * u)))
        half = 0.5 * (1.0 + t)
        slope[pl.ds(aligned(h, chans), chans), :] = half + (0.5 * root) * u * (1.0 - t * t) * (
            1.0 + (3 * 0.044715) * square
        )
        value = u * half
        hwide[pl.ds(aligned(h + 1, chans), chans), own] = value.astype(BF16)
        return pack_edge(h, value, packed)

    def weights_at(kernel_at, h):
        place = jnp.where(h == 0, 0, jnp.where(h == rows - 1, 2, 1))
        return wedge[kernel_at * 3 + place]

    def back_row(h, packed):
        back = conv_row(weights_at(1, h), gwide, h)
        value = back * slope[pl.ds(aligned(h, chans), chans), :]
        dwide[pl.ds(aligned(h + 1, chans), chans), own] = value.astype(BF16)
        return pack_edge(h, value, packed)

    def set_aside(row):
        place = pl.ds(row * chans, chans)
        rim_row[...] = gwide[place, :]
        gwide[place, :] = jnp.zeros((chans, 2 * LANES), BF16)

    def credit(h, block):
        first, second = shifted(hwide, h)
        moved = jnp.concatenate([first, second], axis=1).astype(F32)
        swapped = jnp.concatenate(
            [moved[2 * chans :], moved[chans : 2 * chans], moved[:chans]], axis=0
        )
        chosen = jnp.where(rim_code == 1, swapped, moved).astype(BF16)
        acc_two[pl.ds(block * chans, chans), :tall] += lax.dot_general(
            rim_row[...], chosen, NT, preferred_element_type=F32
        )

    set_ghost_cols(FIELDS, fwide)
    hidden_packed = inner_rows(hidden_row, none)
    forward_poles(FIELDS)
    set_ghost_cols(COT, gwide)
    d_packed = inner_rows(back_row, none)
    forward_poles(COT)
    inner_gradient(dwide, fwide, acc_one, True)
    inner_gradient(hwide, gwide, acc_two, False)
    set_ghost_rows(FIELDS, fwide, True)
    hidden_packed = end_rows(hidden_row, hidden_packed)
    set_ghost_rows(COT, gwide, False)
    d_packed = end_rows(back_row, d_packed)
    gradient(dwide, fwide, acc_one, True, ends)

    @pl.when(at_top)
    def _():
        set_aside(0)

    @pl.when(at_bottom)
    def _():
        set_aside(rows + 1)

    gradient(hwide, gwide, acc_two, False, ends)

    @pl.when(at_top)
    def _():
        credit(0, 2)

    @pl.when(at_bottom)
    def _():
        credit(rows - 1, 0)

    sums[pl.ds(0, tall), :] = acc_one[:, :LANES]
    sums[pl.ds(tall, tall), :] = acc_two[:, :LANES]
    half_lane = lax.broadcasted_iota(jnp.int32, (tall, LANES), 1) < chans
    sums[pl.ds(2 * tall, tall), :] = jnp.where(
        half_lane, acc_one[:, LANES:], pltpu.roll(acc_two[:, LANES:], chans, 1)
    )
    for j in range(owners):
        rs_send[j] = sums[pl.ds(j * piece, piece), :].astype(BF16)

    def rs_copy(j):
        return put(
            rs_send.at[j], rs_recv.at[mine], rs_ssem.at[j], rs_rsem.at[mine], in_group(owner_at(j))
        )

    def rs_start(j, c):
        @pl.when(owner_at(j) != mine)
        def _():
            rs_copy(j).start()

        return c

    lax.fori_loop(0, owners, rs_start, 0)

    @pl.when(owns)
    def _():
        rs_recv[mine] = rs_send[own_piece]

    set_edges(HIDDEN, hwide, hidden_packed)
    start_exchange(HIDDEN)
    set_edges(DPRE, dwide, d_packed)
    start_exchange(DPRE)

    def out_row(h, c):
        stage[pl.ds(h, chans, stride=rows), :] = conv_row(w_ref[1], hwide, h)
        return c

    def df_row(h, c):
        stage_two[pl.ds(h, chans, stride=rows), :] = conv_row(weights_at(0, h), dwide, h)
        return c

    set_ghost_cols(HIDDEN, hwide)
    inner_rows(out_row, 0)

    def ar_copy(k):
        return put(ar_send, ar_recv.at[z], ar_ssem.at[k], ar_rsem.at[z], along_z(k))

    @pl.when(owns)
    def _():
        def wait(k, c):
            source = group_peer(k)
            put(
                rs_recv.at[mine], rs_recv.at[source], rs_ssem.at[0], rs_rsem.at[source], here
            ).wait_recv()
            return c

        lax.fori_loop(1, group, wait, 0)
        total = rs_recv[0].astype(F32)
        for k in range(1, group):
            total = total + rs_recv[k].astype(F32)
        ar_send[...] = total.astype(BF16)
        ar_recv[z] = total.astype(BF16)

        def start(k, c):
            ar_copy(k).start()
            return c

        lax.fori_loop(1, depth, start, 0)

    forward_poles(HIDDEN)
    forward_poles(DPRE)
    set_ghost_cols(DPRE, dwide)
    inner_rows(df_row, 0)
    set_ghost_rows(HIDDEN, hwide, True)
    end_rows(out_row, 0)
    set_ghost_rows(DPRE, dwide, False)
    end_rows(df_row, 0)
    out_ref[...] = stage[...].astype(BF16)
    df_ref[...] = stage_two[...].astype(BF16)

    def ag_copy(k):
        return put(
            ag_buf.at[own_piece], ag_buf.at[own_piece], ag_ssem.at[k], ag_rsem.at[own_piece],
            in_group(group_peer(k)),
        )

    @pl.when(owns)
    def _():
        def wait(k, c):
            source = lax.rem(z + k, depth)
            put(ar_send, ar_recv.at[source], ar_ssem.at[k], ar_rsem.at[source], here).wait_recv()
            return c

        lax.fori_loop(1, depth, wait, 0)
        total = ar_recv[0].astype(F32)
        for k in range(1, depth):
            total = total + ar_recv[k].astype(F32)
        ag_buf[own_piece] = total.astype(BF16)

        def start(k, c):
            ag_copy(k).start()
            return c

        lax.fori_loop(1, group, start, 0)

    for x in range(4):
        wait_sent(x)

    def rs_sent(j, c):
        @pl.when(owner_at(j) != mine)
        def _():
            rs_copy(j).wait_send()

        return c

    lax.fori_loop(0, owners, rs_sent, 0)

    @pl.when(owns)
    def _():
        def sent(k, c):
            ar_copy(k).wait_send()
            return c

        lax.fori_loop(1, depth, sent, 0)

    def ag_wait(j, c):
        @pl.when(owner_at(j) != mine)
        def _():
            put(ag_buf.at[j], ag_buf.at[j], ag_ssem.at[0], ag_rsem.at[j], here).wait_recv()

        return c

    lax.fori_loop(0, owners, ag_wait, 0)
    for j in range(owners):
        sums[pl.ds(j * piece, piece), :] = ag_buf[j].astype(F32) * scale
    one, two, rest = (sums[pl.ds(i * tall, tall), :] for i in range(3))
    one_parts = (one, pltpu.roll(one, chans, 1), rest)
    two_parts = (two, pltpu.roll(two, chans, 1), pltpu.roll(rest, chans, 1))
    for a in range(3):
        cut = slice(a * chans, (a + 1) * chans)
        for b in range(3):
            g1_ref[b, a] = one_parts[b][cut, :chans]
            g2_ref[2 - a, 2 - b] = two_parts[b][cut, :chans]

    @pl.when(owns)
    def _():
        def sent(k, c):
            ag_copy(k).wait_send()
            return c

        lax.fori_loop(1, group, sent, 0)


def hand_over(*refs):
    count = (len(refs) - 1) // 2
    sems = refs[-1]
    copies = [
        pltpu.make_async_copy(refs[i], refs[count + i], sems.at[i]) for i in range(count)
    ]
    for copy in copies:
        copy.start()
    for copy in copies:
        copy.wait()


def on_device(
    nlon, nlat, fields_in, weight_one, weight_two, cotangent,
    north_map, north_code, south_map, south_code,
):
    chans, rows, cols = fields_in.shape
    scale = 1.0 / math.sqrt(float(rows * cols * nlon * nlat))
    tall = 3 * chans
    planes = 2 if nlat % 2 == 0 else 1
    group, depth = nlon * planes, nlat // planes
    owners = max(k for k in range(1, group + 1) if 3 * tall % (8 * k) == 0)
    piece = 3 * tall // owners
    vmem = pl.BlockSpec(memory_space=pltpu.VMEM)
    smem = pl.BlockSpec(memory_space=pltpu.SMEM)
    hbm = pl.BlockSpec(memory_space=pltpu.HBM)
    wide = pltpu.VMEM(((rows + 2) * chans, 2 * LANES), BF16)
    flat16 = pltpu.VMEM((chans * rows, LANES), BF16)
    flat32 = pltpu.VMEM((chans * rows, LANES), F32)
    polar = pltpu.VMEM((nlon, chans, LANES), BF16)
    dma = pltpu.SemaphoreType.DMA

    def in_hbm(x):
        return pltpu.with_memory_space_constraint(x, pltpu.HBM)

    scratch = [
        flat16, flat16,
        pltpu.VMEM((9 * chans, chans), BF16), pltpu.VMEM((9 * chans, chans), BF16),
        flat32, flat32, wide, wide, wide, wide, flat32,
        pltpu.VMEM((4, tall, tall), BF16), pltpu.VMEM((6, tall, tall), BF16),
        pltpu.VMEM((chans, 2 * LANES), BF16),
        pltpu.VMEM((4, 3, chans, LANES), BF16), pltpu.VMEM((4, 8, chans, LANES), BF16),
        polar, polar, polar, polar,
        pltpu.VMEM((tall, 2 * LANES), F32), pltpu.VMEM((tall, 2 * LANES), F32),
        pltpu.VMEM((3 * tall, LANES), F32),
        pltpu.VMEM((owners, piece, LANES), BF16), pltpu.VMEM((group, piece, LANES), BF16),
        pltpu.VMEM((piece, LANES), BF16), pltpu.VMEM((depth, piece, LANES), BF16),
        pltpu.VMEM((owners, piece, LANES), BF16),
        dma((4,)), dma((4, 8)), dma((4, 8)), dma((4, nlon // 2)), dma((4, nlon // 2)), dma((4,)), dma((4,)),
        dma((owners,)), dma((group,)), dma((depth,)), dma((depth,)),
        dma((group,)), dma((owners,)),
    ]
    results = pl.pallas_call(
        functools.partial(kernel, nlon, nlat, planes, rows, chans, owners, scale),
        out_shape=(
            pltpu.VMEM((chans * rows, cols), BF16),
            pltpu.VMEM((chans * rows, cols), BF16),
            pltpu.VMEM((3, 3, chans, chans), F32),
            pltpu.VMEM((3, 3, chans, chans), F32),
        ),
        in_specs=[hbm, hbm, hbm, hbm, smem, smem, smem, smem],
        out_specs=(vmem, vmem, vmem, vmem),
        scratch_shapes=scratch,
        compiler_params=pltpu.CompilerParams(
            collective_id=0, has_side_effects=True, vmem_limit_bytes=VMEM_BYTES
        ),
    )(
        in_hbm(fields_in.reshape(chans * rows, cols)), in_hbm(cotangent.reshape(chans * rows, cols)),
        in_hbm(weight_one.reshape(9 * chans, chans)), in_hbm(weight_two.reshape(9 * chans, chans)),
        north_map, north_code, south_map, south_code,
    )
    output, d_fields, grad_one, grad_two = pl.pallas_call(
        hand_over,
        out_shape=tuple(jax.ShapeDtypeStruct(x.shape, x.dtype) for x in results),
        in_specs=[vmem] * 4,
        out_specs=(hbm,) * 4,
        scratch_shapes=[dma((4,))],
    )(*[pltpu.with_memory_space_constraint(x, pltpu.VMEM) for x in results])
    shape = (chans, rows, cols)
    return (output.reshape(shape), d_fields.reshape(shape), grad_one, grad_two)


def solution(mesh):
    placed = (P(None, "lat", "lon"), P(), P(), P(None, "lat", "lon"), P(), P(), P(), P())
    return jax.shard_map(
        functools.partial(on_device, mesh.shape["lon"], mesh.shape["lat"]),
        mesh=mesh,
        in_specs=placed,
        out_specs=(P(None, "lat", "lon"), P(None, "lat", "lon"), P(), P()),
        check_vma=False,
    )
```

```python
import functools
import math

import jax
import jax.numpy as jnp
from jax import lax
from jax.experimental import pallas as pl
from jax.experimental.pallas import tpu as pltpu
from jax.sharding import PartitionSpec as P

MESH = pl.DeviceIdType.MESH
LANES = 128
F32 = jnp.float32
BF16 = jnp.bfloat16
NT = (((1,), (1,)), ((), ()))
FIELDS, COT, HIDDEN, DPRE = range(4)
VMEM_BYTES = 48 * 1024 * 1024


def aligned(start, step):
    return pl.multiple_of(start * step, step)


def kernel(
    nlon, nlat, planes, rows, chans, owners, scale,
    fields_hbm, cot_hbm, one_hbm, two_hbm, nmap_hbm, ncode_hbm, smap_hbm, scode_hbm,
    out_ref, df_ref, g1_ref, g2_ref,
    fields_in, cot_in, one_ref, two_ref, north_map, north_code, south_map, south_code,
    stage, stage_two, fwide, gwide, hwide, dwide, slope, w_ref, wedge, rim_row,
    send, recv, pole_f, pole_c, pole_h, pole_d, acc_one, acc_two, sums,
    rs_send, rs_recv, ar_send, ar_recv, ag_buf,
    local_sem, near_send, near_recv, pole_send, pole_recv, hand_send, hand_recv,
    rs_ssem, rs_rsem, ar_ssem, ar_rsem, ag_ssem, ag_rsem,
):
    lon = lax.axis_index("lon")
    lat = lax.axis_index("lat")
    depth = nlat // planes
    plane = lax.div(lat, depth)
    z = lax.rem(lat, depth)
    group = nlon * planes
    mine = lon + nlon * plane
    west = lax.rem(lon + nlon - 1, nlon)
    east = lax.rem(lon + 1, nlon)
    has_north = lat > 0
    has_south = lat < nlat - 1
    at_top = lat == 0
    at_bottom = lat == nlat - 1
    at_pole = jnp.logical_or(at_top, at_bottom)
    tall = 3 * chans
    lane = lax.broadcasted_iota(jnp.int32, (chans, LANES), 1)
    own = pl.ds(0, LANES)
    ghost_cols = pl.ds(LANES, LANES)
    piece = 3 * tall // owners

    def in_group(g):
        return lax.div(g, nlon) * depth + z, lax.rem(g, nlon)

    def group_peer(k):
        return lax.rem(mine + k, group)

    def along_z(k):
        return plane * depth + lax.rem(z + k, depth), lon

    spread_owners = group % 4 == 0 and owners == group // 4 * 3

    def owner_at(j):
        return lax.div(j, 3) * 4 + lax.rem(j, 3) if spread_owners else j

    def ownership(g):
        if spread_owners:
            return lax.rem(g, 4) < 3, lax.div(g, 4) * 3 + lax.rem(g, 4)
        return g < owners, g

    owns, own_piece = ownership(mine)

    if group == 32 and planes == 2:
        far = {0: 0, 1: 1, 2: 2, 3: 1}
        steps = [(x, y, c, h) for x in range(4) for y in range(2) for c in range(2) for h in range(2)]
        steps = sorted(steps[1:], key=lambda t: -(far[t[0]] + (2 * t[3] - t[1] if t[3] else t[1])))
        others = [
            lax.rem(lax.div(lon, 4) + x, 4) * 4
            + lax.rem(lax.rem(lax.div(lon, 2), 2) + y, 2) * 2
            + lax.rem(lax.rem(lon, 2) + c, 2)
            + nlon * lax.rem(plane + h, 2)
            for x, y, c, h in steps
        ]
    else:
        others = [lax.rem(mine + k, group) for k in range(1, group)]
    z_steps = sorted(range(1, depth), key=lambda k: -min(k, depth - k))

    barrier = pltpu.get_barrier_semaphore()

    def greet(place):
        pl.semaphore_signal(
            barrier, inc=1, device_id={"lat": place[0], "lon": place[1]}, device_id_type=MESH
        )

    def greet_group(k, c):
        greet(in_group(group_peer(k)))
        return c

    def greet_z(k, c):
        greet(along_z(k))
        return c

    @pl.when(has_north)
    def _():
        for at in (west, lon, east):
            greet((lat - 1, at))

    @pl.when(has_south)
    def _():
        for at in (west, lon, east):
            greet((lat + 1, at))

    lax.fori_loop(1, group, greet_group, 0)
    lax.fori_loop(1, depth, greet_z, 0)
    beside = 3 * has_north.astype(jnp.int32) + 3 * has_south.astype(jnp.int32)

    loads = [
        pltpu.make_async_copy(source, target, local_sem.at[i])
        for i, (source, target) in enumerate(
            [
                (fields_hbm, fields_in), (cot_hbm, cot_in), (one_hbm, one_ref), (two_hbm, two_ref),
                (nmap_hbm, north_map), (ncode_hbm, north_code),
                (smap_hbm, south_map), (scode_hbm, south_code),
            ]
        )
    ]
    for load in loads:
        load.start()

    def put(src, dst, ssem, rsem, place):
        return pltpu.make_async_remote_copy(
            src_ref=src, dst_ref=dst, send_sem=ssem, recv_sem=rsem,
            device_id={"lat": place[0], "lon": place[1]}, device_id_type=MESH,
        )

    here = (lat, lon)
    pole = (pole_f, pole_c, pole_h, pole_d)

    def near_copies(x):
        def one(part, slot, at, place):
            return put(
                send.at[x, part], recv.at[x, slot], near_send.at[x, at], near_recv.at[x, slot],
                place,
            )

        sides = [one(2, 1, 0, (lat, west)), one(2, 0, 1, (lat, east))]
        up = [
            one(0, 7, 2, (lat - 1, west)), one(0, 6, 3, (lat - 1, lon)), one(0, 5, 4, (lat - 1, east))
        ]
        down = [
            one(1, 4, 5, (lat + 1, west)), one(1, 3, 6, (lat + 1, lon)), one(1, 2, 7, (lat + 1, east))
        ]
        return sides, up, down

    half = nlon // 2
    core = lax.rem(lon, 2)
    chip = lax.div(lon, 2)
    sibling = (lat, lon + 1 - 2 * core)

    def strip_at(k):
        return lax.rem(k, 2) * half + lax.div(k, 2)

    def pole_copy(x, part, k):
        return put(
            send.at[x, part], pole[x].at[core * half + chip], pole_send.at[x, k],
            pole_recv.at[x, chip], (lat, lax.rem(lon + 2 * k, nlon)),
        )

    def hand_on(x, at):
        block = pole[x].at[pl.ds(at * half, half)]
        return put(block, block, hand_send.at[x], hand_recv.at[x], sibling)

    def forward_poles(x):
        @pl.when(at_pole)
        def _():
            def step(k, c):
                source = lax.rem(chip + k, half)
                put(
                    send.at[x, 0], pole[x].at[core * half + source], pole_send.at[x, k],
                    pole_recv.at[x, source], here,
                ).wait_recv()
                return c

            lax.fori_loop(1, half, step, 0)
            hand_on(x, core).start()

    def start_exchange(x):
        sides, up, down = near_copies(x)
        for copy in sides:
            copy.start()

        @pl.when(has_north)
        def _():
            for copy in up:
                copy.start()

        @pl.when(has_south)
        def _():
            for copy in down:
                copy.start()

    def start_poles(x):
        def pole_start(part):
            def step(k, c):
                pole_copy(x, part, k).start()
                return c

            lax.fori_loop(1, half, step, 0)
            pole[x][core * half + chip] = send[x, part]

        @pl.when(at_top)
        def _():
            pole_start(0)

        @pl.when(at_bottom)
        def _():
            pole_start(1)

    def arrived(x, slot):
        put(
            send.at[x, 0], recv.at[x, slot], near_send.at[x, 0], near_recv.at[x, slot], here
        ).wait_recv()

    def wait_rows(x):
        @pl.when(has_north)
        def _():
            for slot in (2, 3, 4):
                arrived(x, slot)

        @pl.when(has_south)
        def _():
            for slot in (5, 6, 7):
                arrived(x, slot)

        @pl.when(at_pole)
        def _():
            hand_on(x, 1 - core).wait_recv()

    def wait_sent(x):
        sides, up, down = near_copies(x)
        for copy in sides:
            copy.wait_send()

        @pl.when(has_north)
        def _():
            for copy in up:
                copy.wait_send()

        @pl.when(has_south)
        def _():
            for copy in down:
                copy.wait_send()

        @pl.when(at_pole)
        def _():
            def step(k, c):
                pole_copy(x, 0, k).wait_send()
                return c

            lax.fori_loop(1, half, step, 0)
            hand_on(x, core).wait_send()

    def map_at(k):
        return jnp.where(at_top, north_map[k], south_map[k])

    def code_at(k):
        return jnp.where(at_top, north_code[k], south_code[k])

    def find_owner(k, c):
        hit = map_at(k) == lon
        return jnp.where(hit, k, c[0]), jnp.where(hit, code_at(k), c[1])

    def turned(row, code):
        i = lax.broadcasted_iota(jnp.int32, (LANES, LANES), 0)
        j = lax.broadcasted_iota(jnp.int32, (LANES, LANES), 1)
        match = (i + (2 * code - 1) * j) == (LANES - 1) * code
        turn = jnp.where(match, 1.0, 0.0).astype(BF16)
        return jnp.dot(row, turn, preferred_element_type=F32)

    def set_ghost_row(wide, row, left, mid, right):
        place = pl.ds(row * chans, chans)
        wide[place, own] = mid.astype(BF16)
        wide[place, ghost_cols] = jnp.where(lane == 0, right.astype(F32), left.astype(F32)).astype(
            BF16
        )

    def set_ghost_cols(x, wide):
        arrived(x, 0)
        arrived(x, 1)
        merged = jnp.where(lane % 2 == 0, recv[x, 1].astype(F32), recv[x, 0].astype(F32))

        def step(h, c):
            place = pl.ds(aligned(h + 1, chans), chans)
            wide[place, ghost_cols] = pltpu.roll(merged, lax.rem(LANES - 2 * h, LANES), 1).astype(
                BF16
            )
            return c

        lax.fori_loop(0, rows, step, 0, unroll=rows)

    def pack_edge(h, value, packed):
        keep = jnp.logical_or(lane == 2 * h, lane == lax.rem(2 * h + LANES - 1, LANES))
        return jnp.where(keep, pltpu.roll(value, 2 * h, 1), packed)

    def set_edges(x, wide, packed):
        send[x, 0] = wide[pl.ds(chans, chans), own]
        send[x, 1] = wide[pl.ds(rows * chans, chans), own]
        send[x, 2] = packed.astype(BF16)

    none = jnp.zeros((chans, LANES), F32)

    def take_in(source, stage, wide):
        stage[...] = source[...].astype(F32)

        def step(h, packed):
            value = stage[pl.ds(h, chans, stride=rows), :]
            wide[pl.ds(aligned(h + 1, chans), chans), own] = value.astype(BF16)
            return pack_edge(h, value, packed)

        return lax.fori_loop(0, rows, step, none, unroll=rows)

    def set_ghost_rows(x, wide, forward):
        wait_rows(x)

        @pl.when(has_north)
        def _():
            set_ghost_row(wide, 0, recv[x, 2], recv[x, 3], recv[x, 4])

        @pl.when(has_south)
        def _():
            set_ghost_row(wide, rows + 1, recv[x, 5], recv[x, 6], recv[x, 7])

        def across(row):
            if forward:
                strips = [turned(pole[x][strip_at(map_at(k))], code_at(k)) for k in (west, lon, east)]
                set_ghost_row(wide, row, *strips)
                return
            before, mid, after = [
                turned(pole[x][strip_at(lax.rem(rim_source + shift, nlon))], rim_code)
                for shift in (nlon - 1, 0, 1)
            ]
            flip = rim_code == 1
            set_ghost_row(
                wide, row, jnp.where(flip, after, before), mid, jnp.where(flip, before, after)
            )

        @pl.when(at_top)
        def _():
            across(0)

        @pl.when(at_bottom)
        def _():
            across(rows + 1)

    def weight_forms():
        def spot(shape, shift):
            i = lax.broadcasted_iota(jnp.int32, shape, 0)
            j = lax.broadcasted_iota(jnp.int32, shape, 1)
            return jnp.where(i + shift == j, 1.0, 0.0).astype(BF16)

        for at, ref in ((0, one_ref), (1, two_ref)):
            total = jnp.zeros((tall, tall), F32)
            for r in range(3):
                total = total + jnp.dot(
                    ref[r * tall : (r + 1) * tall, :],
                    spot((chans, tall), r * chans),
                    preferred_element_type=F32,
                )
            w_ref[at] = total.astype(BF16)
            for s in range(3):
                blocks = [
                    ref[((2 - r) * 3 + 2 - s) * chans : ((2 - r) * 3 + 3 - s) * chans, :]
                    for r in range(3)
                ]
                w_ref[2 + at, s * chans : (s + 1) * chans, :] = lax.dot_general(
                    spot((chans, chans), 0),
                    jnp.concatenate(blocks, axis=0),
                    NT,
                    preferred_element_type=F32,
                ).astype(BF16)

    def rim_weights():
        for kernel_at in range(2):
            base = w_ref[2 + kernel_at]
            for place in range(3):
                wedge[kernel_at * 3 + place] = base

            def replace(place, into, out_of):
                full = base.astype(F32)
                shown = lax.broadcasted_iota(jnp.int32, full.shape, 1) // chans == into
                i = lax.broadcasted_iota(jnp.int32, full.shape, 0)
                j = lax.broadcasted_iota(jnp.int32, full.shape, 1)
                move = jnp.where(i - out_of * chans == j - into * chans, 1.0, 0.0).astype(BF16)
                moved = jnp.dot(base, move, preferred_element_type=F32)
                swapped = jnp.concatenate(
                    [moved[2 * chans :], moved[chans : 2 * chans], moved[:chans]], axis=0
                )
                chosen = jnp.where(rim_code == 1, swapped, moved)
                wedge[kernel_at * 3 + place] = jnp.where(shown, chosen, full).astype(BF16)

            @pl.when(at_top)
            def _():
                replace(0, 0, 2)

            @pl.when(at_bottom)
            def _():
                replace(2, 2, 0)

    def conv_row(weights, wide, h):
        window = wide[pl.ds(aligned(h, chans), tall), :]
        y = jnp.dot(weights, window, preferred_element_type=F32)
        left = jnp.where(lane == LANES - 1, y[:chans, LANES:], y[:chans, :LANES])
        right = jnp.where(lane == 0, y[2 * chans :, LANES:], y[2 * chans :, :LANES])
        return (
            pltpu.roll(left, 1, 1) + y[chans : 2 * chans, :LANES] + pltpu.roll(right, LANES - 1, 1)
        )

    def shifted(wide, h):
        g = wide[pl.ds(aligned(h + 1, chans), chans), own].astype(F32)
        ahead = pltpu.roll(g, LANES - 1, 1)
        behind = pltpu.roll(g, 1, 1)
        zero = jnp.zeros_like(g)
        first = jnp.concatenate(
            [jnp.where(lane != LANES - 1, ahead, zero), g, jnp.where(lane != 0, behind, zero)],
            axis=0,
        )
        second = jnp.concatenate(
            [jnp.where(lane == LANES - 1, ahead, zero), zero, jnp.where(lane == 0, behind, zero)],
            axis=0,
        )
        return [first.astype(BF16), second.astype(BF16)]

    def gradient(shift_wide, window_wide, acc, shifted_first, hs):
        moved, windows = [], []
        for h in hs:
            moved += shifted(shift_wide, h)
            windows.append(window_wide[pl.ds(aligned(h, chans), tall), :])
        moved, windows = jnp.concatenate(moved, axis=1), jnp.concatenate(windows, axis=1)
        a, b = (moved, windows) if shifted_first else (windows, moved)
        acc[:, :tall] += lax.dot_general(a, b, NT, preferred_element_type=F32)

    def inner_gradient(shift_wide, window_wide, acc, shifted_first):
        count = (rows - 2) // 2

        def step(i, c):
            first = 1 + i * count
            gradient(
                shift_wide, window_wide, acc, shifted_first, [first + u for u in range(count)]
            )
            return c

        acc[...] = jnp.zeros_like(acc)
        lax.fori_loop(0, 2, step, 0)

    ends = (0, rows - 1)

    def inner_rows(row, carry):
        return lax.fori_loop(1, rows - 1, row, carry, unroll=rows - 2)

    def end_rows(row, carry):
        for h in ends:
            carry = row(h, carry)
        return carry

    loads[0].wait()
    packed = take_in(fields_in, stage, fwide)
    set_edges(FIELDS, fwide, packed)
    pl.semaphore_wait(barrier, group - 1 + depth - 1 + beside)
    start_exchange(FIELDS)
    start_poles(FIELDS)
    loads[1].wait()
    packed = take_in(cot_in, stage_two, gwide)
    set_edges(COT, gwide, packed)
    start_exchange(COT)
    start_poles(COT)
    for load in loads[2:]:
        load.wait()
    rim_source, rim_code = lax.fori_loop(0, nlon, find_owner, (jnp.int32(0), jnp.int32(0)))
    weight_forms()
    rim_weights()

    root = math.sqrt(2.0 / math.pi)

    def hidden_row(h, packed):
        u = conv_row(w_ref[0], fwide, h)
        square = u * u
        t = jnp.tanh(root * (u + 0.044715 * (square * u)))
        half = 0.5 * (1.0 + t)
        slope[pl.ds(aligned(h, chans), chans), :] = half + (0.5 * root) * u * (1.0 - t * t) * (
            1.0 + (3 * 0.044715) * square
        )
        value = u * half
        hwide[pl.ds(aligned(h + 1, chans), chans), own] = value.astype(BF16)
        return pack_edge(h, value, packed)

    def weights_at(kernel_at, h):
        place = jnp.where(h == 0, 0, jnp.where(h == rows - 1, 2, 1))
        return wedge[kernel_at * 3 + place]

    def back_row(h, packed):
        back = conv_row(weights_at(1, h), gwide, h)
        value = back * slope[pl.ds(aligned(h, chans), chans), :]
        dwide[pl.ds(aligned(h + 1, chans), chans), own] = value.astype(BF16)
        return pack_edge(h, value, packed)

    def set_aside(row):
        place = pl.ds(row * chans, chans)
        rim_row[...] = gwide[place, :]
        gwide[place, :] = jnp.zeros((chans, 2 * LANES), BF16)

    def credit(h, block):
        first, second = shifted(hwide, h)
        moved = jnp.concatenate([first, second], axis=1).astype(F32)
        swapped = jnp.concatenate(
            [moved[2 * chans :], moved[chans : 2 * chans], moved[:chans]], axis=0
        )
        chosen = jnp.where(rim_code == 1, swapped, moved).astype(BF16)
        acc_two[pl.ds(block * chans, chans), :tall] += lax.dot_general(
            rim_row[...], chosen, NT, preferred_element_type=F32
        )

    set_ghost_cols(FIELDS, fwide)
    hidden_packed = inner_rows(hidden_row, none)
    forward_poles(FIELDS)
    set_ghost_cols(COT, gwide)
    d_packed = inner_rows(back_row, none)
    forward_poles(COT)
    inner_gradient(dwide, fwide, acc_one, True)
    inner_gradient(hwide, gwide, acc_two, False)
    set_ghost_rows(FIELDS, fwide, True)
    set_ghost_rows(COT, gwide, False)
    hidden_packed = end_rows(hidden_row, hidden_packed)
    d_packed = end_rows(back_row, d_packed)

    @pl.when(at_top)
    def _():
        set_aside(0)

    @pl.when(at_bottom)
    def _():
        set_aside(rows + 1)

    gradient(dwide, fwide, acc_one, True, ends)
    gradient(hwide, gwide, acc_two, False, ends)

    @pl.when(at_top)
    def _():
        credit(0, 2)

    @pl.when(at_bottom)
    def _():
        credit(rows - 1, 0)

    sums[pl.ds(0, tall), :] = acc_one[:, :LANES]
    sums[pl.ds(tall, tall), :] = acc_two[:, :LANES]
    half_lane = lax.broadcasted_iota(jnp.int32, (tall, LANES), 1) < chans
    sums[pl.ds(2 * tall, tall), :] = jnp.where(
        half_lane, acc_one[:, LANES:], pltpu.roll(acc_two[:, LANES:], chans, 1)
    )
    for j in range(owners):
        rs_send[j] = sums[pl.ds(j * piece, piece), :].astype(BF16)

    def rs_copy(j):
        return put(
            rs_send.at[j], rs_recv.at[mine], rs_ssem.at[j], rs_rsem.at[mine], in_group(owner_at(j))
        )

    for other in others:
        takes, taken = ownership(other)

        @pl.when(takes)
        def _():
            put(
                rs_send.at[taken], rs_recv.at[mine], rs_ssem.at[taken], rs_rsem.at[mine],
                in_group(other),
            ).start()

    @pl.when(owns)
    def _():
        rs_recv[mine] = rs_send[own_piece]

    set_edges(HIDDEN, hwide, hidden_packed)
    start_exchange(HIDDEN)
    set_edges(DPRE, dwide, d_packed)
    start_exchange(DPRE)

    def out_row(h, c):
        stage[pl.ds(h, chans, stride=rows), :] = conv_row(w_ref[1], hwide, h)
        return c

    def df_row(h, c):
        stage_two[pl.ds(h, chans, stride=rows), :] = conv_row(weights_at(0, h), dwide, h)
        return c

    set_ghost_cols(HIDDEN, hwide)
    inner_rows(out_row, 0)

    def ar_copy(k):
        return put(ar_send, ar_recv.at[z], ar_ssem.at[k], ar_rsem.at[z], along_z(k))

    @pl.when(owns)
    def _():
        def wait(k, c):
            source = group_peer(k)
            put(
                rs_recv.at[mine], rs_recv.at[source], rs_ssem.at[0], rs_rsem.at[source], here
            ).wait_recv()
            return c

        lax.fori_loop(1, group, wait, 0)
        total = rs_recv[0].astype(F32)
        for k in range(1, group):
            total = total + rs_recv[k].astype(F32)
        ar_send[...] = total.astype(BF16)
        ar_recv[z] = total.astype(BF16)

        for k in z_steps:
            ar_copy(k).start()

    start_poles(HIDDEN)
    start_poles(DPRE)
    set_ghost_cols(DPRE, dwide)
    inner_rows(df_row, 0)

    def ag_copy(k):
        return put(
            ag_buf.at[own_piece], ag_buf.at[own_piece], ag_ssem.at[k], ag_rsem.at[own_piece],
            in_group(others[k]),
        )

    @pl.when(owns)
    def _():
        def wait(k, c):
            source = lax.rem(z + k, depth)
            put(ar_send, ar_recv.at[source], ar_ssem.at[k], ar_rsem.at[source], here).wait_recv()
            return c

        lax.fori_loop(1, depth, wait, 0)
        total = ar_recv[0].astype(F32)
        for k in range(1, depth):
            total = total + ar_recv[k].astype(F32)
        ag_buf[own_piece] = total.astype(BF16)

        for k in range(group - 1):
            ag_copy(k).start()

    forward_poles(HIDDEN)
    forward_poles(DPRE)
    set_ghost_rows(HIDDEN, hwide, True)
    set_ghost_rows(DPRE, dwide, False)
    end_rows(out_row, 0)
    end_rows(df_row, 0)
    out_ref[...] = stage[...].astype(BF16)
    df_ref[...] = stage_two[...].astype(BF16)

    for x in range(4):
        wait_sent(x)

    def rs_sent(j, c):
        @pl.when(owner_at(j) != mine)
        def _():
            rs_copy(j).wait_send()

        return c

    lax.fori_loop(0, owners, rs_sent, 0)

    @pl.when(owns)
    def _():
        def sent(k, c):
            ar_copy(k).wait_send()
            return c

        lax.fori_loop(1, depth, sent, 0)

    def ag_wait(j, c):
        @pl.when(owner_at(j) != mine)
        def _():
            put(ag_buf.at[j], ag_buf.at[j], ag_ssem.at[0], ag_rsem.at[j], here).wait_recv()

        return c

    lax.fori_loop(0, owners, ag_wait, 0)
    for j in range(owners):
        sums[pl.ds(j * piece, piece), :] = ag_buf[j].astype(F32) * scale
    one, two, rest = (sums[pl.ds(i * tall, tall), :] for i in range(3))
    one_parts = (one, pltpu.roll(one, chans, 1), rest)
    two_parts = (two, pltpu.roll(two, chans, 1), pltpu.roll(rest, chans, 1))
    for a in range(3):
        cut = slice(a * chans, (a + 1) * chans)
        for b in range(3):
            g1_ref[b, a] = one_parts[b][cut, :chans]
            g2_ref[2 - a, 2 - b] = two_parts[b][cut, :chans]

    @pl.when(owns)
    def _():
        for k in range(group - 1):
            ag_copy(k).wait_send()


def hand_over(*refs):
    count = (len(refs) - 1) // 2
    sems = refs[-1]
    copies = [
        pltpu.make_async_copy(refs[i], refs[count + i], sems.at[i]) for i in range(count)
    ]
    for copy in copies:
        copy.start()
    for copy in copies:
        copy.wait()


def on_device(
    nlon, nlat, fields_in, weight_one, weight_two, cotangent,
    north_map, north_code, south_map, south_code,
):
    chans, rows, cols = fields_in.shape
    scale = 1.0 / math.sqrt(float(rows * cols * nlon * nlat))
    tall = 3 * chans
    planes = 2 if nlat % 2 == 0 else 1
    group, depth = nlon * planes, nlat // planes
    owners = max(k for k in range(1, group + 1) if 3 * tall % (8 * k) == 0)
    piece = 3 * tall // owners
    vmem = pl.BlockSpec(memory_space=pltpu.VMEM)
    hbm = pl.BlockSpec(memory_space=pltpu.HBM)
    wide = pltpu.VMEM(((rows + 2) * chans, 2 * LANES), BF16)
    flat16 = pltpu.VMEM((chans * rows, LANES), BF16)
    flat32 = pltpu.VMEM((chans * rows, LANES), F32)
    polar = pltpu.VMEM((nlon, chans, LANES), BF16)
    maps = pltpu.SMEM((nlon,), jnp.int32)
    dma = pltpu.SemaphoreType.DMA

    def in_hbm(x):
        return pltpu.with_memory_space_constraint(x, pltpu.HBM)

    scratch = [
        flat16, flat16,
        pltpu.VMEM((9 * chans, chans), BF16), pltpu.VMEM((9 * chans, chans), BF16),
        maps, maps, maps, maps,
        flat32, flat32, wide, wide, wide, wide, flat32,
        pltpu.VMEM((4, tall, tall), BF16), pltpu.VMEM((6, tall, tall), BF16),
        pltpu.VMEM((chans, 2 * LANES), BF16),
        pltpu.VMEM((4, 3, chans, LANES), BF16), pltpu.VMEM((4, 8, chans, LANES), BF16),
        polar, polar, polar, polar,
        pltpu.VMEM((tall, 2 * LANES), F32), pltpu.VMEM((tall, 2 * LANES), F32),
        pltpu.VMEM((3 * tall, LANES), F32),
        pltpu.VMEM((owners, piece, LANES), BF16), pltpu.VMEM((group, piece, LANES), BF16),
        pltpu.VMEM((piece, LANES), BF16), pltpu.VMEM((depth, piece, LANES), BF16),
        pltpu.VMEM((owners, piece, LANES), BF16),
        dma((8,)), dma((4, 8)), dma((4, 8)), dma((4, nlon // 2)), dma((4, nlon // 2)), dma((4,)), dma((4,)),
        dma((owners,)), dma((group,)), dma((depth,)), dma((depth,)),
        dma((group,)), dma((owners,)),
    ]
    results = pl.pallas_call(
        functools.partial(kernel, nlon, nlat, planes, rows, chans, owners, scale),
        out_shape=(
            pltpu.VMEM((chans * rows, cols), BF16),
            pltpu.VMEM((chans * rows, cols), BF16),
            pltpu.VMEM((3, 3, chans, chans), F32),
            pltpu.VMEM((3, 3, chans, chans), F32),
        ),
        in_specs=[hbm] * 8,
        out_specs=(vmem, vmem, vmem, vmem),
        scratch_shapes=scratch,
        compiler_params=pltpu.CompilerParams(
            collective_id=0, has_side_effects=True, vmem_limit_bytes=VMEM_BYTES
        ),
    )(
        in_hbm(fields_in.reshape(chans * rows, cols)), in_hbm(cotangent.reshape(chans * rows, cols)),
        in_hbm(weight_one.reshape(9 * chans, chans)), in_hbm(weight_two.reshape(9 * chans, chans)),
        in_hbm(north_map), in_hbm(north_code), in_hbm(south_map), in_hbm(south_code),
    )
    output, d_fields, grad_one, grad_two = pl.pallas_call(
        hand_over,
        out_shape=tuple(jax.ShapeDtypeStruct(x.shape, x.dtype) for x in results),
        in_specs=[vmem] * 4,
        out_specs=(hbm,) * 4,
        scratch_shapes=[dma((4,))],
    )(*[pltpu.with_memory_space_constraint(x, pltpu.VMEM) for x in results])
    shape = (chans, rows, cols)
    return (output.reshape(shape), d_fields.reshape(shape), grad_one, grad_two)


def solution(mesh):
    placed = (P(None, "lat", "lon"), P(), P(), P(None, "lat", "lon"), P(), P(), P(), P())
    return jax.shard_map(
        functools.partial(on_device, mesh.shape["lon"], mesh.shape["lat"]),
        mesh=mesh,
        in_specs=placed,
        out_specs=(P(None, "lat", "lon"), P(None, "lat", "lon"), P(), P()),
        check_vma=False,
    )
```

```python
import functools
import math

import jax
import jax.numpy as jnp
from jax import lax
from jax.experimental import pallas as pl
from jax.experimental.pallas import tpu as pltpu
from jax.sharding import PartitionSpec as P

MESH = pl.DeviceIdType.MESH
LANES = 128
F32 = jnp.float32
BF16 = jnp.bfloat16
NT = (((1,), (1,)), ((), ()))
FIELDS, COT, HIDDEN, DPRE = range(4)
VMEM_BYTES = 48 * 1024 * 1024


def aligned(start, step):
    return pl.multiple_of(start * step, step)


def kernel(
    nlon, nlat, planes, rows, chans, owners, scale,
    fields_hbm, cot_hbm, one_hbm, two_hbm, nmap_hbm, ncode_hbm, smap_hbm, scode_hbm,
    out_ref, df_ref, g1_ref, g2_ref,
    fields_in, cot_in, one_ref, two_ref, north_map, north_code, south_map, south_code,
    stage, stage_two, fwide, gwide, hwide, dwide, slope, w_ref, wedge, rim_row,
    send, recv, pole_f, pole_c, pole_h, pole_d, acc_one, acc_two, sums,
    rs_send, rs_recv, ar_send, ar_recv, ag_buf,
    local_sem, near_send, near_recv, pole_send, pole_recv, hand_send, hand_recv,
    rs_ssem, rs_rsem, ar_ssem, ar_rsem, ag_ssem, ag_rsem, told,
):
    lon = lax.axis_index("lon")
    lat = lax.axis_index("lat")
    depth = nlat // planes
    plane = lax.div(lat, depth)
    z = lax.rem(lat, depth)
    group = nlon * planes
    mine = lon + nlon * plane
    west = lax.rem(lon + nlon - 1, nlon)
    east = lax.rem(lon + 1, nlon)
    has_north = lat > 0
    has_south = lat < nlat - 1
    at_top = lat == 0
    at_bottom = lat == nlat - 1
    at_pole = jnp.logical_or(at_top, at_bottom)
    tall = 3 * chans
    lane = lax.broadcasted_iota(jnp.int32, (chans, LANES), 1)
    own = pl.ds(0, LANES)
    ghost_cols = pl.ds(LANES, LANES)
    piece = 3 * tall // owners

    def in_group(g):
        return lax.div(g, nlon) * depth + z, lax.rem(g, nlon)

    def group_peer(k):
        return lax.rem(mine + k, group)

    def along_z(k):
        return plane * depth + lax.rem(z + k, depth), lon

    spread_owners = group % 4 == 0 and owners == group // 4 * 3

    def owner_at(j):
        return lax.div(j, 3) * 4 + lax.rem(j, 3) if spread_owners else j

    def ownership(g):
        if spread_owners:
            return lax.rem(g, 4) < 3, lax.div(g, 4) * 3 + lax.rem(g, 4)
        return g < owners, g

    owns, own_piece = ownership(mine)

    if group == 32 and planes == 2:
        far = {0: 0, 1: 1, 2: 2, 3: 1}
        steps = [(x, y, c, h) for x in range(4) for y in range(2) for c in range(2) for h in range(2)]
        steps = sorted(steps[1:], key=lambda t: -(far[t[0]] + (2 * t[3] - t[1] if t[3] else t[1])))
        others = [
            lax.rem(lax.div(lon, 4) + x, 4) * 4
            + lax.rem(lax.rem(lax.div(lon, 2), 2) + y, 2) * 2
            + lax.rem(lax.rem(lon, 2) + c, 2)
            + nlon * lax.rem(plane + h, 2)
            for x, y, c, h in steps
        ]
    else:
        others = [lax.rem(mine + k, group) for k in range(1, group)]
    z_steps = sorted(range(1, depth), key=lambda k: -min(k, depth - k))

    barrier = pltpu.get_barrier_semaphore()

    def greet(place):
        pl.semaphore_signal(
            barrier, inc=1, device_id={"lat": place[0], "lon": place[1]}, device_id_type=MESH
        )

    def greet_group(k, c):
        greet(in_group(group_peer(k)))
        return c

    def greet_z(k, c):
        greet(along_z(k))
        return c

    @pl.when(has_north)
    def _():
        for at in (west, lon, east):
            greet((lat - 1, at))

    @pl.when(has_south)
    def _():
        for at in (west, lon, east):
            greet((lat + 1, at))

    relayed = planes == 2 and 4 <= depth <= 8
    partner = ((1 - plane) * depth + z, lon)
    if relayed:
        def greet_row(k, c):
            greet((lat, lax.rem(lon + k, nlon)))
            return c

        lax.fori_loop(1, nlon, greet_row, 0)
        for place in (along_z(1), along_z(depth - 1), partner):
            greet(place)
        greeted = nlon - 1 + 3
    else:
        lax.fori_loop(1, group, greet_group, 0)
        lax.fori_loop(1, depth, greet_z, 0)
        greeted = group - 1 + depth - 1

    def tell(at, place):
        pl.semaphore_signal(
            told.at[at], inc=1, device_id={"lat": place[0], "lon": place[1]}, device_id_type=MESH
        )

    def tell_near():
        if relayed:
            tell(0, along_z(1))
            tell(1, along_z(depth - 1))
            tell(2, partner)

    def tell_far():
        if relayed:
            for at in range(3):
                pl.semaphore_wait(told.at[at], 1)
            tell(3, along_z(2))
            tell(4, along_z(depth - 2))

    def all_told():
        if relayed:
            for at in (3, 4):
                pl.semaphore_wait(told.at[at], 1)

    beside = 3 * has_north.astype(jnp.int32) + 3 * has_south.astype(jnp.int32)

    loads = [
        pltpu.make_async_copy(source, target, local_sem.at[i])
        for i, (source, target) in enumerate(
            [
                (fields_hbm, fields_in), (cot_hbm, cot_in), (one_hbm, one_ref), (two_hbm, two_ref),
                (nmap_hbm, north_map), (ncode_hbm, north_code),
                (smap_hbm, south_map), (scode_hbm, south_code),
            ]
        )
    ]
    for load in loads:
        load.start()

    def put(src, dst, ssem, rsem, place):
        return pltpu.make_async_remote_copy(
            src_ref=src, dst_ref=dst, send_sem=ssem, recv_sem=rsem,
            device_id={"lat": place[0], "lon": place[1]}, device_id_type=MESH,
        )

    here = (lat, lon)
    pole = (pole_f, pole_c, pole_h, pole_d)

    def near_copies(x):
        def one(part, slot, at, place):
            return put(
                send.at[x, part], recv.at[x, slot], near_send.at[x, at], near_recv.at[x, slot],
                place,
            )

        sides = [one(2, 1, 0, (lat, west)), one(2, 0, 1, (lat, east))]
        up = [
            one(0, 7, 2, (lat - 1, west)), one(0, 6, 3, (lat - 1, lon)), one(0, 5, 4, (lat - 1, east))
        ]
        down = [
            one(1, 4, 5, (lat + 1, west)), one(1, 3, 6, (lat + 1, lon)), one(1, 2, 7, (lat + 1, east))
        ]
        return sides, up, down

    half = nlon // 2
    core = lax.rem(lon, 2)
    chip = lax.div(lon, 2)
    sibling = (lat, lon + 1 - 2 * core)

    def strip_at(k):
        return lax.rem(k, 2) * half + lax.div(k, 2)

    def pole_copy(x, part, k):
        return put(
            send.at[x, part], pole[x].at[core * half + chip], pole_send.at[x, k],
            pole_recv.at[x, chip], (lat, lax.rem(lon + 2 * k, nlon)),
        )

    def hand_on(x, at):
        block = pole[x].at[pl.ds(at * half, half)]
        return put(block, block, hand_send.at[x], hand_recv.at[x], sibling)

    def forward_poles(x):
        @pl.when(at_pole)
        def _():
            def step(k, c):
                source = lax.rem(chip + k, half)
                put(
                    send.at[x, 0], pole[x].at[core * half + source], pole_send.at[x, k],
                    pole_recv.at[x, source], here,
                ).wait_recv()
                return c

            lax.fori_loop(1, half, step, 0)
            hand_on(x, core).start()

    def start_exchange(x):
        sides, up, down = near_copies(x)
        for copy in sides:
            copy.start()

        @pl.when(has_north)
        def _():
            for copy in up:
                copy.start()

        @pl.when(has_south)
        def _():
            for copy in down:
                copy.start()

    def start_poles(x):
        def pole_start(part):
            def step(k, c):
                pole_copy(x, part, k).start()
                return c

            lax.fori_loop(1, half, step, 0)
            pole[x][core * half + chip] = send[x, part]

        @pl.when(at_top)
        def _():
            pole_start(0)

        @pl.when(at_bottom)
        def _():
            pole_start(1)

    def arrived(x, slot):
        put(
            send.at[x, 0], recv.at[x, slot], near_send.at[x, 0], near_recv.at[x, slot], here
        ).wait_recv()

    def wait_rows(x):
        @pl.when(has_north)
        def _():
            for slot in (2, 3, 4):
                arrived(x, slot)

        @pl.when(has_south)
        def _():
            for slot in (5, 6, 7):
                arrived(x, slot)

        @pl.when(at_pole)
        def _():
            hand_on(x, 1 - core).wait_recv()

    def wait_sent(x):
        sides, up, down = near_copies(x)
        for copy in sides:
            copy.wait_send()

        @pl.when(has_north)
        def _():
            for copy in up:
                copy.wait_send()

        @pl.when(has_south)
        def _():
            for copy in down:
                copy.wait_send()

        @pl.when(at_pole)
        def _():
            def step(k, c):
                pole_copy(x, 0, k).wait_send()
                return c

            lax.fori_loop(1, half, step, 0)
            hand_on(x, core).wait_send()

    def map_at(k):
        return jnp.where(at_top, north_map[k], south_map[k])

    def code_at(k):
        return jnp.where(at_top, north_code[k], south_code[k])

    def find_owner(k, c):
        hit = map_at(k) == lon
        return jnp.where(hit, k, c[0]), jnp.where(hit, code_at(k), c[1])

    def turned(row, code):
        i = lax.broadcasted_iota(jnp.int32, (LANES, LANES), 0)
        j = lax.broadcasted_iota(jnp.int32, (LANES, LANES), 1)
        match = (i + (2 * code - 1) * j) == (LANES - 1) * code
        turn = jnp.where(match, 1.0, 0.0).astype(BF16)
        return jnp.dot(row, turn, preferred_element_type=F32)

    def set_ghost_row(wide, row, left, mid, right):
        place = pl.ds(row * chans, chans)
        wide[place, own] = mid.astype(BF16)
        wide[place, ghost_cols] = jnp.where(lane == 0, right.astype(F32), left.astype(F32)).astype(
            BF16
        )

    def set_ghost_cols(x, wide):
        arrived(x, 0)
        arrived(x, 1)
        merged = jnp.where(lane % 2 == 0, recv[x, 1].astype(F32), recv[x, 0].astype(F32))

        def step(h, c):
            place = pl.ds(aligned(h + 1, chans), chans)
            wide[place, ghost_cols] = pltpu.roll(merged, lax.rem(LANES - 2 * h, LANES), 1).astype(
                BF16
            )
            return c

        lax.fori_loop(0, rows, step, 0, unroll=rows)

    def pack_edge(h, value, packed):
        keep = jnp.logical_or(lane == 2 * h, lane == lax.rem(2 * h + LANES - 1, LANES))
        return jnp.where(keep, pltpu.roll(value, 2 * h, 1), packed)

    def set_edges(x, wide, packed):
        send[x, 0] = wide[pl.ds(chans, chans), own]
        send[x, 1] = wide[pl.ds(rows * chans, chans), own]
        send[x, 2] = packed.astype(BF16)

    none = jnp.zeros((chans, LANES), F32)

    def take_in(source, stage, wide):
        stage[...] = source[...].astype(F32)

        def step(h, packed):
            value = stage[pl.ds(h, chans, stride=rows), :]
            wide[pl.ds(aligned(h + 1, chans), chans), own] = value.astype(BF16)
            return pack_edge(h, value, packed)

        return lax.fori_loop(0, rows, step, none, unroll=rows)

    def set_ghost_rows(x, wide, forward):
        wait_rows(x)

        @pl.when(has_north)
        def _():
            set_ghost_row(wide, 0, recv[x, 2], recv[x, 3], recv[x, 4])

        @pl.when(has_south)
        def _():
            set_ghost_row(wide, rows + 1, recv[x, 5], recv[x, 6], recv[x, 7])

        def across(row):
            if forward:
                strips = [turned(pole[x][strip_at(map_at(k))], code_at(k)) for k in (west, lon, east)]
                set_ghost_row(wide, row, *strips)
                return
            before, mid, after = [
                turned(pole[x][strip_at(lax.rem(rim_source + shift, nlon))], rim_code)
                for shift in (nlon - 1, 0, 1)
            ]
            flip = rim_code == 1
            set_ghost_row(
                wide, row, jnp.where(flip, after, before), mid, jnp.where(flip, before, after)
            )

        @pl.when(at_top)
        def _():
            across(0)

        @pl.when(at_bottom)
        def _():
            across(rows + 1)

    def weight_forms():
        def spot(shape, shift):
            i = lax.broadcasted_iota(jnp.int32, shape, 0)
            j = lax.broadcasted_iota(jnp.int32, shape, 1)
            return jnp.where(i + shift == j, 1.0, 0.0).astype(BF16)

        for at, ref in ((0, one_ref), (1, two_ref)):
            total = jnp.zeros((tall, tall), F32)
            for r in range(3):
                total = total + jnp.dot(
                    ref[r * tall : (r + 1) * tall, :],
                    spot((chans, tall), r * chans),
                    preferred_element_type=F32,
                )
            w_ref[at] = total.astype(BF16)
            for s in range(3):
                blocks = [
                    ref[((2 - r) * 3 + 2 - s) * chans : ((2 - r) * 3 + 3 - s) * chans, :]
                    for r in range(3)
                ]
                w_ref[2 + at, s * chans : (s + 1) * chans, :] = lax.dot_general(
                    spot((chans, chans), 0),
                    jnp.concatenate(blocks, axis=0),
                    NT,
                    preferred_element_type=F32,
                ).astype(BF16)

    def rim_weights():
        for kernel_at in range(2):
            base = w_ref[2 + kernel_at]
            for place in range(3):
                wedge[kernel_at * 3 + place] = base

            def replace(place, into, out_of):
                full = base.astype(F32)
                shown = lax.broadcasted_iota(jnp.int32, full.shape, 1) // chans == into
                i = lax.broadcasted_iota(jnp.int32, full.shape, 0)
                j = lax.broadcasted_iota(jnp.int32, full.shape, 1)
                move = jnp.where(i - out_of * chans == j - into * chans, 1.0, 0.0).astype(BF16)
                moved = jnp.dot(base, move, preferred_element_type=F32)
                swapped = jnp.concatenate(
                    [moved[2 * chans :], moved[chans : 2 * chans], moved[:chans]], axis=0
                )
                chosen = jnp.where(rim_code == 1, swapped, moved)
                wedge[kernel_at * 3 + place] = jnp.where(shown, chosen, full).astype(BF16)

            @pl.when(at_top)
            def _():
                replace(0, 0, 2)

            @pl.when(at_bottom)
            def _():
                replace(2, 2, 0)

    def conv_row(weights, wide, h):
        window = wide[pl.ds(aligned(h, chans), tall), :]
        y = jnp.dot(weights, window, preferred_element_type=F32)
        left = jnp.where(lane == LANES - 1, y[:chans, LANES:], y[:chans, :LANES])
        right = jnp.where(lane == 0, y[2 * chans :, LANES:], y[2 * chans :, :LANES])
        return (
            pltpu.roll(left, 1, 1) + y[chans : 2 * chans, :LANES] + pltpu.roll(right, LANES - 1, 1)
        )

    def shifted(wide, h):
        g = wide[pl.ds(aligned(h + 1, chans), chans), own].astype(F32)
        ahead = pltpu.roll(g, LANES - 1, 1)
        behind = pltpu.roll(g, 1, 1)
        zero = jnp.zeros_like(g)
        first = jnp.concatenate(
            [jnp.where(lane != LANES - 1, ahead, zero), g, jnp.where(lane != 0, behind, zero)],
            axis=0,
        )
        second = jnp.concatenate(
            [jnp.where(lane == LANES - 1, ahead, zero), zero, jnp.where(lane == 0, behind, zero)],
            axis=0,
        )
        return [first.astype(BF16), second.astype(BF16)]

    def gradient(shift_wide, window_wide, acc, shifted_first, hs):
        moved, windows = [], []
        for h in hs:
            moved += shifted(shift_wide, h)
            windows.append(window_wide[pl.ds(aligned(h, chans), tall), :])
        moved, windows = jnp.concatenate(moved, axis=1), jnp.concatenate(windows, axis=1)
        a, b = (moved, windows) if shifted_first else (windows, moved)
        acc[:, :tall] += lax.dot_general(a, b, NT, preferred_element_type=F32)

    def inner_gradient(shift_wide, window_wide, acc, shifted_first):
        count = (rows - 2) // 2

        def step(i, c):
            first = 1 + i * count
            gradient(
                shift_wide, window_wide, acc, shifted_first, [first + u for u in range(count)]
            )
            return c

        acc[...] = jnp.zeros_like(acc)
        lax.fori_loop(0, 2, step, 0)

    ends = (0, rows - 1)

    def inner_rows(row, carry):
        return lax.fori_loop(1, rows - 1, row, carry, unroll=rows - 2)

    def end_rows(row, carry):
        for h in ends:
            carry = row(h, carry)
        return carry

    loads[0].wait()
    packed = take_in(fields_in, stage, fwide)
    set_edges(FIELDS, fwide, packed)
    pl.semaphore_wait(barrier, greeted + beside)
    start_exchange(FIELDS)
    start_poles(FIELDS)
    tell_near()
    loads[1].wait()
    packed = take_in(cot_in, stage_two, gwide)
    set_edges(COT, gwide, packed)
    start_exchange(COT)
    start_poles(COT)
    for load in loads[2:]:
        load.wait()
    rim_source, rim_code = lax.fori_loop(0, nlon, find_owner, (jnp.int32(0), jnp.int32(0)))
    weight_forms()
    rim_weights()

    root = math.sqrt(2.0 / math.pi)

    def hidden_row(h, packed):
        u = conv_row(w_ref[0], fwide, h)
        square = u * u
        t = jnp.tanh(root * (u + 0.044715 * (square * u)))
        half = 0.5 * (1.0 + t)
        slope[pl.ds(aligned(h, chans), chans), :] = half + (0.5 * root) * u * (1.0 - t * t) * (
            1.0 + (3 * 0.044715) * square
        )
        value = u * half
        hwide[pl.ds(aligned(h + 1, chans), chans), own] = value.astype(BF16)
        return pack_edge(h, value, packed)

    def weights_at(kernel_at, h):
        place = jnp.where(h == 0, 0, jnp.where(h == rows - 1, 2, 1))
        return wedge[kernel_at * 3 + place]

    def back_row(h, packed):
        back = conv_row(weights_at(1, h), gwide, h)
        value = back * slope[pl.ds(aligned(h, chans), chans), :]
        dwide[pl.ds(aligned(h + 1, chans), chans), own] = value.astype(BF16)
        return pack_edge(h, value, packed)

    def set_aside(row):
        place = pl.ds(row * chans, chans)
        rim_row[...] = gwide[place, :]
        gwide[place, :] = jnp.zeros((chans, 2 * LANES), BF16)

    def credit(h, block):
        first, second = shifted(hwide, h)
        moved = jnp.concatenate([first, second], axis=1).astype(F32)
        swapped = jnp.concatenate(
            [moved[2 * chans :], moved[chans : 2 * chans], moved[:chans]], axis=0
        )
        chosen = jnp.where(rim_code == 1, swapped, moved).astype(BF16)
        acc_two[pl.ds(block * chans, chans), :tall] += lax.dot_general(
            rim_row[...], chosen, NT, preferred_element_type=F32
        )

    set_ghost_cols(FIELDS, fwide)
    hidden_packed = inner_rows(hidden_row, none)
    tell_far()
    forward_poles(FIELDS)
    set_ghost_cols(COT, gwide)
    d_packed = inner_rows(back_row, none)
    forward_poles(COT)
    all_told()
    inner_gradient(dwide, fwide, acc_one, True)
    inner_gradient(hwide, gwide, acc_two, False)
    set_ghost_rows(FIELDS, fwide, True)
    set_ghost_rows(COT, gwide, False)
    hidden_packed = end_rows(hidden_row, hidden_packed)
    d_packed = end_rows(back_row, d_packed)

    @pl.when(at_top)
    def _():
        set_aside(0)

    @pl.when(at_bottom)
    def _():
        set_aside(rows + 1)

    gradient(dwide, fwide, acc_one, True, ends)
    gradient(hwide, gwide, acc_two, False, ends)

    @pl.when(at_top)
    def _():
        credit(0, 2)

    @pl.when(at_bottom)
    def _():
        credit(rows - 1, 0)

    sums[pl.ds(0, tall), :] = acc_one[:, :LANES]
    sums[pl.ds(tall, tall), :] = acc_two[:, :LANES]
    half_lane = lax.broadcasted_iota(jnp.int32, (tall, LANES), 1) < chans
    sums[pl.ds(2 * tall, tall), :] = jnp.where(
        half_lane, acc_one[:, LANES:], pltpu.roll(acc_two[:, LANES:], chans, 1)
    )
    for j in range(owners):
        rs_send[j] = sums[pl.ds(j * piece, piece), :].astype(BF16)

    def rs_copy(j):
        return put(
            rs_send.at[j], rs_recv.at[mine], rs_ssem.at[j], rs_rsem.at[mine], in_group(owner_at(j))
        )

    for other in others:
        takes, taken = ownership(other)

        @pl.when(takes)
        def _():
            put(
                rs_send.at[taken], rs_recv.at[mine], rs_ssem.at[taken], rs_rsem.at[mine],
                in_group(other),
            ).start()

    @pl.when(owns)
    def _():
        rs_recv[mine] = rs_send[own_piece]

    set_edges(HIDDEN, hwide, hidden_packed)
    start_exchange(HIDDEN)
    set_edges(DPRE, dwide, d_packed)
    start_exchange(DPRE)

    def out_row(h, c):
        stage[pl.ds(h, chans, stride=rows), :] = conv_row(w_ref[1], hwide, h)
        return c

    def df_row(h, c):
        stage_two[pl.ds(h, chans, stride=rows), :] = conv_row(weights_at(0, h), dwide, h)
        return c

    set_ghost_cols(HIDDEN, hwide)
    inner_rows(out_row, 0)

    def ar_copy(k):
        return put(ar_send, ar_recv.at[z], ar_ssem.at[k], ar_rsem.at[z], along_z(k))

    @pl.when(owns)
    def _():
        def wait(k, c):
            source = group_peer(k)
            put(
                rs_recv.at[mine], rs_recv.at[source], rs_ssem.at[0], rs_rsem.at[source], here
            ).wait_recv()
            return c

        lax.fori_loop(1, group, wait, 0)
        total = rs_recv[0].astype(F32)
        for k in range(1, group):
            total = total + rs_recv[k].astype(F32)
        ar_send[...] = total.astype(BF16)
        ar_recv[z] = total.astype(BF16)

        for k in z_steps:
            ar_copy(k).start()

    start_poles(HIDDEN)
    start_poles(DPRE)
    set_ghost_cols(DPRE, dwide)
    inner_rows(df_row, 0)

    def ag_copy(k):
        return put(
            ag_buf.at[own_piece], ag_buf.at[own_piece], ag_ssem.at[k], ag_rsem.at[own_piece],
            in_group(others[k]),
        )

    @pl.when(owns)
    def _():
        def wait(k, c):
            source = lax.rem(z + k, depth)
            put(ar_send, ar_recv.at[source], ar_ssem.at[k], ar_rsem.at[source], here).wait_recv()
            return c

        lax.fori_loop(1, depth, wait, 0)
        total = ar_recv[0].astype(F32)
        for k in range(1, depth):
            total = total + ar_recv[k].astype(F32)
        ag_buf[own_piece] = total.astype(BF16)

        for k in range(group - 1):
            ag_copy(k).start()

    forward_poles(HIDDEN)
    forward_poles(DPRE)
    set_ghost_rows(HIDDEN, hwide, True)
    set_ghost_rows(DPRE, dwide, False)
    end_rows(out_row, 0)
    end_rows(df_row, 0)
    out_ref[...] = stage[...].astype(BF16)
    df_ref[...] = stage_two[...].astype(BF16)

    for x in range(4):
        wait_sent(x)

    def rs_sent(j, c):
        @pl.when(owner_at(j) != mine)
        def _():
            rs_copy(j).wait_send()

        return c

    lax.fori_loop(0, owners, rs_sent, 0)

    @pl.when(owns)
    def _():
        def sent(k, c):
            ar_copy(k).wait_send()
            return c

        lax.fori_loop(1, depth, sent, 0)

    def ag_wait(j, c):
        @pl.when(owner_at(j) != mine)
        def _():
            put(ag_buf.at[j], ag_buf.at[j], ag_ssem.at[0], ag_rsem.at[j], here).wait_recv()

        return c

    lax.fori_loop(0, owners, ag_wait, 0)
    for j in range(owners):
        sums[pl.ds(j * piece, piece), :] = ag_buf[j].astype(F32) * scale
    one, two, rest = (sums[pl.ds(i * tall, tall), :] for i in range(3))
    one_parts = (one, pltpu.roll(one, chans, 1), rest)
    two_parts = (two, pltpu.roll(two, chans, 1), pltpu.roll(rest, chans, 1))
    for a in range(3):
        cut = slice(a * chans, (a + 1) * chans)
        for b in range(3):
            g1_ref[b, a] = one_parts[b][cut, :chans]
            g2_ref[2 - a, 2 - b] = two_parts[b][cut, :chans]

    @pl.when(owns)
    def _():
        for k in range(group - 1):
            ag_copy(k).wait_send()


def hand_over(*refs):
    count = (len(refs) - 1) // 2
    sems = refs[-1]
    copies = [
        pltpu.make_async_copy(refs[i], refs[count + i], sems.at[i]) for i in range(count)
    ]
    for copy in copies:
        copy.start()
    for copy in copies:
        copy.wait()


def on_device(
    nlon, nlat, fields_in, weight_one, weight_two, cotangent,
    north_map, north_code, south_map, south_code,
):
    chans, rows, cols = fields_in.shape
    scale = 1.0 / math.sqrt(float(rows * cols * nlon * nlat))
    tall = 3 * chans
    planes = 2 if nlat % 2 == 0 else 1
    group, depth = nlon * planes, nlat // planes
    owners = max(k for k in range(1, group + 1) if 3 * tall % (8 * k) == 0)
    piece = 3 * tall // owners
    vmem = pl.BlockSpec(memory_space=pltpu.VMEM)
    hbm = pl.BlockSpec(memory_space=pltpu.HBM)
    wide = pltpu.VMEM(((rows + 2) * chans, 2 * LANES), BF16)
    flat16 = pltpu.VMEM((chans * rows, LANES), BF16)
    flat32 = pltpu.VMEM((chans * rows, LANES), F32)
    polar = pltpu.VMEM((nlon, chans, LANES), BF16)
    maps = pltpu.SMEM((nlon,), jnp.int32)
    dma = pltpu.SemaphoreType.DMA

    def in_hbm(x):
        return pltpu.with_memory_space_constraint(x, pltpu.HBM)

    scratch = [
        flat16, flat16,
        pltpu.VMEM((9 * chans, chans), BF16), pltpu.VMEM((9 * chans, chans), BF16),
        maps, maps, maps, maps,
        flat32, flat32, wide, wide, wide, wide, flat32,
        pltpu.VMEM((4, tall, tall), BF16), pltpu.VMEM((6, tall, tall), BF16),
        pltpu.VMEM((chans, 2 * LANES), BF16),
        pltpu.VMEM((4, 3, chans, LANES), BF16), pltpu.VMEM((4, 8, chans, LANES), BF16),
        polar, polar, polar, polar,
        pltpu.VMEM((tall, 2 * LANES), F32), pltpu.VMEM((tall, 2 * LANES), F32),
        pltpu.VMEM((3 * tall, LANES), F32),
        pltpu.VMEM((owners, piece, LANES), BF16), pltpu.VMEM((group, piece, LANES), BF16),
        pltpu.VMEM((piece, LANES), BF16), pltpu.VMEM((depth, piece, LANES), BF16),
        pltpu.VMEM((owners, piece, LANES), BF16),
        dma((8,)), dma((4, 8)), dma((4, 8)), dma((4, nlon // 2)), dma((4, nlon // 2)), dma((4,)), dma((4,)),
        dma((owners,)), dma((group,)), dma((depth,)), dma((depth,)),
        dma((group,)), dma((owners,)), pltpu.SemaphoreType.REGULAR((5,)),
    ]
    results = pl.pallas_call(
        functools.partial(kernel, nlon, nlat, planes, rows, chans, owners, scale),
        out_shape=(
            pltpu.VMEM((chans * rows, cols), BF16),
            pltpu.VMEM((chans * rows, cols), BF16),
            pltpu.VMEM((3, 3, chans, chans), F32),
            pltpu.VMEM((3, 3, chans, chans), F32),
        ),
        in_specs=[hbm] * 8,
        out_specs=(vmem, vmem, vmem, vmem),
        scratch_shapes=scratch,
        compiler_params=pltpu.CompilerParams(
            collective_id=0, has_side_effects=True, vmem_limit_bytes=VMEM_BYTES
        ),
    )(
        in_hbm(fields_in.reshape(chans * rows, cols)), in_hbm(cotangent.reshape(chans * rows, cols)),
        in_hbm(weight_one.reshape(9 * chans, chans)), in_hbm(weight_two.reshape(9 * chans, chans)),
        in_hbm(north_map), in_hbm(north_code), in_hbm(south_map), in_hbm(south_code),
    )
    output, d_fields, grad_one, grad_two = pl.pallas_call(
        hand_over,
        out_shape=tuple(jax.ShapeDtypeStruct(x.shape, x.dtype) for x in results),
        in_specs=[vmem] * 4,
        out_specs=(hbm,) * 4,
        scratch_shapes=[dma((4,))],
    )(*[pltpu.with_memory_space_constraint(x, pltpu.VMEM) for x in results])
    shape = (chans, rows, cols)
    return (output.reshape(shape), d_fields.reshape(shape), grad_one, grad_two)


def solution(mesh):
    placed = (P(None, "lat", "lon"), P(), P(), P(None, "lat", "lon"), P(), P(), P(), P())
    return jax.shard_map(
        functools.partial(on_device, mesh.shape["lon"], mesh.shape["lat"]),
        mesh=mesh,
        in_specs=placed,
        out_specs=(P(None, "lat", "lon"), P(None, "lat", "lon"), P(), P()),
        check_vma=False,
    )
```

```python
import functools
import math

import jax
import jax.numpy as jnp
from jax import lax
from jax.experimental import pallas as pl
from jax.experimental.pallas import tpu as pltpu
from jax.sharding import PartitionSpec as P

MESH = pl.DeviceIdType.MESH
LANES = 128
F32 = jnp.float32
BF16 = jnp.bfloat16
NT = (((1,), (1,)), ((), ()))
FIELDS, COT, HIDDEN, DPRE = range(4)
VMEM_BYTES = 48 * 1024 * 1024


def aligned(start, step):
    return pl.multiple_of(start * step, step)


def kernel(
    nlon, nlat, planes, rows, chans, owners, scale,
    fields_hbm, cot_hbm, one_hbm, two_hbm, nmap_hbm, ncode_hbm, smap_hbm, scode_hbm,
    out_ref, df_ref, g1_ref, g2_ref,
    fields_in, cot_in, one_ref, two_ref, north_map, north_code, south_map, south_code,
    stage, stage_two, fwide, gwide, hwide, dwide, slope, w_ref, wedge, rim_row,
    send, recv, pole_f, pole_c, pole_h, pole_d, acc_one, acc_two, sums,
    rs_send, rs_recv, ar_send, ar_recv, ag_buf,
    local_sem, near_send, near_recv, pole_send, pole_recv, hand_send, hand_recv,
    rs_ssem, rs_rsem, ar_ssem, ar_rsem, ag_ssem, ag_rsem, told,
):
    lon = lax.axis_index("lon")
    lat = lax.axis_index("lat")
    depth = nlat // planes
    plane = lax.div(lat, depth)
    z = lax.rem(lat, depth)
    group = nlon * planes
    mine = lon + nlon * plane
    west = lax.rem(lon + nlon - 1, nlon)
    east = lax.rem(lon + 1, nlon)
    has_north = lat > 0
    has_south = lat < nlat - 1
    at_top = lat == 0
    at_bottom = lat == nlat - 1
    at_pole = jnp.logical_or(at_top, at_bottom)
    tall = 3 * chans
    lane = lax.broadcasted_iota(jnp.int32, (chans, LANES), 1)
    own = pl.ds(0, LANES)
    ghost_cols = pl.ds(LANES, LANES)
    piece = 3 * tall // owners

    def in_group(g):
        return lax.div(g, nlon) * depth + z, lax.rem(g, nlon)

    def group_peer(k):
        return lax.rem(mine + k, group)

    def along_z(k):
        return plane * depth + lax.rem(z + k, depth), lon

    spread_owners = group % 4 == 0 and owners == group // 4 * 3

    def owner_at(j):
        return lax.div(j, 3) * 4 + lax.rem(j, 3) if spread_owners else j

    def ownership(g):
        if spread_owners:
            return lax.rem(g, 4) < 3, lax.div(g, 4) * 3 + lax.rem(g, 4)
        return g < owners, g

    owns, own_piece = ownership(mine)

    if group == 32 and planes == 2:
        far = {0: 0, 1: 1, 2: 2, 3: 1}
        steps = [(x, y, c, h) for x in range(4) for y in range(2) for c in range(2) for h in range(2)]
        steps = sorted(steps[1:], key=lambda t: -(far[t[0]] + (2 * t[3] - t[1] if t[3] else t[1])))
        others = [
            lax.rem(lax.div(lon, 4) + x, 4) * 4
            + lax.rem(lax.rem(lax.div(lon, 2), 2) + y, 2) * 2
            + lax.rem(lax.rem(lon, 2) + c, 2)
            + nlon * lax.rem(plane + h, 2)
            for x, y, c, h in steps
        ]
    else:
        others = [lax.rem(mine + k, group) for k in range(1, group)]
    z_steps = sorted(range(1, depth), key=lambda k: -min(k, depth - k))

    barrier = pltpu.get_barrier_semaphore()

    def greet(place):
        pl.semaphore_signal(
            barrier, inc=1, device_id={"lat": place[0], "lon": place[1]}, device_id_type=MESH
        )

    def greet_group(k, c):
        greet(in_group(group_peer(k)))
        return c

    def greet_z(k, c):
        greet(along_z(k))
        return c

    @pl.when(has_north)
    def _():
        for at in (west, lon, east):
            greet((lat - 1, at))

    @pl.when(has_south)
    def _():
        for at in (west, lon, east):
            greet((lat + 1, at))

    relayed = planes == 2 and 4 <= depth <= 8
    partner = ((1 - plane) * depth + z, lon)
    if relayed:
        def greet_row(k, c):
            greet((lat, lax.rem(lon + k, nlon)))
            return c

        lax.fori_loop(1, nlon, greet_row, 0)
        for place in (along_z(1), along_z(depth - 1), partner):
            greet(place)
        greeted = nlon - 1 + 3
    else:
        lax.fori_loop(1, group, greet_group, 0)
        lax.fori_loop(1, depth, greet_z, 0)
        greeted = group - 1 + depth - 1

    def tell(at, place):
        pl.semaphore_signal(
            told.at[at], inc=1, device_id={"lat": place[0], "lon": place[1]}, device_id_type=MESH
        )

    def tell_near():
        if relayed:
            tell(0, along_z(1))
            tell(1, along_z(depth - 1))
            tell(2, partner)

    def tell_far():
        if relayed:
            for at in range(3):
                pl.semaphore_wait(told.at[at], 1)
            tell(3, along_z(2))
            tell(4, along_z(depth - 2))

    def all_told():
        if relayed:
            for at in (3, 4):
                pl.semaphore_wait(told.at[at], 1)

    beside = 3 * has_north.astype(jnp.int32) + 3 * has_south.astype(jnp.int32)

    loads = [
        pltpu.make_async_copy(source, target, local_sem.at[i])
        for i, (source, target) in enumerate(
            [
                (fields_hbm, fields_in), (cot_hbm, cot_in), (one_hbm, one_ref), (two_hbm, two_ref),
                (nmap_hbm, north_map), (ncode_hbm, north_code),
                (smap_hbm, south_map), (scode_hbm, south_code),
            ]
        )
    ]
    for load in loads:
        load.start()

    def put(src, dst, ssem, rsem, place):
        return pltpu.make_async_remote_copy(
            src_ref=src, dst_ref=dst, send_sem=ssem, recv_sem=rsem,
            device_id={"lat": place[0], "lon": place[1]}, device_id_type=MESH,
        )

    here = (lat, lon)
    pole = (pole_f, pole_c, pole_h, pole_d)

    def near_copies(x):
        def one(part, slot, at, place):
            return put(
                send.at[x, part], recv.at[x, slot], near_send.at[x, at], near_recv.at[x, slot],
                place,
            )

        sides = [one(2, 1, 0, (lat, west)), one(2, 0, 1, (lat, east))]
        up = [
            one(0, 7, 2, (lat - 1, west)), one(0, 6, 3, (lat - 1, lon)), one(0, 5, 4, (lat - 1, east))
        ]
        down = [
            one(1, 4, 5, (lat + 1, west)), one(1, 3, 6, (lat + 1, lon)), one(1, 2, 7, (lat + 1, east))
        ]
        return sides, up, down

    half = nlon // 2
    core = lax.rem(lon, 2)
    chip = lax.div(lon, 2)
    sibling = (lat, lon + 1 - 2 * core)

    def strip_at(k):
        return lax.rem(k, 2) * half + lax.div(k, 2)

    def pole_copy(x, part, k):
        return put(
            send.at[x, part], pole[x].at[core * half + chip], pole_send.at[x, k],
            pole_recv.at[x, chip], (lat, lax.rem(lon + 2 * k, nlon)),
        )

    def hand_on(x, at):
        block = pole[x].at[pl.ds(at * half, half)]
        return put(block, block, hand_send.at[x], hand_recv.at[x], sibling)

    def forward_poles(x):
        @pl.when(at_pole)
        def _():
            def step(k, c):
                source = lax.rem(chip + k, half)
                put(
                    send.at[x, 0], pole[x].at[core * half + source], pole_send.at[x, k],
                    pole_recv.at[x, source], here,
                ).wait_recv()
                return c

            lax.fori_loop(1, half, step, 0)
            hand_on(x, core).start()

    def start_exchange(x):
        sides, up, down = near_copies(x)
        for copy in sides:
            copy.start()

        @pl.when(has_north)
        def _():
            for copy in up:
                copy.start()

        @pl.when(has_south)
        def _():
            for copy in down:
                copy.start()

    def start_poles(x):
        def pole_start(part):
            def step(k, c):
                pole_copy(x, part, k).start()
                return c

            lax.fori_loop(1, half, step, 0)
            pole[x][core * half + chip] = send[x, part]

        @pl.when(at_top)
        def _():
            pole_start(0)

        @pl.when(at_bottom)
        def _():
            pole_start(1)

    def arrived(x, slot):
        put(
            send.at[x, 0], recv.at[x, slot], near_send.at[x, 0], near_recv.at[x, slot], here
        ).wait_recv()

    def wait_rows(x):
        @pl.when(has_north)
        def _():
            for slot in (2, 3, 4):
                arrived(x, slot)

        @pl.when(has_south)
        def _():
            for slot in (5, 6, 7):
                arrived(x, slot)

        @pl.when(at_pole)
        def _():
            hand_on(x, 1 - core).wait_recv()

    def wait_sent(x):
        sides, up, down = near_copies(x)
        for copy in sides:
            copy.wait_send()

        @pl.when(has_north)
        def _():
            for copy in up:
                copy.wait_send()

        @pl.when(has_south)
        def _():
            for copy in down:
                copy.wait_send()

        @pl.when(at_pole)
        def _():
            def step(k, c):
                pole_copy(x, 0, k).wait_send()
                return c

            lax.fori_loop(1, half, step, 0)
            hand_on(x, core).wait_send()

    def map_at(k):
        return jnp.where(at_top, north_map[k], south_map[k])

    def code_at(k):
        return jnp.where(at_top, north_code[k], south_code[k])

    def find_owner(k, c):
        hit = map_at(k) == lon
        return jnp.where(hit, k, c[0]), jnp.where(hit, code_at(k), c[1])

    def turned(row, code):
        i = lax.broadcasted_iota(jnp.int32, (LANES, LANES), 0)
        j = lax.broadcasted_iota(jnp.int32, (LANES, LANES), 1)
        match = (i + (2 * code - 1) * j) == (LANES - 1) * code
        turn = jnp.where(match, 1.0, 0.0).astype(BF16)
        return jnp.dot(row, turn, preferred_element_type=F32)

    def set_ghost_row(wide, row, left, mid, right):
        place = pl.ds(row * chans, chans)
        wide[place, own] = mid.astype(BF16)
        wide[place, ghost_cols] = jnp.where(lane == 0, right.astype(F32), left.astype(F32)).astype(
            BF16
        )

    def set_ghost_cols(x, wide):
        arrived(x, 0)
        arrived(x, 1)
        merged = jnp.where(lane % 2 == 0, recv[x, 1].astype(F32), recv[x, 0].astype(F32))

        def step(h, c):
            place = pl.ds(aligned(h + 1, chans), chans)
            wide[place, ghost_cols] = pltpu.roll(merged, lax.rem(LANES - 2 * h, LANES), 1).astype(
                BF16
            )
            return c

        lax.fori_loop(0, rows, step, 0, unroll=rows)

    def pack_edge(h, value, packed):
        keep = jnp.logical_or(lane == 2 * h, lane == lax.rem(2 * h + LANES - 1, LANES))
        return jnp.where(keep, pltpu.roll(value, 2 * h, 1), packed)

    def set_edges(x, wide, packed):
        send[x, 0] = wide[pl.ds(chans, chans), own]
        send[x, 1] = wide[pl.ds(rows * chans, chans), own]
        send[x, 2] = packed.astype(BF16)

    none = jnp.zeros((chans, LANES), F32)

    def take_in(source, stage, wide):
        stage[...] = source[...].astype(F32)

        def step(h, packed):
            value = stage[pl.ds(h, chans, stride=rows), :]
            wide[pl.ds(aligned(h + 1, chans), chans), own] = value.astype(BF16)
            return pack_edge(h, value, packed)

        return lax.fori_loop(0, rows, step, none, unroll=rows)

    def set_ghost_rows(x, wide, forward):
        wait_rows(x)

        @pl.when(has_north)
        def _():
            set_ghost_row(wide, 0, recv[x, 2], recv[x, 3], recv[x, 4])

        @pl.when(has_south)
        def _():
            set_ghost_row(wide, rows + 1, recv[x, 5], recv[x, 6], recv[x, 7])

        def across(row):
            if forward:
                strips = [turned(pole[x][strip_at(map_at(k))], code_at(k)) for k in (west, lon, east)]
                set_ghost_row(wide, row, *strips)
                return
            before, mid, after = [
                turned(pole[x][strip_at(lax.rem(rim_source + shift, nlon))], rim_code)
                for shift in (nlon - 1, 0, 1)
            ]
            flip = rim_code == 1
            set_ghost_row(
                wide, row, jnp.where(flip, after, before), mid, jnp.where(flip, before, after)
            )

        @pl.when(at_top)
        def _():
            across(0)

        @pl.when(at_bottom)
        def _():
            across(rows + 1)

    def weight_forms():
        def spot(shape, shift):
            i = lax.broadcasted_iota(jnp.int32, shape, 0)
            j = lax.broadcasted_iota(jnp.int32, shape, 1)
            return jnp.where(i + shift == j, 1.0, 0.0).astype(BF16)

        for at, ref in ((0, one_ref), (1, two_ref)):
            total = jnp.zeros((tall, tall), F32)
            for r in range(3):
                total = total + jnp.dot(
                    ref[r * tall : (r + 1) * tall, :],
                    spot((chans, tall), r * chans),
                    preferred_element_type=F32,
                )
            w_ref[at] = total.astype(BF16)
            for s in range(3):
                blocks = [
                    ref[((2 - r) * 3 + 2 - s) * chans : ((2 - r) * 3 + 3 - s) * chans, :]
                    for r in range(3)
                ]
                w_ref[2 + at, s * chans : (s + 1) * chans, :] = lax.dot_general(
                    spot((chans, chans), 0),
                    jnp.concatenate(blocks, axis=0),
                    NT,
                    preferred_element_type=F32,
                ).astype(BF16)

    def rim_weights():
        for kernel_at in range(2):
            base = w_ref[2 + kernel_at]
            for place in range(3):
                wedge[kernel_at * 3 + place] = base

            def replace(place, into, out_of):
                full = base.astype(F32)
                shown = lax.broadcasted_iota(jnp.int32, full.shape, 1) // chans == into
                i = lax.broadcasted_iota(jnp.int32, full.shape, 0)
                j = lax.broadcasted_iota(jnp.int32, full.shape, 1)
                move = jnp.where(i - out_of * chans == j - into * chans, 1.0, 0.0).astype(BF16)
                moved = jnp.dot(base, move, preferred_element_type=F32)
                swapped = jnp.concatenate(
                    [moved[2 * chans :], moved[chans : 2 * chans], moved[:chans]], axis=0
                )
                chosen = jnp.where(rim_code == 1, swapped, moved)
                wedge[kernel_at * 3 + place] = jnp.where(shown, chosen, full).astype(BF16)

            @pl.when(at_top)
            def _():
                replace(0, 0, 2)

            @pl.when(at_bottom)
            def _():
                replace(2, 2, 0)

    def conv_row(weights, wide, h):
        window = wide[pl.ds(aligned(h, chans), tall), :]
        y = jnp.dot(weights, window, preferred_element_type=F32)
        left = jnp.where(lane == LANES - 1, y[:chans, LANES:], y[:chans, :LANES])
        right = jnp.where(lane == 0, y[2 * chans :, LANES:], y[2 * chans :, :LANES])
        return (
            pltpu.roll(left, 1, 1) + y[chans : 2 * chans, :LANES] + pltpu.roll(right, LANES - 1, 1)
        )

    def shifted(wide, h):
        g = wide[pl.ds(aligned(h + 1, chans), chans), own].astype(F32)
        ahead = pltpu.roll(g, LANES - 1, 1)
        behind = pltpu.roll(g, 1, 1)
        zero = jnp.zeros_like(g)
        first = jnp.concatenate(
            [jnp.where(lane != LANES - 1, ahead, zero), g, jnp.where(lane != 0, behind, zero)],
            axis=0,
        )
        second = jnp.concatenate(
            [jnp.where(lane == LANES - 1, ahead, zero), zero, jnp.where(lane == 0, behind, zero)],
            axis=0,
        )
        return [first.astype(BF16), second.astype(BF16)]

    def gradient(shift_wide, window_wide, acc, shifted_first, hs):
        moved, windows = [], []
        for h in hs:
            moved += shifted(shift_wide, h)
            windows.append(window_wide[pl.ds(aligned(h, chans), tall), :])
        moved, windows = jnp.concatenate(moved, axis=1), jnp.concatenate(windows, axis=1)
        a, b = (moved, windows) if shifted_first else (windows, moved)
        acc[:, :tall] += lax.dot_general(a, b, NT, preferred_element_type=F32)

    def inner_gradient(shift_wide, window_wide, acc, shifted_first):
        count = (rows - 2) // 2

        def step(i, c):
            first = 1 + i * count
            gradient(
                shift_wide, window_wide, acc, shifted_first, [first + u for u in range(count)]
            )
            return c

        acc[...] = jnp.zeros_like(acc)
        lax.fori_loop(0, 2, step, 0)

    ends = (0, rows - 1)

    def inner_rows(row, carry):
        return lax.fori_loop(1, rows - 1, row, carry, unroll=rows - 2)

    def end_rows(row, carry):
        for h in ends:
            carry = row(h, carry)
        return carry

    loads[0].wait()
    packed = take_in(fields_in, stage, fwide)
    set_edges(FIELDS, fwide, packed)
    pl.semaphore_wait(barrier, greeted + beside)
    start_exchange(FIELDS)
    start_poles(FIELDS)
    tell_near()
    loads[1].wait()
    packed = take_in(cot_in, stage_two, gwide)
    set_edges(COT, gwide, packed)
    start_exchange(COT)
    start_poles(COT)
    for load in loads[2:]:
        load.wait()
    rim_source, rim_code = lax.fori_loop(0, nlon, find_owner, (jnp.int32(0), jnp.int32(0)))
    weight_forms()
    rim_weights()

    root = math.sqrt(2.0 / math.pi)

    def hidden_row(h, packed):
        u = conv_row(w_ref[0], fwide, h)
        square = u * u
        t = jnp.tanh(root * (u + 0.044715 * (square * u)))
        half = 0.5 * (1.0 + t)
        slope[pl.ds(aligned(h, chans), chans), :] = half + (0.5 * root) * u * (1.0 - t * t) * (
            1.0 + (3 * 0.044715) * square
        )
        value = u * half
        hwide[pl.ds(aligned(h + 1, chans), chans), own] = value.astype(BF16)
        return pack_edge(h, value, packed)

    def weights_at(kernel_at, h):
        place = jnp.where(h == 0, 0, jnp.where(h == rows - 1, 2, 1))
        return wedge[kernel_at * 3 + place]

    def back_row(h, packed):
        back = conv_row(weights_at(1, h), gwide, h)
        value = back * slope[pl.ds(aligned(h, chans), chans), :]
        dwide[pl.ds(aligned(h + 1, chans), chans), own] = value.astype(BF16)
        return pack_edge(h, value, packed)

    def set_aside(row):
        place = pl.ds(row * chans, chans)
        rim_row[...] = gwide[place, :]
        gwide[place, :] = jnp.zeros((chans, 2 * LANES), BF16)

    def credit(h, block):
        first, second = shifted(hwide, h)
        moved = jnp.concatenate([first, second], axis=1).astype(F32)
        swapped = jnp.concatenate(
            [moved[2 * chans :], moved[chans : 2 * chans], moved[:chans]], axis=0
        )
        chosen = jnp.where(rim_code == 1, swapped, moved).astype(BF16)
        acc_two[pl.ds(block * chans, chans), :tall] += lax.dot_general(
            rim_row[...], chosen, NT, preferred_element_type=F32
        )

    set_ghost_cols(FIELDS, fwide)
    hidden_packed = inner_rows(hidden_row, none)
    tell_far()
    forward_poles(FIELDS)
    set_ghost_cols(COT, gwide)
    d_packed = inner_rows(back_row, none)
    forward_poles(COT)
    all_told()
    inner_gradient(dwide, fwide, acc_one, True)
    inner_gradient(hwide, gwide, acc_two, False)
    set_ghost_rows(FIELDS, fwide, True)
    set_ghost_rows(COT, gwide, False)
    hidden_packed = end_rows(hidden_row, hidden_packed)
    d_packed = end_rows(back_row, d_packed)

    gradient(dwide, fwide, acc_one, True, ends)
    early = tall // piece

    def rs_copy(j):
        return put(
            rs_send.at[j], rs_recv.at[mine], rs_ssem.at[j], rs_rsem.at[mine], in_group(owner_at(j))
        )

    def send_pieces(first, end):
        for j in range(first, end):
            rs_send[j] = sums[pl.ds(j * piece, piece), :].astype(BF16)
        for other in others:
            takes, taken = ownership(other)
            due = jnp.logical_and(taken >= first, taken < end)

            @pl.when(jnp.logical_and(takes, due))
            def _():
                put(
                    rs_send.at[taken], rs_recv.at[mine], rs_ssem.at[taken], rs_rsem.at[mine],
                    in_group(other),
                ).start()

    sums[pl.ds(0, tall), :] = acc_one[:, :LANES]
    send_pieces(0, early)

    @pl.when(at_top)
    def _():
        set_aside(0)

    @pl.when(at_bottom)
    def _():
        set_aside(rows + 1)

    gradient(hwide, gwide, acc_two, False, ends)

    @pl.when(at_top)
    def _():
        credit(0, 2)

    @pl.when(at_bottom)
    def _():
        credit(rows - 1, 0)

    sums[pl.ds(tall, tall), :] = acc_two[:, :LANES]
    half_lane = lax.broadcasted_iota(jnp.int32, (tall, LANES), 1) < chans
    sums[pl.ds(2 * tall, tall), :] = jnp.where(
        half_lane, acc_one[:, LANES:], pltpu.roll(acc_two[:, LANES:], chans, 1)
    )
    send_pieces(early, owners)

    @pl.when(owns)
    def _():
        rs_recv[mine] = rs_send[own_piece]

    set_edges(HIDDEN, hwide, hidden_packed)
    start_exchange(HIDDEN)
    set_edges(DPRE, dwide, d_packed)
    start_exchange(DPRE)

    def out_row(h, c):
        stage[pl.ds(h, chans, stride=rows), :] = conv_row(w_ref[1], hwide, h)
        return c

    def df_row(h, c):
        stage_two[pl.ds(h, chans, stride=rows), :] = conv_row(weights_at(0, h), dwide, h)
        return c

    set_ghost_cols(HIDDEN, hwide)
    inner_rows(out_row, 0)

    def ar_copy(k):
        return put(ar_send, ar_recv.at[z], ar_ssem.at[k], ar_rsem.at[z], along_z(k))

    @pl.when(owns)
    def _():
        def wait(k, c):
            source = group_peer(k)
            put(
                rs_recv.at[mine], rs_recv.at[source], rs_ssem.at[0], rs_rsem.at[source], here
            ).wait_recv()
            return c

        lax.fori_loop(1, group, wait, 0)
        total = rs_recv[0].astype(F32)
        for k in range(1, group):
            total = total + rs_recv[k].astype(F32)
        ar_send[...] = total.astype(BF16)
        ar_recv[z] = total.astype(BF16)

        for k in z_steps:
            ar_copy(k).start()

    start_poles(HIDDEN)
    start_poles(DPRE)
    set_ghost_cols(DPRE, dwide)
    inner_rows(df_row, 0)

    def ag_copy(k):
        return put(
            ag_buf.at[own_piece], ag_buf.at[own_piece], ag_ssem.at[k], ag_rsem.at[own_piece],
            in_group(others[k]),
        )

    @pl.when(owns)
    def _():
        def wait(k, c):
            source = lax.rem(z + k, depth)
            put(ar_send, ar_recv.at[source], ar_ssem.at[k], ar_rsem.at[source], here).wait_recv()
            return c

        lax.fori_loop(1, depth, wait, 0)
        total = ar_recv[0].astype(F32)
        for k in range(1, depth):
            total = total + ar_recv[k].astype(F32)
        ag_buf[own_piece] = total.astype(BF16)

        for k in range(group - 1):
            ag_copy(k).start()

    forward_poles(HIDDEN)
    forward_poles(DPRE)
    set_ghost_rows(HIDDEN, hwide, True)
    set_ghost_rows(DPRE, dwide, False)
    end_rows(out_row, 0)
    end_rows(df_row, 0)
    out_ref[...] = stage[...].astype(BF16)
    df_ref[...] = stage_two[...].astype(BF16)

    for x in range(4):
        wait_sent(x)

    def rs_sent(j, c):
        @pl.when(owner_at(j) != mine)
        def _():
            rs_copy(j).wait_send()

        return c

    lax.fori_loop(0, owners, rs_sent, 0)

    @pl.when(owns)
    def _():
        def sent(k, c):
            ar_copy(k).wait_send()
            return c

        lax.fori_loop(1, depth, sent, 0)

    def ag_wait(j, c):
        @pl.when(owner_at(j) != mine)
        def _():
            put(ag_buf.at[j], ag_buf.at[j], ag_ssem.at[0], ag_rsem.at[j], here).wait_recv()

        return c

    lax.fori_loop(0, owners, ag_wait, 0)
    for j in range(owners):
        sums[pl.ds(j * piece, piece), :] = ag_buf[j].astype(F32) * scale
    one, two, rest = (sums[pl.ds(i * tall, tall), :] for i in range(3))
    one_parts = (one, pltpu.roll(one, chans, 1), rest)
    two_parts = (two, pltpu.roll(two, chans, 1), pltpu.roll(rest, chans, 1))
    for a in range(3):
        cut = slice(a * chans, (a + 1) * chans)
        for b in range(3):
            g1_ref[b, a] = one_parts[b][cut, :chans]
            g2_ref[2 - a, 2 - b] = two_parts[b][cut, :chans]

    @pl.when(owns)
    def _():
        for k in range(group - 1):
            ag_copy(k).wait_send()


def hand_over(*refs):
    count = (len(refs) - 1) // 2
    sems = refs[-1]
    copies = [
        pltpu.make_async_copy(refs[i], refs[count + i], sems.at[i]) for i in range(count)
    ]
    for copy in copies:
        copy.start()
    for copy in copies:
        copy.wait()


def on_device(
    nlon, nlat, fields_in, weight_one, weight_two, cotangent,
    north_map, north_code, south_map, south_code,
):
    chans, rows, cols = fields_in.shape
    scale = 1.0 / math.sqrt(float(rows * cols * nlon * nlat))
    tall = 3 * chans
    planes = 2 if nlat % 2 == 0 else 1
    group, depth = nlon * planes, nlat // planes
    owners = max(k for k in range(1, group + 1) if 3 * tall % (8 * k) == 0)
    piece = 3 * tall // owners
    vmem = pl.BlockSpec(memory_space=pltpu.VMEM)
    hbm = pl.BlockSpec(memory_space=pltpu.HBM)
    wide = pltpu.VMEM(((rows + 2) * chans, 2 * LANES), BF16)
    flat16 = pltpu.VMEM((chans * rows, LANES), BF16)
    flat32 = pltpu.VMEM((chans * rows, LANES), F32)
    polar = pltpu.VMEM((nlon, chans, LANES), BF16)
    maps = pltpu.SMEM((nlon,), jnp.int32)
    dma = pltpu.SemaphoreType.DMA

    def in_hbm(x):
        return pltpu.with_memory_space_constraint(x, pltpu.HBM)

    scratch = [
        flat16, flat16,
        pltpu.VMEM((9 * chans, chans), BF16), pltpu.VMEM((9 * chans, chans), BF16),
        maps, maps, maps, maps,
        flat32, flat32, wide, wide, wide, wide, flat32,
        pltpu.VMEM((4, tall, tall), BF16), pltpu.VMEM((6, tall, tall), BF16),
        pltpu.VMEM((chans, 2 * LANES), BF16),
        pltpu.VMEM((4, 3, chans, LANES), BF16), pltpu.VMEM((4, 8, chans, LANES), BF16),
        polar, polar, polar, polar,
        pltpu.VMEM((tall, 2 * LANES), F32), pltpu.VMEM((tall, 2 * LANES), F32),
        pltpu.VMEM((3 * tall, LANES), F32),
        pltpu.VMEM((owners, piece, LANES), BF16), pltpu.VMEM((group, piece, LANES), BF16),
        pltpu.VMEM((piece, LANES), BF16), pltpu.VMEM((depth, piece, LANES), BF16),
        pltpu.VMEM((owners, piece, LANES), BF16),
        dma((8,)), dma((4, 8)), dma((4, 8)), dma((4, nlon // 2)), dma((4, nlon // 2)), dma((4,)), dma((4,)),
        dma((owners,)), dma((group,)), dma((depth,)), dma((depth,)),
        dma((group,)), dma((owners,)), pltpu.SemaphoreType.REGULAR((5,)),
    ]
    results = pl.pallas_call(
        functools.partial(kernel, nlon, nlat, planes, rows, chans, owners, scale),
        out_shape=(
            pltpu.VMEM((chans * rows, cols), BF16),
            pltpu.VMEM((chans * rows, cols), BF16),
            pltpu.VMEM((3, 3, chans, chans), F32),
            pltpu.VMEM((3, 3, chans, chans), F32),
        ),
        in_specs=[hbm] * 8,
        out_specs=(vmem, vmem, vmem, vmem),
        scratch_shapes=scratch,
        compiler_params=pltpu.CompilerParams(
            collective_id=0, has_side_effects=True, vmem_limit_bytes=VMEM_BYTES
        ),
    )(
        in_hbm(fields_in.reshape(chans * rows, cols)), in_hbm(cotangent.reshape(chans * rows, cols)),
        in_hbm(weight_one.reshape(9 * chans, chans)), in_hbm(weight_two.reshape(9 * chans, chans)),
        in_hbm(north_map), in_hbm(north_code), in_hbm(south_map), in_hbm(south_code),
    )
    output, d_fields, grad_one, grad_two = pl.pallas_call(
        hand_over,
        out_shape=tuple(jax.ShapeDtypeStruct(x.shape, x.dtype) for x in results),
        in_specs=[vmem] * 4,
        out_specs=(hbm,) * 4,
        scratch_shapes=[dma((4,))],
    )(*[pltpu.with_memory_space_constraint(x, pltpu.VMEM) for x in results])
    shape = (chans, rows, cols)
    return (output.reshape(shape), d_fields.reshape(shape), grad_one, grad_two)


def solution(mesh):
    placed = (P(None, "lat", "lon"), P(), P(), P(None, "lat", "lon"), P(), P(), P(), P())
    return jax.shard_map(
        functools.partial(on_device, mesh.shape["lon"], mesh.shape["lat"]),
        mesh=mesh,
        in_specs=placed,
        out_specs=(P(None, "lat", "lon"), P(None, "lat", "lon"), P(), P()),
        check_vma=False,
    )
```
